32 devices in a mesh: fsdp: 8 (over y, x, core), tensor: 4 (over z).
Axes of the slice: x: 2, y: 2, z: 4, core: 2. Of those that a mesh axis runs over, the one named last changes fastest.
Arguments:
- hidden: bfloat16 [4096, 2048], P(('fsdp', 'tensor')), may hold values from -6 to 6
- cotangent: bfloat16 [4096, 2048], P(('fsdp', 'tensor')), may hold values from -6 to 6
- seq_lengths: int32 [8, 3], P('fsdp'), may hold values from 1 to 256, 512 in all within a row
- pack_order: int32 [8, 3], P('fsdp'), may hold values from 0 to 2, each once within a row
- norm_gain: bfloat16 [2048], P(('fsdp', 'tensor')), may hold values from 0.099609375 to 1.8984375
- w_in: bfloat16 [2, 4096, 2048], P(None, ('fsdp', 'tensor')), may hold values from -0.125 to 0.125
- conv_weight: bfloat16 [4096, 4], P(('fsdp', 'tensor')), may hold values from -3 to 3
- conv_bias: bfloat16 [4096], P(('fsdp', 'tensor')), may hold values from -3 to 3
- w_xproj: bfloat16 [4096, 160], P(('fsdp', 'tensor')), may hold values from -0.1875 to 0.1875
- w_dt: bfloat16 [4096, 128], P(('fsdp', 'tensor')), may hold values from -0.5 to 0.5
- dt_bias: bfloat16 [4096], P(('fsdp', 'tensor')), may hold values from -7 to -2
- a_log: bfloat16 [4096, 16], P(('fsdp', 'tensor')), may hold values from -1 to 2.6875
- d_skip: bfloat16 [4096], P(('fsdp', 'tensor')), may hold values from 0.099609375 to 1.8984375
- w_out: bfloat16 [4096, 2048], P(('fsdp', 'tensor')), may hold values from -0.1875 to 0.1875
Outputs:
- output: bfloat16 [4096, 2048], P(('fsdp', 'tensor'))
- grad_hidden: float32 [4096, 2048], P(('fsdp', 'tensor'))
- grad_norm_gain: float32 [2048], P(('fsdp', 'tensor'))
- grad_w_in: float32 [2, 4096, 2048], P(None, ('fsdp', 'tensor'))
- grad_conv_weight: float32 [4096, 4], P(('fsdp', 'tensor'))
- grad_conv_bias: float32 [4096], P(('fsdp', 'tensor'))
- grad_w_xproj: float32 [4096, 160], P(('fsdp', 'tensor'))
- grad_w_dt: float32 [4096, 128], P(('fsdp', 'tensor'))
- grad_dt_bias: float32 [4096], P(('fsdp', 'tensor'))
- grad_a_log: float32 [4096, 16], P(('fsdp', 'tensor'))
- grad_d_skip: float32 [4096], P(('fsdp', 'tensor'))
- grad_w_out: float32 [4096, 2048], P(('fsdp', 'tensor'))
The draws below stay inside these ranges and needn't reach their ends.
Inputs may be any that keep to these rules, and one draw needn't show every extreme that they name: `seq_lengths`: each row holds the lengths of the 3 sequences of one token group; they sum to 512 and the largest of each row is exactly 256. `pack_order`: each row is a permutation of 0 to 2: the sequence packed into each slot.
All inputs are finite; a program needn't handle non-finite values.
Results may differ from the reference program's by a relative error of at most 0.012.
Values may be sent and summed in bfloat16 or wider, within the bound.
No kernel may reach another device: no remote copies, remote signals or barrier semaphores. Data moves between devices by JAX's collectives and lax.ppermute only.
A program may use at most 320 MiB of HBM per device.

```python
import math
import jax
import jax.numpy as jnp
import numpy as np
from jax import lax

D = 2048
DI = 4096
STATE = 16
RANK = 128
KERNEL = 4
XW = 160
GROUP_TOK = 512
SEQ_MOST = 256
TOTAL = 4096
SLOTS = 3
N_FSDP = 8


def steps_of(own_key, extent, split, least, top_value):
    def one(dim, blocks):
        heights = jax.random.uniform(jax.random.fold_in(jax.random.fold_in(own_key, 6), dim), (blocks,), jnp.float32, least / len(split), top_value / len(split))
        return jnp.repeat(jnp.exp(heights), extent[dim] // blocks).reshape((-1,) + (1,) * (len(extent) - dim - 1))

    gain = one(*split[0])
    for cut in split[1:]:
        gain = gain * one(*cut)
    return gain


def profile(number_of, total, limit, skew):
    weights = [(1 << 20) // math.isqrt(grade ** skew) + 1 for grade in range(2, number_of + 1)]
    surplus, counts = total - limit - (number_of - 1), [1] * (number_of - 1)
    while surplus > 0:
        free = [i for i in range(number_of - 1) if counts[i] < limit]
        pool, left = sum([weights[i] for i in free]), surplus
        for i in free:
            more = min(limit - counts[i], max(1, left * weights[i] // pool), surplus)
            counts[i] = counts[i] + more
            surplus = surplus - more
    return np.array([limit] + counts)


def uneven(stream_key, amount, total, limit, lean):
    if amount == 2:
        one = jax.random.randint(stream_key, (), max(1, total - limit), min(limit, total - 1) + 1)
        return jnp.stack([one, total - one])
    sizes = jnp.asarray(profile(amount, total, limit, lean), jnp.int32)
    couples = (amount - 1) // 2
    giver, receiver = sizes[1:1 + 2 * couples:2], sizes[2:2 + 2 * couples:2]
    margin = jnp.minimum(giver - 1, limit - receiver)
    moved = jax.random.randint(jax.random.fold_in(stream_key, 1), (couples,), 0, 1 << 20) % (margin + 1)
    sizes = sizes.at[1:1 + 2 * couples:2].set(giver - moved).at[2:2 + 2 * couples:2].set(receiver + moved)
    return sizes[jax.random.permutation(jax.random.fold_in(stream_key, 2), amount)]


def bell_draw(rng, extent, width, reach, cuts=(), kind=jnp.bfloat16):
    values = jax.random.normal(rng, extent, jnp.float32) * width
    if len(cuts) > 0:
        values = steps_of(rng, extent, cuts, -0.22, 0.18) * values
    return jnp.clip(values, min=-reach, max=reach).astype(kind)


def setup_inputs(seed: int = 0) -> dict:
    keys = jax.random.split(jax.random.key(seed), 15)
    hidden = bell_draw(keys[0], (TOTAL, D), 1.0, 6.0, ((0, 32),))
    cotangent = bell_draw(keys[1], (TOTAL, D), 1.0, 6.0, ((0, 32),))
    seq_lengths = jax.vmap(lambda own: uneven(own, SLOTS, GROUP_TOK, SEQ_MOST, 1))(jax.random.split(keys[2], N_FSDP)).reshape((N_FSDP, SLOTS)).astype(jnp.int32)
    pack_order = jax.vmap(lambda own: jax.random.permutation(own, SLOTS))(jax.random.split(keys[3], N_FSDP)).reshape((N_FSDP, SLOTS)).astype(jnp.int32)
    norm_gain = jnp.clip(1.0 + 0.18 * jax.random.normal(keys[4], (D,), jnp.float32), 0.099609375, 1.8984375).astype(jnp.bfloat16)
    w_in = bell_draw(keys[5], (2, DI, D), D ** -0.5, 0.125, ((1, 32),))
    conv_weight = bell_draw(keys[6], (DI, KERNEL), KERNEL ** -0.5, 3.0, ((0, 32),))
    conv_bias = bell_draw(keys[7], (DI,), 0.5, 3.0, ((0, 32),))
    w_xproj = bell_draw(keys[8], (DI, XW), (DI // 4) ** -0.5, 0.1875, ((0, 32),))
    w_dt = bell_draw(keys[9], (DI, RANK), RANK ** -0.5, 0.5, ((0, 32),))
    dt_bias = jnp.clip(-7.0 + 5.0 * jax.random.uniform(keys[10], (DI,), jnp.float32) ** steps_of(keys[10], (DI,), ((0, 32),), -0.2, 0.2), -7.0, -2.0).astype(jnp.bfloat16)
    a_log = jnp.clip(-1.0 + 3.6875 * jax.random.uniform(keys[11], (DI, STATE), jnp.float32) ** steps_of(keys[11], (DI, STATE), ((0, 32),), -0.2, 0.2), -1.0, 2.6875).astype(jnp.bfloat16)
    d_skip = jnp.clip(1.0 + 0.18 * jax.random.normal(keys[12], (DI,), jnp.float32), 0.099609375, 1.8984375).astype(jnp.bfloat16)
    w_out = bell_draw(keys[13], (DI, D), (DI // 4) ** -0.5, 0.1875, ((0, 32),))
    return {"hidden": hidden, "cotangent": cotangent, "seq_lengths": seq_lengths, "pack_order": pack_order, "norm_gain": norm_gain, "w_in": w_in, "conv_weight": conv_weight, "conv_bias": conv_bias, "w_xproj": w_xproj, "w_dt": w_dt, "dt_bias": dt_bias, "a_log": a_log, "d_skip": d_skip, "w_out": w_out}


EPSILON = 1e-05

@jax.custom_vjp
def low(v):
    return lax.optimization_barrier(v.astype(jnp.bfloat16)).astype(jnp.float32)

@jax.custom_vjp
def low_back(v):
    return v

def low_keep(v):
    return (low(v), None)

def low_pass(kept, grad):
    return (grad,)

def back_keep(v):
    return (v, None)

def back_low(kept, grad):
    return (low(grad),)
low.defvjp(low_keep, low_pass)
low_back.defvjp(back_keep, back_low)

def normalize(values, scales):
    factor = lax.rsqrt(lax.optimization_barrier(jnp.mean(values * values, axis=1, keepdims=True)) + EPSILON)
    return values * factor * scales[None, :]

def distances(lengths, pack_rows, row_count):
    slot_count = lengths.shape[0]
    picks = pack_rows[:, None] == jnp.arange(slot_count, dtype=jnp.int32)[None, :]
    packed = lax.optimization_barrier(jnp.sum(jnp.where(picks, lengths[None, :], 0), axis=1)).astype(jnp.int32)
    starts = (jnp.cumsum(packed) - packed).astype(jnp.int32)
    positions = jnp.arange(row_count, dtype=jnp.int32)
    latest = lax.optimization_barrier(jnp.max(jnp.where(starts[None, :] <= positions[:, None], starts[None, :], 0), axis=1))
    return (positions - latest).astype(jnp.int32)

def convolve(signal, weights, biases, offsets):
    kernel_taps = weights.shape[1]
    result = biases[None, :] + weights[:, kernel_taps - 1][None, :] * signal
    for lag_index in range(1, kernel_taps):
        shifted = jnp.concatenate([jnp.zeros((lag_index, signal.shape[1]), jnp.float32), signal[:-lag_index]], axis=0)
        in_sequence = (offsets >= lag_index).astype(jnp.float32)[:, None]
        result = result + weights[:, kernel_taps - 1 - lag_index][None, :] * shifted * in_sequence
    return result

def combine_steps(earlier, later):
    return (earlier[0] * later[0], later[0] * earlier[1] + later[1])

def block_scan(carried, step_sizes, inputs, b_in, c_out, decays, keep_mask):
    factors = jnp.exp(step_sizes[:, :, None] * decays[None, :, :]) * keep_mask[:, None, None]
    drives = (step_sizes * inputs)[:, :, None] * b_in[:, None, :]
    leading = drives[0:1] + factors[0:1] * carried[None]
    drives = jnp.concatenate([leading, drives[1:]], axis=0)
    states = lax.associative_scan(combine_steps, (factors, drives), axis=0)[1]
    return (states[-1], lax.optimization_barrier(jnp.sum(states * c_out[:, None, :], axis=2)))

def selective(step_sizes, inputs, b_in, c_out, decays, keep_mask, block_len):
    row_count = step_sizes.shape[0]
    blocks = row_count // block_len

    def block_step(carried, pieces):
        return block_scan(carried, pieces[0], pieces[1], pieces[2], pieces[3], decays, pieces[4])
    pieces = (step_sizes.reshape(blocks, block_len, -1), inputs.reshape(blocks, block_len, -1), b_in.reshape(blocks, block_len, -1), c_out.reshape(blocks, block_len, -1), keep_mask.reshape(blocks, block_len))
    initial = jnp.zeros((step_sizes.shape[1], decays.shape[1]), jnp.float32)
    _, outputs = lax.scan(jax.checkpoint(block_step), initial, pieces)
    return outputs.reshape(row_count, -1)

def mix_states(proj, b_in, c_out, inner, gate_in, step_bias, log_rates, skip_scale, keep_mask, block_len):
    step_sizes = jax.nn.softplus(proj + step_bias[None, :])
    decays = -jnp.exp(log_rates)
    scanned = selective(step_sizes, inner, b_in, c_out, decays, keep_mask, block_len)
    return (scanned + skip_scale[None, :] * inner) * jax.nn.silu(gate_in)

def block_layer(values, weight_list, offsets, keep_mask, block_len):
    gain_f, w_in_f, conv_w_f, conv_b_f, w_x_f, w_dt_f, dt_b_f, a_log_f, d_skip_f, w_out_f = weight_list
    highest = lax.Precision.HIGHEST
    rank_cols = w_dt_f.shape[1]
    state_cols = a_log_f.shape[1]
    normed = low(normalize(values, gain_f))
    xz_all = low_back(jnp.einsum('gd,hcd->ghc', normed, w_in_f, precision=highest))
    inner = low(jax.nn.silu(convolve(xz_all[:, 0], conv_w_f, conv_b_f, offsets)))
    mixed = low_back(jnp.dot(inner, w_x_f, precision=highest))
    step_in = low(mixed[:, :rank_cols])
    proj = low_back(jnp.dot(step_in, w_dt_f.T, precision=highest))
    gated = low_back(low(mix_states(proj, mixed[:, rank_cols:rank_cols + state_cols], mixed[:, rank_cols + state_cols:], inner, xz_all[:, 1], dt_b_f, a_log_f, d_skip_f, keep_mask, block_len)))
    return values + jnp.dot(gated, w_out_f, precision=highest)

def reference(hidden, cotangent, seq_lengths, pack_order, norm_gain, w_in, conv_weight, conv_bias, w_xproj, w_dt, dt_bias, a_log, d_skip, w_out):
    weight_list = tuple((item.astype(jnp.float32) for item in (norm_gain, w_in, conv_weight, conv_bias, w_xproj, w_dt, dt_bias, a_log, d_skip, w_out)))
    block_len = math.gcd(GROUP_TOK, 256)
    inputs = hidden.astype(jnp.float32).reshape(N_FSDP, GROUP_TOK, D)
    cotangents = cotangent.astype(jnp.float32).reshape(N_FSDP, GROUP_TOK, D)

    def per_group(totals, pieces):
        values, grad_rows, lengths, pack_rows = pieces
        offsets = distances(lengths, pack_rows, GROUP_TOK)
        keep_mask = (offsets > 0).astype(jnp.float32)

        def forward(inner_values, *weights_in):
            return block_layer(inner_values, weights_in, offsets, keep_mask, block_len)
        result, backward = jax.vjp(forward, values, *weight_list)
        grads = backward(grad_rows)
        totals = tuple((total + grad for total, grad in zip(totals, grads[1:])))
        return (totals, (result.astype(jnp.bfloat16), grads[0]))
    initial = tuple((jnp.zeros_like(item) for item in weight_list))
    totals, (results, input_grads) = lax.scan(per_group, initial, (inputs, cotangents, seq_lengths, pack_order))
    return (results.reshape(TOTAL, D), input_grads.reshape(TOTAL, D), totals[0], totals[1], totals[2], totals[3], totals[4], totals[5], totals[6], totals[7], totals[8], totals[9])
```

```python
import functools
import math

import jax
import jax.numpy as jnp
from jax import lax
from jax.experimental import pallas as pl
from jax.experimental.pallas import tpu as pltpu
from jax.sharding import PartitionSpec as P

EPSILON = 1e-05


def normalize(values, scales):
    factor = lax.rsqrt(jnp.mean(values * values, axis=1, keepdims=True) + EPSILON)
    return values * factor * scales[None, :]


def distances(lengths, pack_rows, row_count):
    slot_count = lengths.shape[0]
    picks = pack_rows[:, None] == jnp.arange(slot_count, dtype=jnp.int32)[None, :]
    packed = jnp.sum(jnp.where(picks, lengths[None, :], 0), axis=1)
    starts = jnp.cumsum(packed) - packed
    positions = jnp.arange(row_count, dtype=jnp.int32)
    latest = jnp.max(jnp.where(starts[None, :] <= positions[:, None], starts[None, :], 0), axis=1)
    return positions - latest


def convolve(signal, weights, biases, offsets):
    kernel_taps = weights.shape[1]
    result = biases[None, :] + weights[:, kernel_taps - 1][None, :] * signal
    for lag_index in range(1, kernel_taps):
        shifted = jnp.concatenate(
            [jnp.zeros((lag_index, signal.shape[1]), jnp.float32), signal[:-lag_index]], axis=0
        )
        in_sequence = (offsets >= lag_index).astype(jnp.float32)[:, None]
        result = result + weights[:, kernel_taps - 1 - lag_index][None, :] * shifted * in_sequence
    return result


f32 = jnp.float32
bf16 = jnp.bfloat16
BIG = 1e30
LANES=128
SUB=8

def tile_rows(ti, j, subs):
    return pl.ds((ti * subs + j) * SUB, SUB)

def put_tiles(ref, value, subs):
    for ti in range(value.shape[0] // SUB):
        for j in range(subs):
            ref[tile_rows(ti, j, subs), :] = value[ti*SUB:(ti+1)*SUB, j*LANES:(j+1)*LANES]

def get_tiles(ref, rows, subs):
    return jnp.concatenate([jnp.concatenate([ref[tile_rows(ti, j, subs), :] for j in range(subs)], axis=1) for ti in range(rows // SUB)], axis=0)

def put_spread(ref, value, count):
    for ti in range(value.shape[0] // SUB):
        for n in range(count):
            ref[pl.ds((ti*count+n)*SUB, SUB), :] = jnp.broadcast_to(value[ti*SUB:(ti+1)*SUB, n:n+1], (SUB, LANES))

def fwd_body(states, subs, keep_ref, step_ref, bc_ref, wdt_ref, db_ref, ds_ref, dec_ref, inner_ref, gate_ref,
             hs_ref, dl_ref, ys_ref, gated_ref, h_sc, du_sc, bb_sc, y_sc):
    chunk = pl.program_id(0)
    rows = step_ref.shape[0]
    span = states * subs
    @pl.when(chunk == 0)
    def _():
        h_sc[...] = jnp.zeros_like(h_sc)
    raw = jnp.dot(step_ref[...], wdt_ref[...], preferred_element_type=f32) + db_ref[...]
    delta = jnp.maximum(raw, 0.0) + jnp.log1p(jnp.exp(-jnp.abs(raw)))
    inner = inner_ref[...].astype(f32)
    put_tiles(dl_ref, delta, subs)
    put_tiles(du_sc, delta * inner, subs)
    put_spread(bb_sc, bc_ref[...], 2 * states)
    hs_ref[pl.ds(0, span), :] = h_sc[...]
    decs = [dec_ref[pl.ds(n*subs, subs), :] for n in range(states)]
    def step(ti, hs):
        hs = list(hs)
        for s in range(SUB):
            t = ti * SUB + s
            row = ti * (subs * SUB) + s
            d = dl_ref[pl.ds(row, subs, stride=SUB), :]
            u = du_sc[pl.ds(row, subs, stride=SUB), :]
            d = jnp.where(keep_ref[chunk*rows + t] > 0, d, BIG)
            y = None
            for n in range(states):
                b = bb_sc[pl.ds((ti*2*states + n)*SUB + s, subs, stride=0), :]
                c = bb_sc[pl.ds((ti*2*states + states + n)*SUB + s, subs, stride=0), :]
                hs[n] = jnp.exp2(d * decs[n]) * hs[n] + u * b
                hs_ref[pl.ds(pl.multiple_of((t + 1) * span + n*subs, subs), subs), :] = hs[n]
                y = c * hs[n] if y is None else y + c * hs[n]
            y_sc[pl.ds(row, subs, stride=SUB), :] = y
        return tuple(hs)
    hs = lax.fori_loop(0, rows // SUB, step, tuple(h_sc[pl.ds(n*subs, subs), :] for n in range(states)))
    for n in range(states):
        h_sc[pl.ds(n*subs, subs), :] = hs[n]
    total = get_tiles(y_sc, rows, subs) + ds_ref[...] * inner
    ys_ref[...] = total
    gate = gate_ref[...]
    gated_ref[...] = (total * gate / (1.0 + jnp.exp(-gate))).astype(bf16)

def scan_forward(keep, step_in, bc, wdt, dt_bias, d_skip, dec, inner, gate, chunk_rows=64):
    rows, channels = inner.shape
    subs = channels // LANES
    states = bc.shape[1] // 2
    rank = step_in.shape[1]
    nch = rows // chunk_rows
    span = states * subs
    row_block = lambda w: pl.BlockSpec((chunk_rows, w), lambda i, *_: (i, 0))
    whole = lambda a: pl.BlockSpec(a.shape, lambda i, *_: (0,) * a.ndim)
    grid_spec = pltpu.PrefetchScalarGridSpec(
        num_scalar_prefetch=1, grid=(nch,),
        in_specs=[row_block(rank), row_block(2*states), whole(wdt), whole(dt_bias), whole(d_skip), whole(dec), row_block(channels), row_block(channels)],
        out_specs=[pl.BlockSpec(((chunk_rows+1)*span, LANES), lambda i, *_: (i, 0)),
                   pl.BlockSpec((chunk_rows*subs, LANES), lambda i, *_: (i, 0)), row_block(channels), row_block(channels)],
        scratch_shapes=[pltpu.VMEM((span, LANES), f32), pltpu.VMEM((chunk_rows*subs, LANES), f32),
                        pltpu.VMEM((chunk_rows*2*states, LANES), f32), pltpu.VMEM((chunk_rows*subs, LANES), f32)])
    return pl.pallas_call(
        functools.partial(fwd_body, states, subs), grid_spec=grid_spec,
        out_shape=[jax.ShapeDtypeStruct((nch*(chunk_rows+1)*span, LANES), f32), jax.ShapeDtypeStruct((rows*subs, LANES), f32),
                   jax.ShapeDtypeStruct((rows, channels), f32), jax.ShapeDtypeStruct((rows, channels), bf16)],
        compiler_params=pltpu.CompilerParams(vmem_limit_bytes=48 << 20), name="scan_forward",
    )(keep, step_in, bc, wdt, dt_bias, d_skip, dec, inner, gate)

def fold_rows(parts, sub_iota):
    if parts[0].shape[0] != SUB:
        return jnp.concatenate([jnp.sum(p, axis=0, keepdims=True) for p in parts], axis=0)
    up = sub_iota < 4
    xs = [jnp.where(up, parts[n], parts[n+4]) + pltpu.roll(jnp.where(up, parts[n+4], parts[n]), 4, 0) for n in range(4)]
    pair = (sub_iota & 3) < 2
    ys = [jnp.where(pair, xs[n] + pltpu.roll(xs[n], 6, 0), xs[n+2] + pltpu.roll(xs[n+2], 2, 0)) for n in range(2)]
    even = (sub_iota & 1) == 0
    return jnp.where(even, ys[0] + pltpu.roll(ys[0], 7, 0), ys[1] + pltpu.roll(ys[1], 1, 0))

def bwd_body(states, subs, keep_ref, bc_ref, wdt_ref, ds_ref, dst_ref, dec_ref, inner_ref, gate_ref, gg_ref, ys_ref, hs_ref, dl_ref,
             gi_ref, gx_ref, gp_ref, gstep_ref, gbc_ref, red_ref, acc_ref, gh_sc, in_sc, gy_sc, bb_sc, gd_sc, go_sc, r_sc):
    i = pl.program_id(0)
    last = pl.num_programs(0) - 1
    chunk = last - i
    rows = inner_ref.shape[0]
    all_rows = r_sc.shape[0] // (2 * states)
    span = states * subs
    @pl.when(i == 0)
    def _():
        gh_sc[...] = jnp.zeros_like(gh_sc)
        acc_ref[...] = jnp.zeros_like(acc_ref)
        red_ref[...] = jnp.zeros_like(red_ref)
    gate = gate_ref[...]
    sig = 1.0 / (1.0 + jnp.exp(-gate))
    gg = gg_ref[...].astype(f32)
    gy_all = gg * (gate * sig)
    gx_ref[...] = (gg * ys_ref[...] * (sig * (1.0 + gate * (1.0 - sig)))).astype(bf16)
    inner_all = inner_ref[...].astype(f32)
    red_ref[pl.ds(0, 1), :] += jnp.sum(gy_all * inner_all, axis=0, keepdims=True)
    put_tiles(gy_sc, gy_all, subs)
    put_tiles(in_sc, inner_all, subs)
    put_spread(bb_sc, bc_ref[...], 2 * states)
    sub_iota = lax.broadcasted_iota(jnp.int32, (SUB, LANES), 0)
    skip = dst_ref[...]
    order = (0, 4, 2, 6, 1, 5, 3, 7)
    def step(k, carried):
        ghs = list(carried[:states]); accs = list(carried[states:])
        ti = rows // SUB - 1 - k
        for s in reversed(range(SUB)):
            t = ti * SUB + s
            row = ti * (subs * SUB) + s
            d = dl_ref[pl.ds(row, subs, stride=SUB), :]
            v = in_sc[pl.ds(row, subs, stride=SUB), :]
            gy = gy_sc[pl.ds(row, subs, stride=SUB), :]
            u = d * v
            da = jnp.where(keep_ref[chunk*rows + t] > 0, d, BIG)
            gd = gs = None
            for g in range(states // SUB):
                pb = [None]*SUB; pc = [None]*SUB
                for o in order:
                    n = g*SUB + o
                    b = bb_sc[pl.ds((ti*2*states + n)*SUB + s, subs, stride=0), :]
                    c = bb_sc[pl.ds((ti*2*states + states + n)*SUB + s, subs, stride=0), :]
                    dec = dec_ref[pl.ds(n*subs, subs), :]
                    before = hs_ref[pl.ds(pl.multiple_of(t*span + n*subs, subs), subs), :]
                    after = hs_ref[pl.ds(pl.multiple_of((t+1)*span + n*subs, subs), subs), :]
                    gh = c * gy + ghs[n]
                    ghs[n] = jnp.exp2(da * dec) * gh
                    q = ghs[n] * before
                    gd = dec * q if gd is None else gd + dec * q
                    accs[n] = accs[n] + q * d
                    gs = gh * b if gs is None else gs + gh * b
                    pb[o] = gh * u
                    pc[o] = after * gy
                r_sc[pl.ds(g*SUB*all_rows + chunk*rows + t, SUB, stride=all_rows), :] = fold_rows(pb, sub_iota)
                r_sc[pl.ds((states + g*SUB)*all_rows + chunk*rows + t, SUB, stride=all_rows), :] = fold_rows(pc, sub_iota)
            gd_sc[pl.ds(row, subs, stride=SUB), :] = gd * math.log(2.0) + gs * v
            go_sc[pl.ds(row, subs, stride=SUB), :] = gy * skip + gs * d
        return tuple(ghs + accs)
    init = tuple(gh_sc[pl.ds(n*subs, subs), :] for n in range(states)) + tuple(acc_ref[pl.ds(n*subs, subs), :] for n in range(states))
    out = lax.fori_loop(0, rows // SUB, step, init)
    for n in range(states):
        gh_sc[pl.ds(n*subs, subs), :] = out[n]
        acc_ref[pl.ds(n*subs, subs), :] = out[states+n]
    gi_ref[...] = get_tiles(go_sc, rows, subs)
    d_all = get_tiles(dl_ref, rows, subs)
    small = d_all * (1.0 - d_all * (0.5 - d_all * (1.0/6 - d_all * (1.0/24))))
    slope = jnp.where(d_all < 0.03125, small, 1.0 - jnp.exp(-d_all))
    gp = get_tiles(gd_sc, rows, subs) * slope
    red_ref[pl.ds(1, 1), :] += jnp.sum(gp, axis=0, keepdims=True)
    low = gp.astype(bf16)
    gp_ref[...] = low
    gstep_ref[...] = lax.dot_general(low, wdt_ref[...], (((1,), (1,)), ((), ())), preferred_element_type=f32)
    @pl.when(i == last)
    def _():
        lane = lax.broadcasted_iota(jnp.int32, (LANES, LANES), 1)
        total = jnp.zeros((all_rows, LANES), f32)
        for n in range(2 * states):
            pick = jnp.where(lane == n, 1.0, 0.0).astype(bf16)
            total = total + jnp.dot(r_sc[pl.ds(n*all_rows, all_rows), :].astype(bf16), pick, preferred_element_type=f32)
        gbc_ref[...] = total

def scan_backward(keep, bc, wdt, d_skip, d_skip_tm, dec, inner, gate, gg, ysum, hs, delta_tm, chunk_rows=64):
    rows, channels = inner.shape
    subs = channels // LANES
    states = bc.shape[1] // 2
    rank = wdt.shape[0]
    nch = rows // chunk_rows
    span = states * subs
    rev = lambda i, *_: (nch - 1 - i, 0)
    row_block = lambda w: pl.BlockSpec((chunk_rows, w), rev)
    whole = lambda a: pl.BlockSpec(a.shape, lambda i, *_: (0,) * a.ndim)
    fixed = lambda shape: pl.BlockSpec(shape, lambda i, *_: (0, 0))
    tm = pltpu.VMEM((chunk_rows*subs, LANES), f32)
    grid_spec = pltpu.PrefetchScalarGridSpec(
        num_scalar_prefetch=1, grid=(nch,),
        in_specs=[row_block(2*states), whole(wdt), whole(d_skip), whole(d_skip_tm), whole(dec), row_block(channels), row_block(channels), row_block(channels), row_block(channels),
                  pl.BlockSpec(((chunk_rows+1)*span, LANES), rev), pl.BlockSpec((chunk_rows*subs, LANES), rev)],
        out_specs=[row_block(channels), row_block(channels), row_block(channels), row_block(rank), fixed((rows, LANES)), fixed((8, channels)), fixed((span, LANES))],
        scratch_shapes=[pltpu.VMEM((span, LANES), f32), tm, tm, pltpu.VMEM((chunk_rows*2*states, LANES), f32), tm, tm, pltpu.VMEM((2*states*rows, LANES), f32)])
    S = jax.ShapeDtypeStruct
    return pl.pallas_call(
        functools.partial(bwd_body, states, subs), grid_spec=grid_spec,
        out_shape=[S((rows, channels), f32), S((rows, channels), bf16), S((rows, channels), bf16), S((rows, rank), f32), S((rows, LANES), f32), S((8, channels), f32), S((span, LANES), f32)],
        compiler_params=pltpu.CompilerParams(vmem_limit_bytes=56 << 20), name="scan_backward",
    )(keep, bc, wdt, d_skip, d_skip_tm, dec, inner, gate, gg, ysum, hs, delta_tm)


def shards(
    hidden,
    cotangent,
    seq_lengths,
    pack_order,
    norm_gain,
    w_in,
    conv_weight,
    conv_bias,
    w_xproj,
    w_dt,
    dt_bias,
    a_log,
    d_skip,
    w_out,
):
    n_fsdp = lax.axis_size("fsdp")
    n_tensor = lax.axis_size("tensor")
    tok_rows = hidden.shape[0]
    group_rows = tok_rows * n_tensor
    rank_cols = w_dt.shape[1]
    state_cols = a_log.shape[1]
    gathered = (
        lax.all_gather(w_in, "fsdp", axis=1, tiled=True),
        lax.all_gather(conv_weight, "fsdp", axis=0, tiled=True),
        lax.all_gather(conv_bias, "fsdp", axis=0, tiled=True),
        lax.all_gather(w_xproj, "fsdp", axis=0, tiled=True),
        lax.all_gather(w_dt, "fsdp", axis=0, tiled=True),
        lax.all_gather(dt_bias, "fsdp", axis=0, tiled=True),
        lax.all_gather(a_log, "fsdp", axis=0, tiled=True),
        lax.all_gather(d_skip, "fsdp", axis=0, tiled=True),
        lax.all_gather(w_out, "fsdp", axis=0, tiled=True),
        lax.all_gather(norm_gain, "fsdp", axis=0, tiled=True),
    )
    w_in_t, conv_w_t, conv_b_t, w_x_t, w_dt_t, dt_b_t, a_log_t, d_skip_t, w_out_t, gain_fsdp = (
        gathered
    )
    rows_all, gain_tensor = (
        lax.all_gather(hidden, "tensor", axis=0, tiled=True),
        lax.all_gather(gain_fsdp, "tensor", axis=0, tiled=True),
    )
    gain_full = gain_tensor.reshape(n_tensor, n_fsdp, -1).transpose(1, 0, 2).reshape(-1).astype(f32)
    offsets = distances(seq_lengths[0], pack_order[0], group_rows)
    row_values = rows_all.astype(f32)
    normed = normalize(row_values, gain_full).astype(bf16)
    xz_all = jnp.einsum("gd,hcd->ghc", normed, w_in_t, preferred_element_type=f32)
    signal = xz_all[:, 0]
    gate_in = xz_all[:, 1]
    inner, front_back = jax.vjp(
        lambda signal_in, taps_in, biases_in: jax.nn.silu(
            convolve(signal_in, taps_in, biases_in, offsets)
        ),
        signal,
        conv_w_t.astype(f32),
        conv_b_t.astype(f32),
    )
    inner_low = inner.astype(bf16)
    pieces_x = jnp.dot(inner_low, w_x_t, preferred_element_type=f32)
    mixed = lax.psum(pieces_x, "tensor")
    step_in = mixed[:, :rank_cols].astype(bf16)
    b_in = mixed[:, rank_cols : rank_cols + state_cols]
    c_out = mixed[:, rank_cols + state_cols :]
    keep = (offsets > 0).astype(jnp.int32)
    bc = mixed[:, rank_cols:]
    channels = inner_low.shape[1]
    decays = -jnp.exp(a_log_t.astype(f32)).T
    rates = (decays * math.log2(math.e)).reshape(-1, LANES)
    w_dt_rows = w_dt_t.T
    skip_row = d_skip_t.astype(f32)[None, :]
    states, deltas, sums, gated_low = scan_forward(
        keep, step_in, bc, w_dt_rows, dt_b_t.astype(f32)[None, :], skip_row, rates, inner_low, gate_in
    )
    branch = lax.psum_scatter(
        jnp.dot(gated_low, w_out_t, preferred_element_type=f32),
        "tensor",
        scatter_dimension=0,
        tiled=True,
    )
    output = (hidden.astype(f32) + branch).astype(bf16)
    cot_all = lax.all_gather(cotangent, "tensor", axis=0, tiled=True)
    grad_gated = jnp.einsum("gd,cd->gc", cot_all, w_out_t, preferred_element_type=f32).astype(bf16)
    out_grad = jnp.einsum("gc,gd->cd", gated_low, cot_all, preferred_element_type=f32)
    g_inner_scan, g_gate, g_proj_low, g_step, g_bc, sums_c, acc_a = scan_backward(
        keep, bc, w_dt_rows, skip_row, skip_row.reshape(-1, LANES), rates, inner_low, gate_in, grad_gated, sums, states, deltas
    )
    g_d_skip = sums_c[0]
    g_dt_bias = sums_c[1]
    g_a_log = (acc_a.reshape(state_cols, channels) * decays).T
    w_dt_grad = jnp.einsum("gc,gr->cr", g_proj_low, step_in, preferred_element_type=f32)
    mixed_grad = lax.psum(jnp.concatenate([g_step, g_bc[:, : 2 * state_cols]], axis=1), "tensor")
    mixed_low = mixed_grad.astype(bf16)
    g_inner = g_inner_scan + jnp.einsum("gk,ck->gc", mixed_low, w_x_t, preferred_element_type=f32)
    w_x_grad = jnp.einsum("gc,gk->ck", inner_low, mixed_low, preferred_element_type=f32)
    g_signal, g_conv_w, g_conv_b = front_back(g_inner)
    g_xz = jnp.stack([g_signal.astype(bf16), g_gate], axis=1)
    w_in_grad = jnp.einsum("ghc,gd->hcd", g_xz, normed, preferred_element_type=f32)
    g_normed = jnp.einsum("ghc,hcd->gd", g_xz, w_in_t, preferred_element_type=f32)
    gain_term = jax.vjp(lambda scales: normalize(row_values, scales), gain_full)[1](g_normed)[0]
    gain_term = gain_term.reshape(n_fsdp, n_tensor, -1).transpose(1, 0, 2).reshape(-1)
    g_norm_own, gain_part = (
        lax.psum_scatter(g_normed, "tensor", scatter_dimension=0, tiled=True),
        lax.psum_scatter(gain_term, "tensor", scatter_dimension=0, tiled=True),
    )
    norm_back = jax.vjp(lambda own_values: normalize(own_values, gain_full), hidden.astype(f32))[1]
    grad_hidden = cotangent.astype(f32) + norm_back(g_norm_own)[0]
    results = (
        lax.psum_scatter(w_in_grad, "fsdp", scatter_dimension=1, tiled=True),
        lax.psum_scatter(g_conv_w, "fsdp", scatter_dimension=0, tiled=True),
        lax.psum_scatter(g_conv_b, "fsdp", scatter_dimension=0, tiled=True),
        lax.psum_scatter(w_x_grad, "fsdp", scatter_dimension=0, tiled=True),
        lax.psum_scatter(w_dt_grad, "fsdp", scatter_dimension=0, tiled=True),
        lax.psum_scatter(g_dt_bias, "fsdp", scatter_dimension=0, tiled=True),
        lax.psum_scatter(g_a_log, "fsdp", scatter_dimension=0, tiled=True),
        lax.psum_scatter(g_d_skip, "fsdp", scatter_dimension=0, tiled=True),
        lax.psum_scatter(out_grad, "fsdp", scatter_dimension=0, tiled=True),
        lax.psum_scatter(gain_part, "fsdp", scatter_dimension=0, tiled=True),
    )
    return (
        output,
        grad_hidden,
        results[9],
        results[0],
        results[1],
        results[2],
        results[3],
        results[4],
        results[5],
        results[6],
        results[7],
        results[8],
    )


def solution(mesh):
    placed = (
        P(("fsdp", "tensor"), None),
        P(("fsdp", "tensor"), None),
        P("fsdp", None),
        P("fsdp", None),
        P(("fsdp", "tensor")),
        P(None, ("fsdp", "tensor"), None),
        P(("fsdp", "tensor"), None),
        P(("fsdp", "tensor")),
        P(("fsdp", "tensor"), None),
        P(("fsdp", "tensor"), None),
        P(("fsdp", "tensor")),
        P(("fsdp", "tensor"), None),
        P(("fsdp", "tensor")),
        P(("fsdp", "tensor"), None),
    )
    return jax.shard_map(
        shards,
        mesh=mesh,
        in_specs=placed,
        out_specs=(
            P(("fsdp", "tensor"), None),
            P(("fsdp", "tensor"), None),
            P(("fsdp", "tensor")),
            P(None, ("fsdp", "tensor"), None),
            P(("fsdp", "tensor"), None),
            P(("fsdp", "tensor")),
            P(("fsdp", "tensor"), None),
            P(("fsdp", "tensor"), None),
            P(("fsdp", "tensor")),
            P(("fsdp", "tensor"), None),
            P(("fsdp", "tensor")),
            P(("fsdp", "tensor"), None),
        ),
        check_vma=False,
    )
```

```python
import functools
import math

import jax
import jax.numpy as jnp
from jax import lax
from jax.experimental import pallas as pl
from jax.experimental.pallas import tpu as pltpu
from jax.sharding import PartitionSpec as P

EPSILON = 1e-05
f32 = jnp.float32
bf16 = jnp.bfloat16
BIG = 1e30
LANES = 128
SUB = 8


def cost(micros):
    return pl.CostEstimate(flops=int(micros * 1e9), transcendentals=0, bytes_accessed=int(micros * 1e6))


def tile_rows(ti, j, subs):
    return pl.ds((ti * subs + j) * SUB, SUB)


def put_tiles(ref, value, subs):
    for ti in range(value.shape[0] // SUB):
        for j in range(subs):
            ref[tile_rows(ti, j, subs), :] = value[ti * SUB : (ti + 1) * SUB, j * LANES : (j + 1) * LANES]


def get_tiles(ref, rows, subs):
    lines = []
    for ti in range(rows // SUB):
        lines.append(jnp.concatenate([ref[tile_rows(ti, j, subs), :] for j in range(subs)], axis=1))
    return jnp.concatenate(lines, axis=0)


def put_spread(ref, value, count):
    for ti in range(value.shape[0] // SUB):
        for n in range(count):
            ref[pl.ds((ti * count + n) * SUB, SUB), :] = jnp.broadcast_to(
                value[ti * SUB : (ti + 1) * SUB, n : n + 1], (SUB, LANES)
            )


def fwd_body(
    states, subs, keep_ref, step_ref, bc_ref, wdt_ref, db_ref, ds_ref, dec_ref, inner_ref, gate_ref, h0_ref,
    hs_ref, dl_ref, ys_ref, gated_ref, h_ref, du_sc, bb_sc, y_sc,
):
    chunk = pl.program_id(0)
    rows = step_ref.shape[0]
    span = states * subs

    @pl.when(chunk == 0)
    def _():
        h_ref[...] = h0_ref[...]

    raw = jnp.dot(step_ref[...], wdt_ref[...], preferred_element_type=f32) + db_ref[...]
    delta = jnp.maximum(raw, 0.0) + jnp.log1p(jnp.exp(-jnp.abs(raw)))
    inner = inner_ref[...].astype(f32)
    put_tiles(dl_ref, delta, subs)
    put_tiles(du_sc, delta * inner, subs)
    put_spread(bb_sc, bc_ref[...], 2 * states)
    hs_ref[pl.ds(0, span), :] = h_ref[...]
    decs = [dec_ref[pl.ds(n * subs, subs), :] for n in range(states)]

    def step(ti, hs):
        hs = list(hs)
        for s in range(SUB):
            t = ti * SUB + s
            row = ti * (subs * SUB) + s
            d = dl_ref[pl.ds(row, subs, stride=SUB), :]
            u = du_sc[pl.ds(row, subs, stride=SUB), :]
            d = jnp.where(keep_ref[chunk * rows + t] > 0, d, BIG)
            y = None
            for n in range(states):
                b = bb_sc[pl.ds((ti * 2 * states + n) * SUB + s, subs, stride=0), :]
                c = bb_sc[pl.ds((ti * 2 * states + states + n) * SUB + s, subs, stride=0), :]
                hs[n] = jnp.exp2(d * decs[n]) * hs[n] + u * b
                hs_ref[pl.ds(pl.multiple_of((t + 1) * span + n * subs, subs), subs), :] = hs[n]
                y = c * hs[n] if y is None else y + c * hs[n]
            y_sc[pl.ds(row, subs, stride=SUB), :] = y
        return tuple(hs)

    start = tuple(h_ref[pl.ds(n * subs, subs), :] for n in range(states))
    hs = lax.fori_loop(0, rows // SUB, step, start)
    for n in range(states):
        h_ref[pl.ds(n * subs, subs), :] = hs[n]
    total = get_tiles(y_sc, rows, subs) + ds_ref[...] * inner
    ys_ref[...] = total
    gate = gate_ref[...]
    gated_ref[...] = (total * gate / (1.0 + jnp.exp(-gate))).astype(bf16)


def scan_forward(keep, step_in, bc, wdt, dt_bias, d_skip, dec, inner, gate, h0, chunk_rows=64):
    rows, channels = inner.shape
    subs = channels // LANES
    states = bc.shape[1] // 2
    rank = step_in.shape[1]
    chunks = rows // chunk_rows
    span = states * subs

    def row_block(width):
        return pl.BlockSpec((chunk_rows, width), lambda i, *_: (i, 0))

    def whole(a):
        return pl.BlockSpec(a.shape, lambda i, *_: (0, 0))

    grid_spec = pltpu.PrefetchScalarGridSpec(
        num_scalar_prefetch=1,
        grid=(chunks,),
        in_specs=[
            row_block(rank), row_block(2 * states), whole(wdt), whole(dt_bias), whole(d_skip), whole(dec),
            row_block(channels), row_block(channels), whole(h0),
        ],
        out_specs=[
            pl.BlockSpec(((chunk_rows + 1) * span, LANES), lambda i, *_: (i, 0)),
            pl.BlockSpec((chunk_rows * subs, LANES), lambda i, *_: (i, 0)),
            row_block(channels), row_block(channels), whole(h0),
        ],
        scratch_shapes=[
            pltpu.VMEM((chunk_rows * subs, LANES), f32),
            pltpu.VMEM((chunk_rows * 2 * states, LANES), f32),
            pltpu.VMEM((chunk_rows * subs, LANES), f32),
        ],
    )
    made = jax.ShapeDtypeStruct
    return pl.pallas_call(
        functools.partial(fwd_body, states, subs),
        grid_spec=grid_spec,
        out_shape=[
            made((chunks * (chunk_rows + 1) * span, LANES), f32), made((rows * subs, LANES), f32),
            made((rows, channels), f32), made((rows, channels), bf16), made((span, LANES), f32),
        ],
        compiler_params=pltpu.CompilerParams(vmem_limit_bytes=58 << 20),
        cost_estimate=cost(1.0 * rows * channels / (512 * 1024)),
        name="scan_forward",
    )(keep, step_in, bc, wdt, dt_bias, d_skip, dec, inner, gate, h0)


def fold_rows(parts, sub_iota):
    if parts[0].shape[0] != SUB:
        return jnp.concatenate([jnp.sum(p, axis=0, keepdims=True) for p in parts], axis=0)
    upper = sub_iota < 4
    xs = [
        jnp.where(upper, parts[n], parts[n + 4]) + pltpu.roll(jnp.where(upper, parts[n + 4], parts[n]), 4, 0)
        for n in range(4)
    ]
    pair = (sub_iota & 3) < 2
    ys = [
        jnp.where(pair, xs[n] + pltpu.roll(xs[n], 6, 0), xs[n + 2] + pltpu.roll(xs[n + 2], 2, 0))
        for n in range(2)
    ]
    even = (sub_iota & 1) == 0
    return jnp.where(even, ys[0] + pltpu.roll(ys[0], 7, 0), ys[1] + pltpu.roll(ys[1], 1, 0))


def bwd_body(
    states, subs, keep_ref, bc_ref, wdt_ref, ds_ref, dst_ref, dec_ref, inner_ref, gate_ref, gg_ref, ys_ref, hs_ref,
    dl_ref, gh0_ref, gi_ref, gx_ref, gp_ref, mixed_ref, red_ref, acc_ref, gh_ref, in_sc, gy_sc, bb_sc, gd_sc, go_sc,
    r_sc,
):
    i = pl.program_id(0)
    last = pl.num_programs(0) - 1
    chunk = last - i
    rows = inner_ref.shape[0]
    all_rows = r_sc.shape[0] // (2 * states)
    span = states * subs
    rank = wdt_ref.shape[0]

    @pl.when(i == 0)
    def _():
        gh_ref[...] = gh0_ref[...]
        acc_ref[...] = jnp.zeros_like(acc_ref)
        red_ref[...] = jnp.zeros_like(red_ref)

    gate = gate_ref[...]
    sig = 1.0 / (1.0 + jnp.exp(-gate))
    gg = gg_ref[...].astype(f32)
    gy_all = gg * (gate * sig)
    gx_ref[...] = (gg * ys_ref[...] * (sig * (1.0 + gate * (1.0 - sig)))).astype(bf16)
    inner_all = inner_ref[...].astype(f32)
    red_ref[pl.ds(0, 1), :] += jnp.sum(gy_all * inner_all, axis=0, keepdims=True)
    put_tiles(gy_sc, gy_all, subs)
    put_tiles(in_sc, inner_all, subs)
    put_spread(bb_sc, bc_ref[...], 2 * states)
    sub_iota = lax.broadcasted_iota(jnp.int32, (SUB, LANES), 0)
    skip = dst_ref[...]
    order = (0, 4, 2, 6, 1, 5, 3, 7)

    def step(k, carried):
        ghs = list(carried[:states])
        accs = list(carried[states:])
        ti = rows // SUB - 1 - k
        for s in reversed(range(SUB)):
            t = ti * SUB + s
            row = ti * (subs * SUB) + s
            d = dl_ref[pl.ds(row, subs, stride=SUB), :]
            v = in_sc[pl.ds(row, subs, stride=SUB), :]
            gy = gy_sc[pl.ds(row, subs, stride=SUB), :]
            u = d * v
            da = jnp.where(keep_ref[chunk * rows + t] > 0, d, BIG)
            gd = gs = None
            for g in range(states // SUB):
                pb = [None] * SUB
                pc = [None] * SUB
                for o in order:
                    n = g * SUB + o
                    b = bb_sc[pl.ds((ti * 2 * states + n) * SUB + s, subs, stride=0), :]
                    c = bb_sc[pl.ds((ti * 2 * states + states + n) * SUB + s, subs, stride=0), :]
                    dec = dec_ref[pl.ds(n * subs, subs), :]
                    before = hs_ref[pl.ds(pl.multiple_of(t * span + n * subs, subs), subs), :]
                    after = hs_ref[pl.ds(pl.multiple_of((t + 1) * span + n * subs, subs), subs), :]
                    gh = c * gy + ghs[n]
                    ghs[n] = jnp.exp2(da * dec) * gh
                    q = ghs[n] * before
                    gd = dec * q if gd is None else gd + dec * q
                    accs[n] = accs[n] + q * d
                    gs = gh * b if gs is None else gs + gh * b
                    pb[o] = gh * u
                    pc[o] = after * gy
                at = chunk * rows + t
                r_sc[pl.ds(g * SUB * all_rows + at, SUB, stride=all_rows), :] = fold_rows(pb, sub_iota)
                r_sc[pl.ds((states + g * SUB) * all_rows + at, SUB, stride=all_rows), :] = fold_rows(pc, sub_iota)
            gd_sc[pl.ds(row, subs, stride=SUB), :] = gd * math.log(2.0) + gs * v
            go_sc[pl.ds(row, subs, stride=SUB), :] = gy * skip + gs * d
        return tuple(ghs + accs)

    init = tuple(gh_ref[pl.ds(n * subs, subs), :] for n in range(states))
    init = init + tuple(acc_ref[pl.ds(n * subs, subs), :] for n in range(states))
    out = lax.fori_loop(0, rows // SUB, step, init)
    for n in range(states):
        gh_ref[pl.ds(n * subs, subs), :] = out[n]
        acc_ref[pl.ds(n * subs, subs), :] = out[states + n]
    gi_ref[...] = get_tiles(go_sc, rows, subs)
    d_all = get_tiles(dl_ref, rows, subs)
    series = d_all * (1.0 - d_all * (0.5 - d_all * (1.0 / 6 - d_all * (1.0 / 24))))
    slope = jnp.where(d_all < 0.03125, series, 1.0 - jnp.exp(-d_all))
    gp = get_tiles(gd_sc, rows, subs) * slope
    red_ref[pl.ds(1, 1), :] += jnp.sum(gp, axis=0, keepdims=True)
    low = gp.astype(bf16)
    gp_ref[...] = low
    mixed_ref[pl.ds(pl.multiple_of(chunk * rows, rows), rows), pl.ds(0, rank)] = lax.dot_general(
        low, wdt_ref[...], (((1,), (1,)), ((), ())), preferred_element_type=f32
    ).astype(bf16)

    @pl.when(i == last)
    def _():
        lane = lax.broadcasted_iota(jnp.int32, (LANES, LANES), 1)
        total = jnp.zeros((all_rows, LANES), f32)
        for n in range(2 * states):
            pick = jnp.where(lane == n, 1.0, 0.0).astype(bf16)
            part = r_sc[pl.ds(n * all_rows, all_rows), :].astype(bf16)
            total = total + jnp.dot(part, pick, preferred_element_type=f32)
        mixed_ref[:, pl.ds(rank, 2 * states)] = total[:, : 2 * states].astype(bf16)


def scan_backward(h, keep, bc, wdt, d_skip, dec, inner, gate, gg, ysum, hs, delta_tm, gh0, chunk_rows=64):
    rows, channels = inner.shape
    subs = channels // LANES
    states = bc.shape[1] // 2
    rank = wdt.shape[0]
    chunks = rows // chunk_rows
    span = states * subs
    skip_tm = d_skip.reshape(subs, LANES)

    def back(i, *_):
        return (chunks - 1 - i, 0)

    def row_block(width):
        return pl.BlockSpec((chunk_rows, width), back)

    def fixed(shape):
        return pl.BlockSpec(shape, lambda i, *_: (0, 0))

    tile = pltpu.VMEM((chunk_rows * subs, LANES), f32)
    grid_spec = pltpu.PrefetchScalarGridSpec(
        num_scalar_prefetch=1,
        grid=(chunks,),
        in_specs=[
            row_block(2 * states), fixed(wdt.shape), fixed(d_skip.shape), fixed(skip_tm.shape), fixed(dec.shape),
            row_block(channels), row_block(channels),
            pl.BlockSpec((chunk_rows, channels), lambda i, *_: (h * chunks + chunks - 1 - i, 0)), row_block(channels),
            pl.BlockSpec(((chunk_rows + 1) * span, LANES), back),
            pl.BlockSpec((chunk_rows * subs, LANES), back), fixed(gh0.shape),
        ],
        out_specs=[
            row_block(channels), row_block(channels), row_block(channels), fixed((rows, rank + 2 * states)),
            fixed((8, channels)), fixed((span, LANES)), fixed((span, LANES)),
        ],
        scratch_shapes=[
            tile, tile, pltpu.VMEM((chunk_rows * 2 * states, LANES), f32), tile, tile,
            pltpu.VMEM((2 * states * rows, LANES), f32),
        ],
    )
    made = jax.ShapeDtypeStruct
    return pl.pallas_call(
        functools.partial(bwd_body, states, subs),
        grid_spec=grid_spec,
        out_shape=[
            made((rows, channels), f32), made((rows, channels), bf16), made((rows, channels), bf16),
            made((rows, rank + 2 * states), bf16), made((8, channels), f32), made((span, LANES), f32),
            made((span, LANES), f32),
        ],
        compiler_params=pltpu.CompilerParams(vmem_limit_bytes=58 << 20),
        cost_estimate=cost(45.0 * rows * channels / (512 * 1024)),
        name="scan_backward",
    )(keep, bc, wdt, d_skip, skip_tm, dec, inner, gate, gg, ysum, hs, delta_tm, gh0)


def norm_body(gain_ref, rows_ref, out_ref):
    value = rows_ref[...].astype(f32)
    factor = lax.rsqrt(jnp.mean(value * value, axis=1, keepdims=True) + EPSILON)
    out_ref[...] = (value * factor * gain_ref[...]).astype(bf16)


def norm_rows(rows_all, gain, parts):
    rows, width = rows_all.shape
    block = pl.BlockSpec((rows // parts, width), lambda i: (i, 0))
    return pl.pallas_call(
        norm_body,
        grid=(parts,),
        in_specs=[pl.BlockSpec(gain.shape, lambda i: (0, 0)), block],
        out_specs=block,
        out_shape=jax.ShapeDtypeStruct((rows, width), bf16),
        compiler_params=pltpu.CompilerParams(vmem_limit_bytes=24 << 20),
        cost_estimate=cost(3.0),
        name="norm_rows",
    )(gain, rows_all)


def split_specs(channels, width):
    chunk = min(256, channels // 2)
    half = channels // 2 // chunk
    first = pl.BlockSpec((chunk, width), lambda i, *_: (jnp.minimum(i, half - 1), 0))
    second = pl.BlockSpec((chunk, width), lambda i, *_: (jnp.maximum(i - half, 0), 0))
    return chunk, half, [first, second]


def front_body(
    half, normed_ref, xa_ref, xb_ref, ga_ref, gb_ref, taps_ref, bias_ref, wxp_ref, dist_ref, halo_ref, sig_ref, gate_ref,
    inner_ref, mixed_ref, ext_sc, acc_sc,
):
    i = pl.program_id(0)
    rows = normed_ref.shape[0]
    dims = (((1,), (1,)), ((), ()))

    def project(x_ref, g_ref):
        normed = normed_ref[...]
        ext_sc[pl.ds(SUB, rows), :] = lax.dot_general(normed, x_ref[...], dims, preferred_element_type=f32)
        gate_ref[...] = lax.dot_general(normed, g_ref[...], dims, preferred_element_type=f32)

    @pl.when(i < half)
    def _():
        project(xa_ref, ga_ref)

    @pl.when(i >= half)
    def _():
        project(xb_ref, gb_ref)

    ext_sc[pl.ds(0, SUB), :] = halo_ref[...]
    taps = taps_ref.shape[0]
    signal = ext_sc[pl.ds(SUB, rows), :]
    sig_ref[...] = signal
    dist = dist_ref[...]
    pre = bias_ref[...] + taps_ref[pl.ds(taps - 1, 1), :] * signal
    for lag in range(1, taps):
        shifted = ext_sc[pl.ds(SUB - lag, rows), :]
        pre = pre + jnp.where(dist >= lag, taps_ref[pl.ds(taps - 1 - lag, 1), :] * shifted, 0.0)
    inner = (pre / (1.0 + jnp.exp(-pre))).astype(bf16)
    inner_ref[...] = inner
    part = lax.dot_general(inner, wxp_ref[...], dims, preferred_element_type=f32)

    @pl.when(i == 0)
    def _():
        acc_sc[...] = part

    @pl.when(i > 0)
    def _():
        acc_sc[...] += part

    mixed_ref[...] = acc_sc[...].astype(bf16)


def front(h, rows, normed, w_x, w_g, taps, bias, w_xp, dist, halo):
    width = normed.shape[1]
    channels = taps.shape[1]
    chunk, half, pair = split_specs(channels, width)
    xw = w_xp.shape[0]

    def columns(height):
        return pl.BlockSpec((height, chunk), lambda i: (0, i))

    made = jax.ShapeDtypeStruct
    return pl.pallas_call(
        functools.partial(front_body, half),
        grid=(2 * half,),
        in_specs=[pl.BlockSpec((rows, width), lambda i: (h, 0))]
        + pair
        + pair
        + [
            columns(taps.shape[0]), columns(1), columns(xw), pl.BlockSpec((rows, 1), lambda i: (h, 0)), columns(SUB),
        ],
        out_specs=[columns(rows), columns(rows), columns(rows), pl.BlockSpec((rows, xw), lambda i: (0, 0))],
        out_shape=[
            made((rows, channels), f32), made((rows, channels), f32), made((rows, channels), bf16),
            made((rows, xw), bf16),
        ],
        scratch_shapes=[pltpu.VMEM((rows + SUB, chunk), f32), pltpu.VMEM((rows, xw), f32)],
        compiler_params=pltpu.CompilerParams(vmem_limit_bytes=40 << 20),
        cost_estimate=cost(7.0),
        name="front",
    )(normed, *w_x, *w_g, taps, bias, w_xp, dist, halo)


def turn_body(
    mixed_ref, gis_ref, sig_ref, halo_ref, taps_ref, bias_ref, wxp_ref, dist_ref, next_ref, dnext_ref, gsig_ref, head_ref,
    sums_ref, ext_sc, late_sc,
):
    rows = gis_ref.shape[0]
    taps = taps_ref.shape[0]
    ext_sc[pl.ds(0, SUB), :] = halo_ref[...]
    ext_sc[pl.ds(SUB, rows), :] = sig_ref[...]
    dist = dist_ref[...]
    signal = sig_ref[...]
    pre = bias_ref[...] + taps_ref[pl.ds(taps - 1, 1), :] * signal
    for lag in range(1, taps):
        shifted = ext_sc[pl.ds(SUB - lag, rows), :]
        pre = pre + jnp.where(dist >= lag, taps_ref[pl.ds(taps - 1 - lag, 1), :] * shifted, 0.0)
    sig = 1.0 / (1.0 + jnp.exp(-pre))
    g_inner = gis_ref[...] + jnp.dot(mixed_ref[...], wxp_ref[...], preferred_element_type=f32)
    g_pre = g_inner * (sig * (1.0 + pre * (1.0 - sig)))
    head_ref[...] = g_pre[:SUB, :]
    lines = [None] * taps
    lines[taps - 1] = jnp.sum(g_pre * signal, axis=0, keepdims=True)
    g_signal = taps_ref[pl.ds(taps - 1, 1), :] * g_pre
    for lag in range(1, taps):
        masked = jnp.where(dist >= lag, g_pre, 0.0)
        lines[taps - 1 - lag] = jnp.sum(masked * ext_sc[pl.ds(SUB - lag, rows), :], axis=0, keepdims=True)
        late_sc[pl.ds(0, rows), :] = masked
        late_sc[pl.ds(rows, SUB), :] = jnp.where(dnext_ref[...] >= lag, next_ref[...], 0.0)
        g_signal = g_signal + taps_ref[pl.ds(taps - 1 - lag, 1), :] * late_sc[pl.ds(lag, rows), :]
    lines.append(jnp.sum(g_pre, axis=0, keepdims=True))
    sums_ref[...] = jnp.zeros_like(sums_ref)
    for k, value in enumerate(lines):
        sums_ref[pl.ds(k, 1), :] = value
    gsig_ref[...] = g_signal.astype(bf16)


def turn(h, mixed, gis, signal, halo, taps, bias, w_xp, dist, late, dist_late):
    rows, channels = gis.shape
    chunk = min(256, channels // 2)
    xw = w_xp.shape[0]

    def columns(height):
        return pl.BlockSpec((height, chunk), lambda i: (0, i))

    def fixed(a):
        return pl.BlockSpec(a.shape, lambda i: (0, 0))

    made = jax.ShapeDtypeStruct
    return pl.pallas_call(
        turn_body,
        grid=(channels // chunk,),
        in_specs=[
            fixed(mixed), columns(rows), columns(rows), columns(SUB), columns(taps.shape[0]), columns(1), columns(xw),
            pl.BlockSpec((rows, 1), lambda i: (h, 0)), columns(SUB), fixed(dist_late),
        ],
        out_specs=[columns(rows), columns(SUB), columns(SUB)],
        out_shape=[made((rows, channels), bf16), made((SUB, channels), f32), made((SUB, channels), f32)],
        scratch_shapes=[pltpu.VMEM((rows + SUB, chunk), f32), pltpu.VMEM((rows + SUB, chunk), f32)],
        compiler_params=pltpu.CompilerParams(vmem_limit_bytes=32 << 20),
        cost_estimate=cost(3.0),
        name="turn",
    )(mixed, gis, signal, halo, taps, bias, w_xp, dist, late, dist_late)


def rear_body(half, gs_ref, gx_ref, xa_ref, xb_ref, ga_ref, gb_ref, normed_ref, out_ref, gain_ref, acc_sc):
    i = pl.program_id(0)

    def product(x_ref, g_ref):
        return jnp.dot(gs_ref[...], x_ref[...], preferred_element_type=f32) + jnp.dot(
            gx_ref[...], g_ref[...], preferred_element_type=f32
        )

    @pl.when(i == 0)
    def _():
        acc_sc[...] = product(xa_ref, ga_ref)

    @pl.when(jnp.logical_and(i > 0, i < half))
    def _():
        acc_sc[...] += product(xa_ref, ga_ref)

    @pl.when(i >= half)
    def _():
        acc_sc[...] += product(xb_ref, gb_ref)

    @pl.when(i == pl.num_programs(0) - 1)
    def _():
        total = acc_sc[...]
        out_ref[...] = total.astype(bf16)
        gain_ref[...] = jnp.sum(total * normed_ref[...].astype(f32), axis=0, keepdims=True)


def rear(h, g_signal, g_gate, w_x, w_g, normed):
    width = normed.shape[1]
    rows, channels = g_signal.shape
    chunk, half, pair = split_specs(channels, width)
    columns = pl.BlockSpec((rows, chunk), lambda i: (0, i))
    made = jax.ShapeDtypeStruct
    return pl.pallas_call(
        functools.partial(rear_body, half),
        grid=(2 * half,),
        in_specs=[columns, columns] + pair + pair + [pl.BlockSpec((rows, width), lambda i: (h, 0))],
        out_specs=[pl.BlockSpec((rows, width), lambda i: (0, 0)), pl.BlockSpec((1, width), lambda i: (0, 0))],
        out_shape=[made((rows, width), bf16), made((1, width), f32)],
        scratch_shapes=[pltpu.VMEM((rows, width), f32)],
        compiler_params=pltpu.CompilerParams(vmem_limit_bytes=40 << 20),
        cost_estimate=cost(5.0),
        name="rear",
    )(g_signal, g_gate, *w_x, *w_g, normed)


def distances(lengths, pack_rows, row_count):
    slot_count = lengths.shape[0]
    picks = pack_rows[:, None] == jnp.arange(slot_count, dtype=jnp.int32)[None, :]
    packed = jnp.sum(jnp.where(picks, lengths[None, :], 0), axis=1)
    starts = jnp.cumsum(packed) - packed
    positions = jnp.arange(row_count, dtype=jnp.int32)
    latest = jnp.max(jnp.where(starts[None, :] <= positions[:, None], starts[None, :], 0), axis=1)
    return positions - latest


def after(value, *others):
    return lax.optimization_barrier((value,) + others)[0]


def swap(value, bit):
    count = lax.axis_size("fsdp")
    return lax.ppermute(value, "fsdp", [(i, i ^ bit) for i in range(count)])


def gather_wide(value, order, *waits):
    pieces = {0: value}
    size = value.shape[0]
    axis = 0
    for bit in order:
        keys = sorted(pieces)
        sent = jnp.concatenate([pieces[k] for k in keys], axis=axis) if len(keys) > 1 else value
        if len(keys) > 1 and waits:
            sent = after(sent, *waits)
        got = swap(sent, bit)
        for i, k in enumerate(keys):
            pieces[k | bit] = lax.slice_in_dim(got, i * size, (i + 1) * size, axis=axis)
    return jnp.concatenate([pieces[k] for k in sorted(pieces)], axis=axis)


def halves(blocks, order, axis):
    bit, rest = order[0], order[1:]
    leave = sorted(k for k in blocks if k & bit)
    stay = sorted(k for k in blocks if not k & bit)
    width = blocks[leave[0]].shape[axis]
    lows = [blocks[k].astype(bf16) for k in leave]
    sent = jnp.concatenate(lows, axis=axis) if len(lows) > 1 else lows[0]

    def back(got):
        cut = [lax.slice_in_dim(got, i * width, (i + 1) * width, axis=axis) for i in range(len(leave))]
        return {k: blocks[k].astype(f32) + cut[i].astype(f32) for i, k in enumerate(stay)}, rest

    return sent, back, bit


def reduce_bits(blocks, order, axis):
    while order:
        sent, back, bit = halves(blocks, order, axis)
        blocks, order = back(swap(sent, bit))
    return blocks[0]


class LineSum:
    def __init__(self, parts, low, high):
        self.parts, self.low, self.high = parts, low, high
        self.count = lax.axis_size("tensor")
        self.place = lax.axis_index("tensor")
        self.up = self.down = None
        self.step = 0

    def block(self, index):
        rows = self.parts.shape[0] // (self.high - self.low)
        start = (jnp.clip(index, self.low, self.high - 1) - self.low) * rows
        return lax.dynamic_slice_in_dim(self.parts, start, rows, 0).astype(f32)

    def go(self, *waits):
        self.step += 1
        step, count, sent = self.step, self.count, []
        self.parts = after(self.parts, *waits)
        pairs = [(i, i + 1) for i in range(step) if i + 1 < count and self.low <= count - step + i < self.high]
        if pairs:
            part = self.block(count - step + self.place)
            part = (part if self.up is None else part + self.up.astype(f32)).astype(bf16)
            sent.append(part)
            self.up = lax.ppermute(part, "tensor", pairs)
        pairs = [(i, i - 1) for i in range(count - step, count) if self.low <= i - count + step < self.high]
        if pairs:
            part = self.block(self.place - count + step)
            part = (part if self.down is None else part + self.down.astype(f32)).astype(bf16)
            sent.append(part)
            self.down = lax.ppermute(part, "tensor", pairs)
        return tuple(sent)

    def finish(self):
        while self.step < self.count - 1:
            self.go()
        return self.block(self.place) + self.up.astype(f32) + self.down.astype(f32)


class WeightGrad:
    def __init__(self, lows, other, kept, orders, own_channels):
        self.kept, self.orders, self.own = kept, orders, own_channels
        middle = lows.shape[1] // 2
        self.leave = matmul(lows[:, middle:], other, (0, 0), bf16)
        self.got = swap(self.leave, 1)
        self.lows, self.other = lows[:, :middle], other

    def rest(self, *waits):
        self.stay = matmul(after(self.lows, self.leave, *waits), self.other, (0, 0), bf16)
        return self.stay

    def split(self):
        columns = self.stay.shape[1] // len(self.orders)
        self.streams = []
        for part, order in enumerate(self.orders):
            blocks = {}
            for i, k in enumerate(self.kept):
                cut = (slice(i * self.own, (i + 1) * self.own), slice(part * columns, (part + 1) * columns))
                blocks[k] = self.stay[cut].astype(f32) + self.got[cut].astype(f32)
            self.streams.append((blocks, order))
        return self.go()

    def go(self):
        sents, streams = [], []
        for blocks, order in self.streams:
            sent, back, bit = halves(blocks, order, 0)
            sents.append(sent)
            streams.append((back, swap(sent, bit)))
        self.waiting = streams
        self.streams = streams
        return tuple(sents)

    def take(self, *waits):
        self.streams = [back(after(got, *waits)) for back, got in self.waiting]

    def finish(self):
        if not isinstance(self.streams[0][0], dict):
            self.take()
        while self.streams[0][1]:
            self.go()
            self.take()
        return jnp.concatenate([blocks[0] for blocks, _ in self.streams], axis=1)


def ring_sum(part):
    count = lax.axis_size("tensor")
    total = part.astype(f32)
    for step in range(1, count):
        total = total + lax.ppermute(part, "tensor", [(i, (i + step) % count) for i in range(count)]).astype(f32)
    return total


def pair_sum(part):
    count = lax.axis_size("tensor")
    total, sents = part.astype(f32), []
    bit = 1
    while bit < count:
        sents.append(total.astype(bf16))
        total = total + lax.ppermute(sents[-1], "tensor", [(i, i ^ bit) for i in range(count)]).astype(f32)
        bit *= 2
    return total, sents


def placed(places):
    count = len(places)
    own = lax.axis_index("fsdp")
    owners = jnp.bitwise_xor(jnp.asarray(places, jnp.int32), own.astype(jnp.int32))
    return lax.broadcasted_iota(jnp.int32, (count, count), 0) == owners[None, :]


def matmul(left, right, dims, kind=f32):
    return lax.dot_general(left, right, ((dims[:1], dims[1:]), ((), ())), preferred_element_type=f32).astype(kind)


def shards(
    hidden,
    cotangent,
    seq_lengths,
    pack_order,
    norm_gain,
    w_in,
    conv_weight,
    conv_bias,
    w_xproj,
    w_dt,
    dt_bias,
    a_log,
    d_skip,
    w_out,
):
    n_fsdp = lax.axis_size("fsdp")
    n_tensor = lax.axis_size("tensor")
    place = lax.axis_index("tensor")
    own_channels = w_in.shape[1]
    width = hidden.shape[1]
    group_rows = hidden.shape[0] * n_tensor
    rank = w_dt.shape[1]
    states = a_log.shape[1]
    taps = conv_weight.shape[1]
    wide = [1 << i for i in range(1, n_fsdp.bit_length() - 1)]
    narrow = wide[::-1]
    kept = [k for k in range(n_fsdp) if not k & 1]
    places = kept + [k + 1 for k in kept]
    channels = own_channels * n_fsdp
    middle = channels // 2
    part_rows = group_rows // 2

    rows_all = lax.all_gather(hidden, "tensor", axis=0, tiled=True)
    gain_own = norm_gain.reshape(1, -1)
    lines = lax.broadcasted_iota(jnp.int32, (n_tensor, 1), 0)
    gain_line = jnp.where(lines == place, gain_own, 0)
    for step in range(1, n_tensor):
        got = lax.ppermute(gain_own, "tensor", [(i, (i + step) % n_tensor) for i in range(n_tensor)])
        gain_line = jnp.where(lines == lax.rem(place - step + n_tensor, n_tensor), got, gain_line)
    gain_rows = width // n_fsdp // own_channels
    small = jnp.concatenate(
        [
            w_xproj.T,
            w_dt.T,
            a_log.T,
            conv_weight.T,
            conv_bias[None],
            dt_bias[None],
            d_skip[None],
            gain_line.reshape(gain_rows, own_channels),
        ],
        axis=0,
    )
    small_got = [swap(small, k) for k in kept[1:]]
    w_xa = gather_wide(w_in[0], wide, *small_got)
    w_ga = gather_wide(w_in[1], narrow, *small_got)
    w_xb = swap(w_xa, 1)
    w_gb = swap(w_ga, 1)
    small_a = jnp.concatenate([small] + small_got, axis=1)
    small_all = jnp.concatenate([small_a, swap(small_a, 1)], axis=1)
    w_out_all = lax.all_gather(after(w_out, small), "fsdp", axis=0, tiled=True)
    cot_all = lax.all_gather(after(cotangent, w_xa, w_ga), "tensor", axis=0, tiled=True)
    own = lax.axis_index("fsdp").astype(jnp.int32)

    xw = rank + 2 * states
    w_xp = small_all[:xw]
    w_dt_rows = small_all[xw : xw + rank]
    at = xw + rank
    a_rows = small_all[at : at + states].astype(f32)
    at = at + states
    conv_rows = small_all[at : at + taps].astype(f32)
    at = at + taps
    conv_b = small_all[at : at + 1].astype(f32)
    dt_b = small_all[at + 1 : at + 2].astype(f32)
    skip_row = small_all[at + 2 : at + 3].astype(f32)
    gain_all = small_all[at + 3 :].astype(f32).reshape(1, gain_rows, n_fsdp, own_channels)
    owners = placed(places)
    gain = jnp.sum(jnp.where(owners[:, None, :, None], gain_all, 0.0), axis=2).reshape(1, width)
    decays = -jnp.exp(a_rows)
    rates = (decays * math.log2(math.e)).reshape(-1, LANES)

    offsets = distances(seq_lengths[0], pack_order[0], group_rows)
    keep = (offsets > 0).astype(jnp.int32)
    dist = offsets[:, None]
    normed = norm_rows(rows_all, gain, n_tensor)

    cuts = [slice(0, part_rows), slice(part_rows, group_rows)]
    halo = jnp.zeros((SUB, channels), f32)
    weights = ((w_xa, w_xb), (w_ga, w_gb))
    front_0 = front(0, part_rows, normed, *weights, conv_rows, conv_b, w_xp, dist, halo)
    halo_1 = front_0[0][part_rows - SUB :]
    front_1 = front(1, part_rows, normed, *weights, conv_rows, conv_b, w_xp, dist, halo_1)
    mixed_0 = ring_sum(front_0[3])
    mixed_1 = ring_sum(after(front_1[3], mixed_0))
    fronts, mixes, halos = [front_0, front_1], [mixed_0, mixed_1], [halo, halo_1]
    steps = [mixed[:, :rank].astype(bf16) for mixed in mixes]
    bcs = [mixed[:, rank:] for mixed in mixes]
    carried = jnp.zeros(rates.shape, f32)
    runs = []
    for h in (0, 1):
        bc = after(bcs[h], w_out_all) if h == 0 else bcs[h]
        made = scan_forward(
            keep[cuts[h]], steps[h], bc, w_dt_rows, dt_b, skip_row, rates, fronts[h][2], fronts[h][1], carried
        )
        carried = made[4]
        runs.append(made)
    gated = jnp.concatenate([runs[0][3], runs[1][3]], axis=0)
    step_all = jnp.concatenate(steps, axis=0)
    w_o = [lax.dynamic_slice_in_dim(w_out_all, (own ^ k) * own_channels, own_channels, 0) for k in places]
    w_o = jnp.concatenate(w_o, axis=0)
    grad_gated = matmul(after(cot_all, gated), w_o, (1, 1), bf16)
    gated_late = after(gated, grad_gated)
    branch = matmul(gated_late, w_o, (1, 0), bf16)
    branch_own = lax.psum_scatter(branch, "tensor", scatter_dimension=0, tiled=True)
    output = (hidden.astype(f32) + branch_own.astype(f32)).astype(bf16)
    orders = (wide, narrow)
    out_grad = WeightGrad(after(gated_late, branch), cot_all, kept, orders, own_channels)
    out_grad.rest()

    def backward(h, carried, *waits):
        return scan_backward(
            h, keep[cuts[h]], after(bcs[h], *waits), w_dt_rows, skip_row, rates, fronts[h][2], fronts[h][1],
            grad_gated, runs[h][2], runs[h][0], runs[h][1], carried,
        )

    back_1 = backward(1, jnp.zeros(rates.shape, f32), out_grad.stay)
    back_0 = backward(0, back_1[6])
    low_1 = ring_sum(back_1[3]).astype(bf16)
    low_0, low_sents = pair_sum(after(back_0[3], low_1))
    low_0 = low_0.astype(bf16)
    g_gate = jnp.concatenate([back_0[1], back_1[1]], axis=0)
    sent = out_grad.split()
    gate_grad = WeightGrad(after(g_gate, low_1, *sent), normed, kept, orders, own_channels)
    gate_grad.rest()
    late = jnp.zeros((SUB, channels), f32)
    dist_late = jnp.zeros((SUB, 1), jnp.int32)
    sig_1, late, sums_1 = turn(
        1, after(low_1, gate_grad.stay, *low_sents), back_1[0], fronts[1][0], halos[1], conv_rows, conv_b, w_xp,
        dist, late, dist_late,
    )
    out_grad.take(sig_1)
    sent = out_grad.go() + gate_grad.split()
    part_1, gain_1 = rear(1, after(sig_1, *sent), back_1[1], *weights, normed)
    line_1 = LineSum(part_1, n_tensor // 2, n_tensor)
    sent = line_1.go()
    sig_0, _, sums_0 = turn(
        0, after(low_0, *sent), back_0[0], fronts[0][0], halos[0], conv_rows, conv_b, w_xp, dist, late,
        dist[cuts[1]][:SUB],
    )
    out_grad.take()
    grad_w_out = out_grad.finish()
    gate_grad.take()
    sent = gate_grad.go()
    part_0, gain_0 = rear(0, after(sig_0, *sent), back_0[1], *weights, normed)
    line_0 = LineSum(part_0, 0, n_tensor // 2)
    sent = line_1.go(part_0) + line_0.go()
    g_signal = jnp.concatenate([sig_0, sig_1], axis=0)
    sig_grad = WeightGrad(after(g_signal, *sent), normed, kept, orders, own_channels)
    sig_grad.rest()
    gate_grad.take(sig_grad.stay)
    grad_w_gate = gate_grad.finish()
    sent = sig_grad.split()
    sent = line_1.go(*sent) + line_0.go(*sent)
    sig_grad.take(*sent)
    sent = sig_grad.go()
    line_0.go(*sent)
    sig_grad.take()
    grad_w_sig = sig_grad.finish()

    reds = back_0[4] + back_1[4]
    acc = back_0[5] + back_1[5]
    gain_sum = ((gain_0 + gain_1) / gain).reshape(n_fsdp, gain_rows, 1, own_channels)
    gain_sum = jnp.sum(jnp.where(owners[:, None, :, None], gain_sum, 0.0), axis=0).reshape(gain_rows, channels)
    gain_pad = -gain_rows % SUB
    small_grad = jnp.concatenate(
        [
            matmul(jnp.concatenate([low_0, low_1], axis=0), jnp.concatenate([fronts[0][2], fronts[1][2]], axis=0), (0, 0)),
            matmul(step_all, jnp.concatenate([back_0[2], back_1[2]], axis=0), (0, 0)),
            acc.reshape(states, channels) * decays,
            sums_0 + sums_1,
            reds,
            jnp.concatenate([gain_sum, jnp.zeros((gain_pad, channels), f32)], axis=0),
        ],
        axis=0,
    )
    small_half = small_grad[:, :middle] + swap(small_grad[:, middle:].astype(bf16), 1).astype(f32)
    small_own = small_half[:, :own_channels]
    for i, k in enumerate(kept[1:]):
        cut = small_half[:, (i + 1) * own_channels : (i + 2) * own_channels]
        small_own = small_own + swap(cut.astype(bf16), k).astype(f32)
    at = xw + rank + states
    gain_own = small_own[at + 2 * SUB : at + 2 * SUB + gain_rows].reshape(n_tensor, -1)
    grad_gain = lax.dynamic_slice_in_dim(gain_own, place, 1, 0)
    gain_low = gain_own.astype(bf16)
    for step in range(1, n_tensor):
        sent = lax.dynamic_slice_in_dim(gain_low, lax.rem(place + step, n_tensor), 1, 0)
        got = lax.ppermute(sent, "tensor", [(i, (i + step) % n_tensor) for i in range(n_tensor)])
        grad_gain = grad_gain + got.astype(f32)
    g_norm_own = jnp.where(place >= n_tensor // 2, line_1.finish(), line_0.finish())
    values = hidden.astype(f32)
    factor = lax.rsqrt(jnp.mean(values * values, axis=1, keepdims=True) + EPSILON)
    scaled = g_norm_own * gain
    xhat = values * factor
    grad_hidden = cotangent.astype(f32) + factor * (scaled - xhat * jnp.mean(scaled * xhat, axis=1, keepdims=True))
    columns = small_own.T
    return (
        output,
        grad_hidden,
        grad_gain.reshape(norm_gain.shape),
        jnp.stack([grad_w_sig, grad_w_gate], axis=0),
        columns[:, at : at + taps],
        small_own[at + taps],
        columns[:, :xw],
        columns[:, xw : xw + rank],
        small_own[at + SUB + 1],
        columns[:, at - states : at],
        small_own[at + SUB],
        grad_w_out,
    )


def solution(mesh):
    every = ("fsdp", "tensor")
    rows = P(every, None)
    line = P(every)
    planes = P(None, every, None)
    return jax.shard_map(
        shards,
        mesh=mesh,
        in_specs=(rows, rows, P("fsdp", None), P("fsdp", None), line, planes, rows, line, rows, rows, line, rows, line, rows),
        out_specs=(rows, rows, line, planes, rows, line, rows, rows, line, rows, line, rows),
        check_vma=False,
    )
```

```python
import functools
import math

import jax
import jax.numpy as jnp
from jax import lax
from jax.experimental import pallas as pl
from jax.experimental.pallas import tpu as pltpu
from jax.sharding import PartitionSpec as P

EPSILON = 1e-05
f32 = jnp.float32
bf16 = jnp.bfloat16
BIG = 1e30
LANES = 128
SUB = 8


def cost(micros):
    return pl.CostEstimate(flops=int(micros * 1e9), transcendentals=0, bytes_accessed=int(micros * 1e6))


def tile_rows(ti, j, subs):
    return pl.ds((ti * subs + j) * SUB, SUB)


def put_tiles(ref, value, subs):
    for ti in range(value.shape[0] // SUB):
        for j in range(subs):
            ref[tile_rows(ti, j, subs), :] = value[ti * SUB : (ti + 1) * SUB, j * LANES : (j + 1) * LANES]


def get_tiles(ref, rows, subs):
    lines = []
    for ti in range(rows // SUB):
        lines.append(jnp.concatenate([ref[tile_rows(ti, j, subs), :] for j in range(subs)], axis=1))
    return jnp.concatenate(lines, axis=0)


def put_spread(ref, value, count):
    for ti in range(value.shape[0] // SUB):
        for n in range(count):
            ref[pl.ds((ti * count + n) * SUB, SUB), :] = jnp.broadcast_to(
                value[ti * SUB : (ti + 1) * SUB, n : n + 1], (SUB, LANES)
            )


def fwd_body(
    states, subs, first_row, count, keep_ref, *refs
):
    part_refs, refs = refs[:count], refs[count:]
    wdt_ref, db_ref, ds_ref, dec_ref, inner_ref, gate_ref, h0_ref = refs[:7]
    hs_ref, dl_ref, ys_ref, gated_ref, mixed_ref, h_ref, du_sc, bb_sc, y_sc = refs[-9:]
    chunk = pl.program_id(0)
    rows = inner_ref.shape[0]
    span = states * subs
    rank = wdt_ref.shape[0]

    @pl.when(chunk == 0)
    def _():
        h_ref[...] = h0_ref[...]

    mixed = part_refs[0][...].astype(f32)
    for part_ref in part_refs[1:]:
        mixed = mixed + part_ref[...].astype(f32)
    mixed_ref[...] = mixed
    step_in = mixed[:, :rank].astype(bf16)
    raw = jnp.dot(step_in, wdt_ref[...], preferred_element_type=f32) + db_ref[...]
    delta = jnp.maximum(raw, 0.0) + jnp.log1p(jnp.exp(-jnp.abs(raw)))
    inner = inner_ref[...].astype(f32)
    put_tiles(dl_ref, delta, subs)
    put_tiles(du_sc, delta * inner, subs)
    put_spread(bb_sc, mixed[:, rank:], 2 * states)
    hs_ref[pl.ds(0, span), :] = h_ref[...]
    decs = [dec_ref[pl.ds(n * subs, subs), :] for n in range(states)]

    def step(ti, hs):
        hs = list(hs)
        for s in range(SUB):
            t = ti * SUB + s
            row = ti * (subs * SUB) + s
            d = dl_ref[pl.ds(row, subs, stride=SUB), :]
            u = du_sc[pl.ds(row, subs, stride=SUB), :]
            d = jnp.where(keep_ref[first_row + chunk * rows + t] > 0, d, BIG)
            y = None
            for n in range(states):
                b = bb_sc[pl.ds((ti * 2 * states + n) * SUB + s, subs, stride=0), :]
                c = bb_sc[pl.ds((ti * 2 * states + states + n) * SUB + s, subs, stride=0), :]
                hs[n] = jnp.exp2(d * decs[n]) * hs[n] + u * b
                hs_ref[pl.ds(pl.multiple_of((t + 1) * span + n * subs, subs), subs), :] = hs[n]
                y = c * hs[n] if y is None else y + c * hs[n]
            y_sc[pl.ds(row, subs, stride=SUB), :] = y
        return tuple(hs)

    start = tuple(h_ref[pl.ds(n * subs, subs), :] for n in range(states))
    hs = lax.fori_loop(0, rows // SUB, step, start)
    for n in range(states):
        h_ref[pl.ds(n * subs, subs), :] = hs[n]
    total = get_tiles(y_sc, rows, subs) + ds_ref[...] * inner
    ys_ref[...] = total
    gate = gate_ref[...]
    gated_ref[...] = (total * gate / (1.0 + jnp.exp(-gate))).astype(bf16)


def scan_forward(h, keep, parts, wdt, dt_bias, d_skip, dec, inner, gate, h0, into=None, chunk_rows=64):
    rows, channels = gate.shape
    subs = channels // LANES
    rank = wdt.shape[0]
    mix = parts[0].shape[1]
    states = (mix - rank) // 2
    chunks = rows // chunk_rows
    span = states * subs

    def row_block(width, start=0):
        return pl.BlockSpec((chunk_rows, width), lambda i, *_: (start + i, 0))

    def whole(a):
        return pl.BlockSpec(a.shape, lambda i, *_: (0, 0))

    extra = [] if into is None else [into]
    grid_spec = pltpu.PrefetchScalarGridSpec(
        num_scalar_prefetch=1,
        grid=(chunks,),
        in_specs=[row_block(mix) for _ in parts]
        + [whole(wdt), whole(dt_bias), whole(d_skip), whole(dec), row_block(channels, h * chunks), row_block(channels), whole(h0)]
        + [pl.BlockSpec(memory_space=pl.ANY) for _ in extra],
        out_specs=[
            pl.BlockSpec(((chunk_rows + 1) * span, LANES), lambda i, *_: (i, 0)),
            pl.BlockSpec((chunk_rows * subs, LANES), lambda i, *_: (i, 0)),
            row_block(channels), row_block(channels, h * chunks), row_block(mix), whole(h0),
        ],
        scratch_shapes=[
            pltpu.VMEM((chunk_rows * subs, LANES), f32),
            pltpu.VMEM((chunk_rows * 2 * states, LANES), f32),
            pltpu.VMEM((chunk_rows * subs, LANES), f32),
        ],
    )
    made = jax.ShapeDtypeStruct
    return pl.pallas_call(
        functools.partial(fwd_body, states, subs, h * rows, len(parts)),
        grid_spec=grid_spec,
        out_shape=[
            made((chunks * (chunk_rows + 1) * span, LANES), f32), made((rows * subs, LANES), f32),
            made((rows, channels), f32), made(inner.shape, bf16), made((rows, mix), f32), made((span, LANES), f32),
        ],
        input_output_aliases={} if into is None else {len(parts) + 8: 3},
        compiler_params=pltpu.CompilerParams(vmem_limit_bytes=58 << 20),
        cost_estimate=cost(0.02),
        name="scan_forward",
    )(keep, *parts, wdt, dt_bias, d_skip, dec, inner, gate, h0, *extra)


def fold_rows(parts, sub_iota):
    if parts[0].shape[0] != SUB:
        return jnp.concatenate([jnp.sum(p, axis=0, keepdims=True) for p in parts], axis=0)
    upper = sub_iota < 4
    xs = [
        jnp.where(upper, parts[n], parts[n + 4]) + pltpu.roll(jnp.where(upper, parts[n + 4], parts[n]), 4, 0)
        for n in range(4)
    ]
    pair = (sub_iota & 3) < 2
    ys = [
        jnp.where(pair, xs[n] + pltpu.roll(xs[n], 6, 0), xs[n + 2] + pltpu.roll(xs[n + 2], 2, 0))
        for n in range(2)
    ]
    even = (sub_iota & 1) == 0
    return jnp.where(even, ys[0] + pltpu.roll(ys[0], 7, 0), ys[1] + pltpu.roll(ys[1], 1, 0))


def bwd_body(
    states, subs, first_row, keep_ref, fwd_ref, wdt_ref, dst_ref, dec_ref, inner_ref, gate_ref, gg_ref, ys_ref, hs_ref,
    dl_ref, gh0_ref, *refs
):
    gi_ref, gx_ref, gp_ref, mixed_ref, red_ref, acc_ref, gh_ref, in_sc, gy_sc, bb_sc, gd_sc, go_sc, r_sc = refs[-13:]
    i = pl.program_id(0)
    last = pl.num_programs(0) - 1
    chunk = last - i
    rows = inner_ref.shape[0]
    all_rows = r_sc.shape[0] // (2 * states)
    span = states * subs
    rank = wdt_ref.shape[0]

    @pl.when(i == 0)
    def _():
        gh_ref[...] = gh0_ref[...]
        acc_ref[...] = jnp.zeros_like(acc_ref)
        red_ref[...] = jnp.zeros_like(red_ref)

    gate = gate_ref[...]
    sig = 1.0 / (1.0 + jnp.exp(-gate))
    gg = gg_ref[...].astype(f32)
    gy_all = gg * (gate * sig)
    gx_ref[...] = (gg * ys_ref[...] * (sig * (1.0 + gate * (1.0 - sig)))).astype(bf16)
    inner_all = inner_ref[...].astype(f32)
    red_ref[pl.ds(0, 1), :] += jnp.sum(gy_all * inner_all, axis=0, keepdims=True)
    put_tiles(gy_sc, gy_all, subs)
    put_tiles(in_sc, inner_all, subs)
    put_spread(bb_sc, fwd_ref[...][:, rank:], 2 * states)
    sub_iota = lax.broadcasted_iota(jnp.int32, (SUB, LANES), 0)
    skip = dst_ref[...]
    order = (0, 4, 2, 6, 1, 5, 3, 7)

    def step(k, carried):
        ghs = list(carried[:states])
        accs = list(carried[states:])
        ti = rows // SUB - 1 - k
        for s in reversed(range(SUB)):
            t = ti * SUB + s
            row = ti * (subs * SUB) + s
            d = dl_ref[pl.ds(row, subs, stride=SUB), :]
            v = in_sc[pl.ds(row, subs, stride=SUB), :]
            gy = gy_sc[pl.ds(row, subs, stride=SUB), :]
            u = d * v
            da = jnp.where(keep_ref[first_row + chunk * rows + t] > 0, d, BIG)
            gd = gs = None
            for g in range(states // SUB):
                pb = [None] * SUB
                pc = [None] * SUB
                for o in order:
                    n = g * SUB + o
                    b = bb_sc[pl.ds((ti * 2 * states + n) * SUB + s, subs, stride=0), :]
                    c = bb_sc[pl.ds((ti * 2 * states + states + n) * SUB + s, subs, stride=0), :]
                    dec = dec_ref[pl.ds(n * subs, subs), :]
                    before = hs_ref[pl.ds(pl.multiple_of(t * span + n * subs, subs), subs), :]
                    after = hs_ref[pl.ds(pl.multiple_of((t + 1) * span + n * subs, subs), subs), :]
                    gh = c * gy + ghs[n]
                    ghs[n] = jnp.exp2(da * dec) * gh
                    q = ghs[n] * before
                    gd = dec * q if gd is None else gd + dec * q
                    accs[n] = accs[n] + q * d
                    gs = gh * b if gs is None else gs + gh * b
                    pb[o] = gh * u
                    pc[o] = after * gy
                at = chunk * rows + t
                r_sc[pl.ds(g * SUB * all_rows + at, SUB, stride=all_rows), :] = fold_rows(pb, sub_iota)
                r_sc[pl.ds((states + g * SUB) * all_rows + at, SUB, stride=all_rows), :] = fold_rows(pc, sub_iota)
            gd_sc[pl.ds(row, subs, stride=SUB), :] = gd * math.log(2.0) + gs * v
            go_sc[pl.ds(row, subs, stride=SUB), :] = gy * skip + gs * d
        return tuple(ghs + accs)

    init = tuple(gh_ref[pl.ds(n * subs, subs), :] for n in range(states))
    init = init + tuple(acc_ref[pl.ds(n * subs, subs), :] for n in range(states))
    out = lax.fori_loop(0, rows // SUB, step, init)
    for n in range(states):
        gh_ref[pl.ds(n * subs, subs), :] = out[n]
        acc_ref[pl.ds(n * subs, subs), :] = out[states + n]
    gi_ref[...] = get_tiles(go_sc, rows, subs)
    d_all = get_tiles(dl_ref, rows, subs)
    series = d_all * (1.0 - d_all * (0.5 - d_all * (1.0 / 6 - d_all * (1.0 / 24))))
    slope = jnp.where(d_all < 0.03125, series, 1.0 - jnp.exp(-d_all))
    gp = get_tiles(gd_sc, rows, subs) * slope
    red_ref[pl.ds(1, 1), :] += jnp.sum(gp, axis=0, keepdims=True)
    low = gp.astype(bf16)
    gp_ref[...] = low
    mixed_ref[pl.ds(pl.multiple_of(chunk * rows, rows), rows), pl.ds(0, rank)] = lax.dot_general(
        low, wdt_ref[...], (((1,), (1,)), ((), ())), preferred_element_type=f32
    ).astype(bf16)

    @pl.when(i == last)
    def _():
        lane = lax.broadcasted_iota(jnp.int32, (LANES, LANES), 1)
        total = jnp.zeros((all_rows, LANES), f32)
        for n in range(2 * states):
            pick = jnp.where(lane == n, 1.0, 0.0).astype(bf16)
            part = r_sc[pl.ds(n * all_rows, all_rows), :].astype(bf16)
            total = total + jnp.dot(part, pick, preferred_element_type=f32)
        mixed_ref[:, pl.ds(rank, 2 * states)] = total[:, : 2 * states].astype(bf16)


def scan_backward(h, keep, mixed, wdt, d_skip, dec, inner, gate, gg, ysum, hs, delta_tm, gh0, into=(), chunk_rows=64):
    rows, channels = gate.shape
    subs = channels // LANES
    rank = wdt.shape[0]
    mix = mixed.shape[1]
    states = (mix - rank) // 2
    chunks = rows // chunk_rows
    span = states * subs
    skip_tm = d_skip.reshape(subs, LANES)

    def row_block(width, start=0):
        return pl.BlockSpec((chunk_rows, width), lambda i, *_: (start + chunks - 1 - i, 0))

    def fixed(shape):
        return pl.BlockSpec(shape, lambda i, *_: (0, 0))

    tile = pltpu.VMEM((chunk_rows * subs, LANES), f32)
    first = h * chunks
    grid_spec = pltpu.PrefetchScalarGridSpec(
        num_scalar_prefetch=1,
        grid=(chunks,),
        in_specs=[
            row_block(mix), fixed(wdt.shape), fixed(skip_tm.shape), fixed(dec.shape),
            row_block(channels, first), row_block(channels), row_block(channels, first), row_block(channels),
            pl.BlockSpec(((chunk_rows + 1) * span, LANES), lambda i, *_: (chunks - 1 - i, 0)),
            pl.BlockSpec((chunk_rows * subs, LANES), lambda i, *_: (chunks - 1 - i, 0)), fixed(gh0.shape),
        ]
        + [pl.BlockSpec(memory_space=pl.ANY) for _ in into],
        out_specs=[
            row_block(channels), row_block(channels, first), row_block(channels, first), fixed((rows, mix)),
            fixed((8, channels)), fixed((span, LANES)), fixed((span, LANES)),
        ],
        scratch_shapes=[
            tile, tile, pltpu.VMEM((chunk_rows * 2 * states, LANES), f32), tile, tile,
            pltpu.VMEM((2 * states * rows, LANES), f32),
        ],
    )
    made = jax.ShapeDtypeStruct
    return pl.pallas_call(
        functools.partial(bwd_body, states, subs, h * rows),
        grid_spec=grid_spec,
        out_shape=[
            made((rows, channels), f32), made(inner.shape, bf16), made(inner.shape, bf16),
            made((rows, mix), bf16), made((8, channels), f32), made((span, LANES), f32),
            made((span, LANES), f32),
        ],
        input_output_aliases={12 + i: 1 + i for i in range(len(into))},
        compiler_params=pltpu.CompilerParams(vmem_limit_bytes=58 << 20),
        cost_estimate=cost(0.02),
        name="scan_backward",
    )(keep, mixed, wdt, skip_tm, dec, inner, gate, gg, ysum, hs, delta_tm, gh0, *into)


def norm_body(gain_ref, rows_ref, out_ref):
    value = rows_ref[...].astype(f32)
    factor = lax.rsqrt(jnp.mean(value * value, axis=1, keepdims=True) + EPSILON)
    out_ref[...] = (value * factor * gain_ref[...]).astype(bf16)


def norm_rows(rows_all, gain, parts):
    rows, width = rows_all.shape
    block = pl.BlockSpec((rows // parts, width), lambda i: (i, 0))
    return pl.pallas_call(
        norm_body,
        grid=(parts,),
        in_specs=[pl.BlockSpec(gain.shape, lambda i: (0, 0)), block],
        out_specs=block,
        out_shape=jax.ShapeDtypeStruct((rows, width), bf16),
        compiler_params=pltpu.CompilerParams(vmem_limit_bytes=24 << 20),
        cost_estimate=cost(0.02),
        name="norm_rows",
    )(gain, rows_all)


def weave(one, two, own):
    pieces = []
    for at in range(0, one.shape[0], own):
        pieces += [one[at : at + own], two[at : at + own]]
    return jnp.concatenate(pieces, axis=0)


def weight_specs(chunk, width):
    whole = pl.BlockSpec((chunk, width), lambda i: (0, 0))
    first = pl.BlockSpec((chunk // 2, width), lambda i: (jnp.minimum(i, 1), 0))
    second = pl.BlockSpec((chunk // 2, width), lambda i: (jnp.maximum(i - 2, 0), 0))
    return [whole] * 4 + [first, first, second, second]


def front_body(
    own, normed_ref, *refs
):
    x_refs, g_refs, refs = refs[:4], refs[4:8], refs[8:]
    taps_ref, bias_ref, wxp_ref, dist_ref = refs[:4]
    refs = refs[4:]
    sig_ref, gate_ref, inner_ref, mixed_ref, ext_sc, acc_sc = refs[-6:]
    i = pl.program_id(0)
    rows = normed_ref.shape[0]
    dims = (((1,), (1,)), ((), ()))

    def project(x_ref, one_ref, two_ref):
        normed = normed_ref[...]
        ext_sc[pl.ds(SUB, rows), :] = lax.dot_general(normed, x_ref[...], dims, preferred_element_type=f32)
        gate = weave(one_ref[...], two_ref[...], own)
        gate_ref[...] = lax.dot_general(normed, gate, dims, preferred_element_type=f32)

    for block in range(4):

        @pl.when(i == block)
        def _(block=block):
            project(x_refs[block], *g_refs[block // 2 * 2 : block // 2 * 2 + 2])

    ext_sc[pl.ds(0, SUB), :] = jnp.zeros((SUB, ext_sc.shape[1]), f32)
    taps = taps_ref.shape[0]
    signal = ext_sc[pl.ds(SUB, rows), :]
    sig_ref[...] = signal
    dist = dist_ref[...]
    pre = bias_ref[...] + taps_ref[pl.ds(taps - 1, 1), :] * signal
    for lag in range(1, taps):
        shifted = ext_sc[pl.ds(SUB - lag, rows), :]
        pre = pre + jnp.where(dist >= lag, taps_ref[pl.ds(taps - 1 - lag, 1), :] * shifted, 0.0)
    inner = (pre / (1.0 + jnp.exp(-pre))).astype(bf16)
    inner_ref[...] = inner
    part = lax.dot_general(inner, wxp_ref[...], dims, preferred_element_type=f32)

    @pl.when(i == 0)
    def _():
        acc_sc[...] = part

    @pl.when(i > 0)
    def _():
        acc_sc[...] += part

    mixed_ref[...] = acc_sc[...].astype(bf16)


def front(normed, weights, taps, bias, w_xp, dist, own):
    rows, width = normed.shape
    channels = taps.shape[1]
    chunk = channels // 4
    xw = w_xp.shape[0]

    def columns(height):
        return pl.BlockSpec((height, chunk), lambda i: (0, i))

    made = jax.ShapeDtypeStruct
    return pl.pallas_call(
        functools.partial(front_body, own),
        grid=(4,),
        in_specs=[pl.BlockSpec((rows, width), lambda i: (0, 0))]
        + weight_specs(chunk, width)
        + [columns(taps.shape[0]), columns(1), columns(xw), pl.BlockSpec((rows, 1), lambda i: (0, 0))],
        out_specs=[columns(rows), columns(rows), columns(rows), pl.BlockSpec((rows, xw), lambda i: (0, 0))],
        out_shape=[
            made((rows, channels), f32), made((rows, channels), f32), made((rows, channels), bf16),
            made((rows, xw), bf16),
        ],
        scratch_shapes=[pltpu.VMEM((rows + SUB, chunk), f32), pltpu.VMEM((rows, xw), f32)],
        compiler_params=pltpu.CompilerParams(vmem_limit_bytes=44 << 20),
        cost_estimate=cost(0.02),
        name="front",
    )(normed, *weights, taps, bias, w_xp, dist)


def turn_body(count, begins, ends, *refs):
    part_refs, refs = refs[:count], refs[count:]
    gis_ref, sig_ref, taps_ref, bias_ref, wxp_ref, dist_ref = refs[:6]
    more = list(refs[6:-6])
    gsig_ref, low_ref, head_ref, sums_ref, ext_sc, late_sc = refs[-6:]
    rows, chunk = gis_ref.shape
    taps = taps_ref.shape[0]
    nothing = jnp.zeros((SUB, chunk), f32)
    ext_sc[pl.ds(0, SUB), :] = nothing if begins else more.pop(0)[...]
    ext_sc[pl.ds(SUB, rows), :] = sig_ref[...]
    dist = dist_ref[...]
    signal = sig_ref[...]
    pre = bias_ref[...] + taps_ref[pl.ds(taps - 1, 1), :] * signal
    for lag in range(1, taps):
        shifted = ext_sc[pl.ds(SUB - lag, rows), :]
        pre = pre + jnp.where(dist >= lag, taps_ref[pl.ds(taps - 1 - lag, 1), :] * shifted, 0.0)
    sig = 1.0 / (1.0 + jnp.exp(-pre))
    mixed = part_refs[0][...].astype(f32)
    for part_ref in part_refs[1:]:
        mixed = mixed + part_ref[...].astype(f32)
    low = mixed.astype(bf16)
    low_ref[...] = low
    g_inner = gis_ref[...] + jnp.dot(low, wxp_ref[...], preferred_element_type=f32)
    g_pre = g_inner * (sig * (1.0 + pre * (1.0 - sig)))
    head_ref[...] = g_pre[:SUB, :]
    lines = [None] * taps
    lines[taps - 1] = jnp.sum(g_pre * signal, axis=0, keepdims=True)
    g_signal = taps_ref[pl.ds(taps - 1, 1), :] * g_pre
    if not ends:
        next_ref, dnext_ref = more.pop(0), more.pop(0)
    for lag in range(1, taps):
        masked = jnp.where(dist >= lag, g_pre, 0.0)
        lines[taps - 1 - lag] = jnp.sum(masked * ext_sc[pl.ds(SUB - lag, rows), :], axis=0, keepdims=True)
        late_sc[pl.ds(0, rows), :] = masked
        late_sc[pl.ds(rows, SUB), :] = nothing if ends else jnp.where(dnext_ref[...] >= lag, next_ref[...], 0.0)
        g_signal = g_signal + taps_ref[pl.ds(taps - 1 - lag, 1), :] * late_sc[pl.ds(lag, rows), :]
    lines.append(jnp.sum(g_pre, axis=0, keepdims=True))
    sums_ref[...] = jnp.zeros_like(sums_ref)
    for k, value in enumerate(lines):
        sums_ref[pl.ds(k, 1), :] = value
    gsig_ref[...] = g_signal.astype(bf16)


def turn(h, parts, gis, signal, taps, bias, w_xp, dist, before=None, later=None):
    rows, channels = gis.shape
    chunk = min(256, channels // 2)
    xw = w_xp.shape[0]

    def columns(height, start=0):
        return pl.BlockSpec((height, chunk), lambda i: (start, i))

    def fixed(a):
        return pl.BlockSpec(a.shape, lambda i: (0, 0))

    extra, extra_specs, alias = [], [], {}
    if before is not None:
        extra.append(before)
        extra_specs.append(columns(SUB, rows // SUB - 1))
    if later is not None:
        extra += [later[2], dist, later[0]]
        extra_specs += [
            columns(SUB), pl.BlockSpec((SUB, 1), lambda i: ((h + 1) * rows // SUB, 0)), pl.BlockSpec(memory_space=pl.ANY)
        ]
        alias = {len(parts) + 6 + len(extra) - 1: 0}
    made = jax.ShapeDtypeStruct
    return pl.pallas_call(
        functools.partial(turn_body, len(parts), before is None, later is None),
        grid=(channels // chunk,),
        in_specs=[fixed(part) for part in parts]
        + [
            columns(rows), columns(rows), columns(taps.shape[0]), columns(1), columns(xw),
            pl.BlockSpec((rows, 1), lambda i: (h, 0)),
        ]
        + extra_specs,
        out_specs=[columns(rows, h), pl.BlockSpec((rows, xw), lambda i: (0, 0)), columns(SUB), columns(SUB)],
        out_shape=[
            made((dist.shape[0], channels), bf16), made((rows, xw), bf16), made((SUB, channels), f32),
            made((SUB, channels), f32),
        ],
        scratch_shapes=[pltpu.VMEM((rows + SUB, chunk), f32), pltpu.VMEM((rows + SUB, chunk), f32)],
        input_output_aliases=alias,
        compiler_params=pltpu.CompilerParams(vmem_limit_bytes=32 << 20),
        cost_estimate=cost(0.02),
        name="turn",
    )(*parts, gis, signal, taps, bias, w_xp, dist, *extra)


def rear_body(own, gs_ref, gx_ref, *refs):
    x_refs, g_refs, (normed_ref, out_ref, gain_ref, acc_sc) = refs[:4], refs[4:8], refs[8:]
    i = pl.program_id(0)
    for block in range(4):

        @pl.when(i == block)
        def _(block=block):
            gate = weave(*[ref[...] for ref in g_refs[block // 2 * 2 : block // 2 * 2 + 2]], own)
            part = jnp.dot(gs_ref[...], x_refs[block][...], preferred_element_type=f32) + jnp.dot(
                gx_ref[...], gate, preferred_element_type=f32
            )
            if block == 0:
                acc_sc[...] = part
            elif block < 3:
                acc_sc[...] += part
            else:
                total = acc_sc[...] + part
                out_ref[...] = total.astype(bf16)
                gain_ref[...] = jnp.sum(total * normed_ref[...].astype(f32), axis=0, keepdims=True)


def rear(g_signal, g_gate, weights, normed, own):
    rows, width = normed.shape
    channels = g_signal.shape[1]
    chunk = channels // 4
    columns = pl.BlockSpec((rows, chunk), lambda i: (0, i))
    whole = pl.BlockSpec((rows, width), lambda i: (0, 0))
    made = jax.ShapeDtypeStruct
    return pl.pallas_call(
        functools.partial(rear_body, own),
        grid=(4,),
        in_specs=[columns, columns] + weight_specs(chunk, width) + [whole],
        out_specs=[whole, pl.BlockSpec((1, width), lambda i: (0, 0))],
        out_shape=[made((rows, width), bf16), made((1, width), f32)],
        scratch_shapes=[pltpu.VMEM((rows, width), f32)],
        compiler_params=pltpu.CompilerParams(vmem_limit_bytes=44 << 20),
        cost_estimate=cost(0.02),
        name="rear",
    )(g_signal, g_gate, *weights, normed)


def cross_body(left_ref, right_ref, gated_ref, *refs):
    quarters, (gg_ref, out_ref) = refs[:4], refs[4:]
    chunk = quarters[0].shape[0]
    half = left_ref.shape[1]
    dims = (((1,), (1,)), ((), ()))
    total = None
    for q in range(4):
        w = quarters[q][...]
        cut = pl.ds(q * chunk, chunk)
        part = lax.dot_general(left_ref[...], w[:, :half], dims, preferred_element_type=f32)
        part = part + lax.dot_general(right_ref[...], w[:, half:], dims, preferred_element_type=f32)
        gg_ref[:, cut] = part.astype(bf16)
        part = jnp.dot(gated_ref[:, cut], w, preferred_element_type=f32)
        total = part if total is None else total + part
    out_ref[...] = total.astype(bf16)


def cross(cots, gated, quarters, parts=2):
    tokens, half = cots[0].shape
    channels = gated.shape[1]
    rows = tokens // parts

    def row_block(columns):
        return pl.BlockSpec((rows, columns), lambda i: (i, 0))

    made = jax.ShapeDtypeStruct
    return pl.pallas_call(
        cross_body,
        grid=(parts,),
        in_specs=[row_block(half), row_block(half), row_block(channels)]
        + [pl.BlockSpec(quarter.shape, lambda i: (0, 0)) for quarter in quarters],
        out_specs=[row_block(channels), row_block(2 * half)],
        out_shape=[made((tokens, channels), bf16), made((tokens, 2 * half), bf16)],
        compiler_params=pltpu.CompilerParams(vmem_limit_bytes=40 << 20),
        cost_estimate=cost(0.02),
        name="cross",
    )(*cots, gated, *quarters)


def stage_body(plans, *refs):
    refs = list(refs)
    sums = []
    for _ in plans:
        base, got = refs.pop(0), refs.pop(0)
        sums.append([base[k].astype(f32) + got[k].astype(f32) for k in range(base.shape[0])])
    for (stay, leave), blocks in zip(plans, sums):
        kept = refs.pop(0)
        for i, k in enumerate(stay):
            kept[i] = blocks[k]
        if leave:
            sent = refs.pop(0)
            for i, k in enumerate(leave):
                sent[i] = blocks[k].astype(bf16)


def stage(streams, plans, steps=2):
    height = streams[0][0][0].shape[1] // steps
    ins, in_specs, outs, out_specs = [], [], [], []
    for (base, got), (stay, leave), column in streams_with(streams, plans):
        width = base.shape[2] if column is None else base.shape[2] // len(streams)
        for a in (base, got):
            ins.append(a)
            in_specs.append(
                pl.BlockSpec((a.shape[0], height, width), lambda i, column=column: (0, i, 0 if column is None else column))
            )
        for blocks, kind in ((stay, f32), (leave, bf16)):
            if blocks:
                outs.append(jax.ShapeDtypeStruct((len(blocks), height * steps, width), kind))
                out_specs.append(pl.BlockSpec((len(blocks), height, width), lambda i: (0, i, 0)))
    return pl.pallas_call(
        functools.partial(stage_body, plans),
        grid=(steps,),
        in_specs=in_specs,
        out_specs=out_specs,
        out_shape=outs,
        compiler_params=pltpu.CompilerParams(vmem_limit_bytes=40 << 20),
        cost_estimate=cost(0.02),
        name="stage",
    )(*ins)


def streams_with(streams, plans):
    for (pair, column), plan in zip(streams, plans):
        yield pair, plan, column


def join_body(*refs):
    out_ref = refs[-1]
    pairs = [(refs[2 * i], refs[2 * i + 1]) for i in range((len(refs) - 1) // 2)]
    width = pairs[0][0].shape[2]
    for i, (base, got) in enumerate(pairs):
        out_ref[0, :, pl.ds(i * width, width)] = base[0].astype(f32) + got[0].astype(f32)


def join(pairs, plane, planes, into=None, steps=2):
    _, rows, width = pairs[0][0].shape
    height = rows // steps
    ins = [a for pair in pairs for a in pair]
    extra = [] if into is None else [into]

    def body(*refs):
        join_body(*refs[: len(ins)], refs[-1])

    return pl.pallas_call(
        body,
        grid=(steps,),
        in_specs=[pl.BlockSpec((1, height, width), lambda i: (0, i, 0)) for _ in ins]
        + [pl.BlockSpec(memory_space=pl.ANY) for _ in extra],
        out_specs=pl.BlockSpec((1, height, width * len(pairs)), lambda i: (plane, i, 0)),
        out_shape=jax.ShapeDtypeStruct((planes, rows, width * len(pairs)), f32),
        input_output_aliases={} if into is None else {len(ins): 0},
        compiler_params=pltpu.CompilerParams(vmem_limit_bytes=24 << 20),
        cost_estimate=cost(0.02),
        name="join",
    )(*ins, *extra)


def grad_body(lows_ref, *refs):
    out_ref = refs[-1]
    at = 0
    for ref in refs[:-1]:
        part = lax.dot_general(lows_ref[...], ref[...], (((0,), (0,)), ((), ())), preferred_element_type=f32)
        out_ref[:, pl.ds(at, ref.shape[1])] = part.astype(bf16)
        at += ref.shape[1]


def grad_half(h, lows, others):
    tokens, channels = lows.shape
    width = sum(other.shape[1] for other in others)
    chunk = min(256, channels // 2)
    steps = channels // 2 // chunk
    return pl.pallas_call(
        grad_body,
        grid=(steps,),
        in_specs=[pl.BlockSpec((tokens, chunk), lambda i: (0, h * steps + i))]
        + [pl.BlockSpec(other.shape, lambda i: (0, 0)) for other in others],
        out_specs=pl.BlockSpec((chunk, width), lambda i: (i, 0)),
        out_shape=jax.ShapeDtypeStruct((channels // 2, width), bf16),
        compiler_params=pltpu.CompilerParams(vmem_limit_bytes=24 << 20),
        cost_estimate=cost(0.02),
        name="grad_half",
    )(lows, *others)


def pack_body(half, rank, states, low_ref, mix_ref, inner_ref, gp_ref, acc_ref, dec_ref, sum_ref, red_ref, gain_ref,
              stay_ref, leave_ref, all_sc):
    i = pl.program_id(0)
    dims = (((0,), (0,)), ((), ()))
    chunk, xw = inner_ref.shape[1], low_ref.shape[1]
    all_sc[pl.ds(0, xw), :] = lax.dot_general(low_ref[...], inner_ref[...], dims, preferred_element_type=f32)
    step_in = mix_ref[...][:, :rank].astype(bf16)
    all_sc[pl.ds(xw, rank), :] = lax.dot_general(step_in, gp_ref[...], dims, preferred_element_type=f32)
    subs = dec_ref.shape[0] // states
    wide = chunk // LANES
    for j in range(wide):
        cut = pl.ds(i * wide + j, states, stride=subs)
        all_sc[pl.ds(xw + rank, states), pl.ds(j * LANES, LANES)] = acc_ref[cut, :] * (dec_ref[cut, :] * math.log(2.0))
    at = xw + rank + states
    all_sc[pl.ds(at, SUB), :] = sum_ref[...]
    all_sc[pl.ds(at + SUB, SUB), :] = red_ref[...]
    all_sc[pl.ds(at + 2 * SUB, SUB), :] = gain_ref[...]

    @pl.when(i < half)
    def _():
        stay_ref[...] = all_sc[...].astype(bf16)

    @pl.when(i >= half)
    def _():
        leave_ref[...] = all_sc[...].astype(bf16)


def pack(rank, states, low, mix, inner, gp, acc, dec, sums, reds, gain_rows):
    tokens, channels = inner.shape
    chunk = min(256, channels // 2)
    half = channels // 2 // chunk
    height = low.shape[1] + rank + states + 3 * SUB

    def columns(rows):
        return pl.BlockSpec((rows, chunk), lambda i: (0, i))

    def fixed(a):
        return pl.BlockSpec(a.shape, lambda i: (0, 0))

    made = jax.ShapeDtypeStruct((height, channels // 2), bf16)
    return pl.pallas_call(
        functools.partial(pack_body, half, rank, states),
        grid=(2 * half,),
        in_specs=[fixed(low), fixed(mix), columns(tokens), columns(tokens), fixed(acc), fixed(dec)] + [columns(SUB)] * 3,
        out_specs=[
            pl.BlockSpec((height, chunk), lambda i: (0, jnp.minimum(i, half - 1))),
            pl.BlockSpec((height, chunk), lambda i: (0, jnp.maximum(i - half, 0))),
        ],
        out_shape=[made, made],
        scratch_shapes=[pltpu.VMEM((height, chunk), f32)],
        compiler_params=pltpu.CompilerParams(vmem_limit_bytes=24 << 20),
        cost_estimate=cost(0.02),
        name="pack",
    )(low, mix, inner, gp, acc, dec, sums, reds, gain_rows)


def last_body(gn_ref, hidden_ref, cot_ref, gain_ref, out_ref):
    value = hidden_ref[...].astype(f32)
    factor = lax.rsqrt(jnp.mean(value * value, axis=1, keepdims=True) + EPSILON)
    xhat = value * factor
    scaled = gn_ref[...].astype(f32) * gain_ref[...]
    out_ref[...] = cot_ref[...].astype(f32) + factor * (scaled - xhat * jnp.mean(scaled * xhat, axis=1, keepdims=True))


def last(gn, hidden, cotangent, gain, parts=2):
    rows, width = hidden.shape
    block = pl.BlockSpec((rows // parts, width), lambda i: (i, 0))
    return pl.pallas_call(
        last_body,
        grid=(parts,),
        in_specs=[block, block, block, pl.BlockSpec(gain.shape, lambda i: (0, 0))],
        out_specs=block,
        out_shape=jax.ShapeDtypeStruct(hidden.shape, f32),
        cost_estimate=cost(0.02),
        name="last",
    )(gn, hidden, cotangent, gain)


def distances(lengths, pack_rows, row_count):
    slot_count = lengths.shape[0]
    picks = pack_rows[:, None] == jnp.arange(slot_count, dtype=jnp.int32)[None, :]
    packed = jnp.sum(jnp.where(picks, lengths[None, :], 0), axis=1)
    starts = jnp.cumsum(packed) - packed
    positions = jnp.arange(row_count, dtype=jnp.int32)
    latest = jnp.max(jnp.where(starts[None, :] <= positions[:, None], starts[None, :], 0), axis=1)
    return positions - latest


def after(value, *others):
    return lax.optimization_barrier((value,) + others)[0]


def swap(value, bit):
    count = lax.axis_size("fsdp")
    return lax.ppermute(value, "fsdp", [(i, i ^ bit) for i in range(count)])


class Gather:
    def __init__(self, value, order):
        self.pieces, self.order, self.size = {0: value}, list(order), value.shape[0]

    def send(self, *waits):
        bit = self.order.pop(0)
        self.keys, self.bit = sorted(self.pieces), bit
        sent = [self.pieces[k] for k in self.keys]
        sent = jnp.concatenate(sent, axis=0) if len(sent) > 1 else sent[0]
        self.sent = after(sent, *waits) if waits else sent
        self.got = swap(self.sent, bit)
        return self.got

    def take(self, *waits):
        got = after(self.got, *waits) if waits else self.got
        for i, k in enumerate(self.keys):
            self.pieces[k | self.bit] = lax.slice_in_dim(got, i * self.size, (i + 1) * self.size, axis=0)


class WeightGrad:
    def __init__(self, lows, other, kept, orders):
        self.orders = [list(order) for order in orders]
        self.keys = [list(kept) for _ in orders]
        self.leave = grad_half(1, lows, other)
        self.lows, self.other = lows, other
        self.columns = True

    def exchange(self, *waits):
        self.gots = [swap(after(self.leave, *waits) if waits else self.leave, 1)] * len(self.orders)

    def rest(self, *waits):
        self.bases = [grad_half(0, after(self.lows, self.leave, *waits), self.other)] * len(self.orders)
        return self.bases[0]

    def go(self, *waits):
        streams, plans, bits = [], [], []
        gots = [after(self.gots[0], *waits)] + self.gots[1:] if waits else self.gots
        if waits and self.columns:
            gots = [gots[0]] * len(gots)
        for s, keys in enumerate(self.keys):
            bit = self.orders[s].pop(0)
            shape = (len(keys), -1, self.bases[s].shape[-1])
            pair = (self.bases[s].reshape(shape), gots[s].reshape(shape))
            streams.append((pair, s if self.columns else None))
            leave = [i for i, k in enumerate(keys) if k & bit]
            stay = [i for i, k in enumerate(keys) if not k & bit]
            plans.append((stay, leave))
            bits.append(bit)
            self.keys[s] = [keys[i] for i in stay]
        made = stage(streams, plans)
        self.bases, sents = made[0::2], made[1::2]
        self.gots = [swap(sent, bit) for sent, bit in zip(sents, bits)]
        self.columns = False
        return tuple(sents)

    def finish(self, plane=0, planes=1, into=None):
        while self.orders[0]:
            self.go()
        return join(list(zip(self.bases, self.gots)), plane, planes, into)


def ring_parts(part):
    count = lax.axis_size("tensor")
    parts = [part]
    for step in range(1, count):
        parts.append(lax.ppermute(part, "tensor", [(i, (i + step) % count) for i in range(count)]))
    return parts


def placed(places):
    count = len(places)
    own = lax.axis_index("fsdp")
    owners = jnp.bitwise_xor(jnp.asarray(places, jnp.int32), own.astype(jnp.int32))
    return lax.broadcasted_iota(jnp.int32, (count, count), 0) == owners[None, :]


def shards(
    hidden,
    cotangent,
    seq_lengths,
    pack_order,
    norm_gain,
    w_in,
    conv_weight,
    conv_bias,
    w_xproj,
    w_dt,
    dt_bias,
    a_log,
    d_skip,
    w_out,
):
    n_fsdp = lax.axis_size("fsdp")
    n_tensor = lax.axis_size("tensor")
    place = lax.axis_index("tensor")
    own_channels = w_in.shape[1]
    width = hidden.shape[1]
    group_rows = hidden.shape[0] * n_tensor
    rank = w_dt.shape[1]
    states = a_log.shape[1]
    taps = conv_weight.shape[1]
    wide = [1 << i for i in range(1, n_fsdp.bit_length() - 1)]
    narrow = wide[::-1]
    kept = [k for k in range(n_fsdp) if not k & 1]
    places = kept + [k + 1 for k in kept]
    channels = own_channels * n_fsdp
    middle = channels // 2

    rows_all = lax.all_gather(hidden, "tensor", axis=0, tiled=True)
    gather_x, gather_g = Gather(w_in[0], wide), Gather(w_in[1], narrow)
    first_x, first_g = gather_x.send(), gather_g.send()
    first_x, first_g = lax.optimization_barrier((first_x, first_g))
    gather_x.got, gather_g.got = first_x, first_g
    gather_x.take()
    gather_g.take()
    for _ in wide[1:]:
        gather_x.send()
        gather_g.send()
        if gather_x.order:
            gather_x.take()
            gather_g.take()
    gain_own = after(norm_gain.reshape(1, -1), first_x, first_g)
    lines = lax.broadcasted_iota(jnp.int32, (n_tensor, 1), 0)
    gain_line = jnp.where(lines == place, gain_own, 0)
    for step in range(1, n_tensor):
        got = lax.ppermute(gain_own, "tensor", [(i, (i + step) % n_tensor) for i in range(n_tensor)])
        gain_line = jnp.where(lines == lax.rem(place - step + n_tensor, n_tensor), got, gain_line)
    gain_rows = width // n_fsdp // own_channels
    small = jnp.concatenate(
        [
            w_xproj.T,
            w_dt.T,
            a_log.T,
            conv_weight.T,
            conv_bias[None],
            dt_bias[None],
            d_skip[None],
            gain_line.reshape(gain_rows, own_channels),
        ],
        axis=0,
    )
    small_a = jnp.concatenate([small] + [swap(small, k) for k in kept[1:]], axis=1)
    small_all = jnp.concatenate([small_a, swap(small_a, 1)], axis=1)
    got_x, got_g = after(gather_x.got, small_a), after(gather_g.got, small_a)
    weights = (
        gather_x.sent, got_x, swap(gather_x.sent, 1), swap(got_x, 1),
        gather_g.sent, got_g, swap(gather_g.sent, 1), swap(got_g, 1),
    )
    half_width = width // 2
    cot_l = lax.all_gather(after(cotangent[:, :half_width], first_x), "tensor", axis=0, tiled=True)
    gather_o = Gather(after(w_out, got_x, got_g), wide)
    gather_o.send()

    xw = rank + 2 * states
    w_xp = small_all[:xw]
    w_dt_rows = small_all[xw : xw + rank]
    at = xw + rank
    a_rows = small_all[at : at + states].astype(f32)
    at = at + states
    conv_rows = small_all[at : at + taps].astype(f32)
    at = at + taps
    conv_b = small_all[at : at + 1].astype(f32)
    dt_b = small_all[at + 1 : at + 2].astype(f32)
    skip_row = small_all[at + 2 : at + 3].astype(f32)
    gain_all = small_all[at + 3 :].astype(f32).reshape(1, gain_rows, n_fsdp, own_channels)
    owners = placed(places)
    gain = jnp.sum(jnp.where(owners[:, None, :, None], gain_all, 0.0), axis=2).reshape(1, width)
    rates = (-jnp.exp(a_rows) * math.log2(math.e)).reshape(-1, LANES)

    offsets = distances(seq_lengths[0], pack_order[0], group_rows)
    keep = (offsets > 0).astype(jnp.int32)
    dist = offsets[:, None]
    normed = norm_rows(rows_all, gain, n_tensor)

    signal, gate, inner, mixed_own = front(normed, weights, conv_rows, conv_b, w_xp, dist, own_channels)
    parts = ring_parts(mixed_own)
    for _ in wide[1:]:
        gather_o.take(mixed_own)
        gather_o.send()
    none = jnp.zeros(rates.shape, f32)
    states_all, deltas, sums, gated, mixed, _ = scan_forward(
        0, keep, parts, w_dt_rows, dt_b, skip_row, rates, inner, gate, none
    )
    cot_r = lax.all_gather(after(cotangent[:, half_width:], *parts), "tensor", axis=0, tiled=True)
    got_o, sent_o = after(gather_o.got, mixed), after(gather_o.sent, mixed)
    quarters = (sent_o, got_o, swap(sent_o, 1), swap(got_o, 1))
    grad_gated, branch = cross((cot_l, cot_r), gated, quarters)
    branch_own = lax.psum_scatter(branch, "tensor", scatter_dimension=0, tiled=True)
    output = (hidden.astype(f32) + branch_own.astype(f32)).astype(bf16)
    orders = (wide, narrow)

    out_grad = WeightGrad(after(gated, branch), (cot_l, cot_r), kept, orders)
    out_grad.exchange()
    out_grad.rest()
    g_scan, g_gate, g_proj, g_mixed, reds, acc, _ = scan_backward(
        0, keep, after(mixed, out_grad.bases[0]), w_dt_rows, skip_row, rates, inner, gate, grad_gated, sums, states_all,
        deltas, none,
    )
    backs = ring_parts(g_mixed)
    gate_grad = WeightGrad(g_gate, (normed,), kept, orders)
    gate_grad.rest()
    sent = out_grad.go(gate_grad.bases[0])
    backs[0] = after(backs[0], *sent)
    gate_grad.exchange(*backs[1:])
    g_signal, low, _, conv_sums = turn(0, backs, g_scan, signal, conv_rows, conv_b, w_xp, dist)
    sent = gate_grad.go(low)
    g_norm, gain_term = rear(
        after(g_signal, branch_own, *sent, *out_grad.gots), g_gate, weights, normed, own_channels
    )
    g_norm = after(g_norm, *gate_grad.gots)
    g_norm_own = lax.psum_scatter(g_norm, "tensor", scatter_dimension=0, tiled=True)
    gain_sum = sum(part.astype(f32) for part in ring_parts((gain_term / gain).astype(bf16)))
    gain_sum = lax.dynamic_index_in_dim(gain_sum.reshape(n_fsdp, n_tensor, -1), place, 1, False)
    gain_sum = jnp.sum(jnp.where(owners[:, :, None], gain_sum[:, None, :], 0.0), axis=0)
    gain_sum = jnp.pad(gain_sum, ((0, 0), (0, own_channels - gain_sum.shape[1]))).reshape(1, channels)
    gain_sum = jnp.concatenate([gain_sum, jnp.zeros((SUB - 1, channels), f32)], axis=0)
    sent = out_grad.go(g_norm)
    sig_grad = WeightGrad(after(g_signal, *sent), (normed,), kept, orders)
    sig_grad.exchange()
    sent = gate_grad.go(sig_grad.leave)
    sig_grad.rest(*sent)
    small_stay, small_leave = pack(
        rank, states, low, mixed, inner, g_proj, acc, rates, conv_sums, reds, after(gain_sum, sig_grad.bases[0])
    )
    small_got = swap(small_leave, 1)
    sent = sig_grad.go(small_leave, *out_grad.gots)
    small_half = small_stay.astype(f32) + after(small_got, *sent).astype(f32)
    small_cuts = [small_half[:, i * own_channels : (i + 1) * own_channels] for i in range(len(kept))]
    small_lows = [cut.astype(bf16) for cut in small_cuts[1:]]
    small_gots = [swap(low, k) for low, k in zip(small_lows, kept[1:])]
    out_grad.gots[0] = after(out_grad.gots[0], *small_lows)
    grad_w_out = out_grad.finish()[0]
    gate_grad.gots[0] = after(gate_grad.gots[0], grad_w_out)
    grad_w_in = gate_grad.finish(1, 2)
    sig_grad.go(grad_w_in)
    small_gots[0] = after(small_gots[0], sig_grad.bases[0])
    small_own = small_cuts[0]
    for got in small_gots:
        small_own = small_own + got.astype(f32)
    grad_hidden = last(after(g_norm_own, small_own), hidden, cotangent, gain)
    grad_w_in = sig_grad.finish(0, 2, grad_w_in)
    at = xw + rank + states
    grad_gain = small_own[at + 2 * SUB, : norm_gain.shape[0]]
    columns = small_own.T
    return (
        output,
        grad_hidden,
        grad_gain,
        grad_w_in,
        columns[:, at : at + taps],
        small_own[at + taps],
        columns[:, :xw],
        columns[:, xw : xw + rank],
        small_own[at + SUB + 1],
        columns[:, at - states : at],
        small_own[at + SUB],
        grad_w_out,
    )


def solution(mesh):
    every = ("fsdp", "tensor")
    rows = P(every, None)
    line = P(every)
    planes = P(None, every, None)
    return jax.shard_map(
        shards,
        mesh=mesh,
        in_specs=(rows, rows, P("fsdp", None), P("fsdp", None), line, planes, rows, line, rows, rows, line, rows, line, rows),
        out_specs=(rows, rows, line, planes, rows, line, rows, rows, line, rows, line, rows),
        check_vma=False,
    )
```

```python
import functools
import math

import jax
import jax.numpy as jnp
from jax import lax
from jax.experimental import pallas as pl
from jax.experimental.pallas import tpu as pltpu
from jax.sharding import PartitionSpec as P

EPSILON = 1e-05
f32 = jnp.float32
bf16 = jnp.bfloat16
BIG = 1e30
LANES = 128
SUB = 8


def cost(micros):
    return pl.CostEstimate(flops=int(micros * 1e9), transcendentals=0, bytes_accessed=int(micros * 1e6))


def tile_rows(ti, j, subs):
    return pl.ds((ti * subs + j) * SUB, SUB)


def put_tiles(ref, value, subs):
    for ti in range(value.shape[0] // SUB):
        for j in range(subs):
            ref[tile_rows(ti, j, subs), :] = value[ti * SUB : (ti + 1) * SUB, j * LANES : (j + 1) * LANES]


def get_tiles(ref, rows, subs):
    lines = []
    for ti in range(rows // SUB):
        lines.append(jnp.concatenate([ref[tile_rows(ti, j, subs), :] for j in range(subs)], axis=1))
    return jnp.concatenate(lines, axis=0)


def put_spread(ref, value, count):
    for ti in range(value.shape[0] // SUB):
        for n in range(count):
            ref[pl.ds((ti * count + n) * SUB, SUB), :] = jnp.broadcast_to(
                value[ti * SUB : (ti + 1) * SUB, n : n + 1], (SUB, LANES)
            )


def fwd_body(
    states, subs, first_row, count, keep_ref, *refs
):
    part_refs, refs = refs[:count], refs[count:]
    wdt_ref, db_ref, ds_ref, dec_ref, inner_ref, gate_ref, h0_ref = refs[:7]
    hs_ref, dl_ref, ys_ref, gated_ref, mixed_ref, h_ref, du_sc, bb_sc, y_sc = refs[-9:]
    chunk = pl.program_id(0)
    rows = inner_ref.shape[0]
    span = states * subs
    rank = wdt_ref.shape[0]

    @pl.when(chunk == 0)
    def _():
        h_ref[...] = h0_ref[...]
        total = part_refs[0][...].astype(f32)
        for part_ref in part_refs[1:]:
            total = total + part_ref[...].astype(f32)
        mixed_ref[:, pl.ds(0, rank)] = total[:rank].T
        blank = jnp.zeros((LANES - 2 * states, total.shape[1]), f32)
        mixed_ref[:, pl.ds(rank, LANES)] = jnp.concatenate([total[rank:], blank], axis=0).T

    own_rows = pl.ds(pl.multiple_of(chunk * rows, rows), rows)
    step_in = mixed_ref[own_rows, pl.ds(0, rank)].astype(bf16)
    raw = jnp.dot(step_in, wdt_ref[...], preferred_element_type=f32) + db_ref[...]
    delta = jnp.maximum(raw, 0.0) + jnp.log1p(jnp.exp(-jnp.abs(raw)))
    inner = inner_ref[...].astype(f32)
    put_tiles(dl_ref, delta, subs)
    put_tiles(du_sc, delta * inner, subs)
    put_spread(bb_sc, mixed_ref[own_rows, pl.ds(rank, LANES)], 2 * states)
    hs_ref[pl.ds(0, span), :] = h_ref[...]
    decs = [dec_ref[pl.ds(n * subs, subs), :] for n in range(states)]

    def step(ti, hs):
        hs = list(hs)
        for s in range(SUB):
            t = ti * SUB + s
            row = ti * (subs * SUB) + s
            d = dl_ref[pl.ds(row, subs, stride=SUB), :]
            u = du_sc[pl.ds(row, subs, stride=SUB), :]
            d = jnp.where(keep_ref[first_row + chunk * rows + t] > 0, d, BIG)
            y = None
            for n in range(states):
                b = bb_sc[pl.ds((ti * 2 * states + n) * SUB + s, subs, stride=0), :]
                c = bb_sc[pl.ds((ti * 2 * states + states + n) * SUB + s, subs, stride=0), :]
                hs[n] = jnp.exp2(d * decs[n]) * hs[n] + u * b
                hs_ref[pl.ds(pl.multiple_of((t + 1) * span + n * subs, subs), subs), :] = hs[n]
                y = c * hs[n] if y is None else y + c * hs[n]
            y_sc[pl.ds(row, subs, stride=SUB), :] = y
        return tuple(hs)

    start = tuple(h_ref[pl.ds(n * subs, subs), :] for n in range(states))
    hs = lax.fori_loop(0, rows // SUB, step, start)
    for n in range(states):
        h_ref[pl.ds(n * subs, subs), :] = hs[n]
    total = get_tiles(y_sc, rows, subs) + ds_ref[...] * inner
    ys_ref[...] = total
    gate = gate_ref[...]
    gated_ref[...] = (total * gate / (1.0 + jnp.exp(-gate))).astype(bf16)


def scan_forward(h, keep, parts, wdt, dt_bias, d_skip, dec, inner, gate, h0, into=None, chunk_rows=64):
    rows, channels = gate.shape
    subs = channels // LANES
    rank = wdt.shape[0]
    states = (parts[0].shape[0] - rank) // 2
    mix = rank + LANES
    chunks = rows // chunk_rows
    span = states * subs

    def row_block(width, start=0):
        return pl.BlockSpec((chunk_rows, width), lambda i, *_: (start + i, 0))

    def whole(a):
        return pl.BlockSpec(a.shape, lambda i, *_: (0, 0))

    extra = [] if into is None else [into]
    grid_spec = pltpu.PrefetchScalarGridSpec(
        num_scalar_prefetch=1,
        grid=(chunks,),
        in_specs=[whole(part) for part in parts]
        + [whole(wdt), whole(dt_bias), whole(d_skip), whole(dec), row_block(channels, h * chunks), row_block(channels), whole(h0)]
        + [pl.BlockSpec(memory_space=pl.ANY) for _ in extra],
        out_specs=[
            pl.BlockSpec(((chunk_rows + 1) * span, LANES), lambda i, *_: (i, 0)),
            pl.BlockSpec((chunk_rows * subs, LANES), lambda i, *_: (i, 0)),
            row_block(channels), row_block(channels, h * chunks), pl.BlockSpec((rows, mix), lambda i, *_: (0, 0)), whole(h0),
        ],
        scratch_shapes=[
            pltpu.VMEM((chunk_rows * subs, LANES), f32),
            pltpu.VMEM((chunk_rows * 2 * states, LANES), f32),
            pltpu.VMEM((chunk_rows * subs, LANES), f32),
        ],
    )
    made = jax.ShapeDtypeStruct
    return pl.pallas_call(
        functools.partial(fwd_body, states, subs, h * rows, len(parts)),
        grid_spec=grid_spec,
        out_shape=[
            made((chunks * (chunk_rows + 1) * span, LANES), f32), made((rows * subs, LANES), f32),
            made((rows, channels), f32), made(inner.shape, bf16), made((rows, mix), f32), made((span, LANES), f32),
        ],
        input_output_aliases={} if into is None else {len(parts) + 8: 3},
        compiler_params=pltpu.CompilerParams(vmem_limit_bytes=58 << 20),
        cost_estimate=cost(40.0),
        name="scan_forward",
    )(keep, *parts, wdt, dt_bias, d_skip, dec, inner, gate, h0, *extra)


def fold_rows(parts, sub_iota):
    if parts[0].shape[0] != SUB:
        return jnp.concatenate([jnp.sum(p, axis=0, keepdims=True) for p in parts], axis=0)
    upper = sub_iota < 4
    xs = [
        jnp.where(upper, parts[n], parts[n + 4]) + pltpu.roll(jnp.where(upper, parts[n + 4], parts[n]), 4, 0)
        for n in range(4)
    ]
    pair = (sub_iota & 3) < 2
    ys = [
        jnp.where(pair, xs[n] + pltpu.roll(xs[n], 6, 0), xs[n + 2] + pltpu.roll(xs[n + 2], 2, 0))
        for n in range(2)
    ]
    even = (sub_iota & 1) == 0
    return jnp.where(even, ys[0] + pltpu.roll(ys[0], 7, 0), ys[1] + pltpu.roll(ys[1], 1, 0))


def bwd_body(
    states, subs, first_row, keep_ref, fwd_ref, wdt_ref, dst_ref, dec_ref, inner_ref, gate_ref, gg_ref, ys_ref, hs_ref,
    dl_ref, gh0_ref, *refs
):
    gi_ref, gx_ref, gp_ref, mixed_ref, red_ref, acc_ref, gh_ref, in_sc, gy_sc, bb_sc, gd_sc, go_sc, r_sc = refs[-13:]
    i = pl.program_id(0)
    last = pl.num_programs(0) - 1
    chunk = last - i
    rows = inner_ref.shape[0]
    all_rows = r_sc.shape[0] // (2 * states)
    span = states * subs
    rank = wdt_ref.shape[0]

    @pl.when(i == 0)
    def _():
        gh_ref[...] = gh0_ref[...]
        acc_ref[...] = jnp.zeros_like(acc_ref)
        red_ref[...] = jnp.zeros_like(red_ref)

    gate = gate_ref[...]
    sig = 1.0 / (1.0 + jnp.exp(-gate))
    gg = gg_ref[...].astype(f32)
    gy_all = gg * (gate * sig)
    gx_ref[...] = (gg * ys_ref[...] * (sig * (1.0 + gate * (1.0 - sig)))).astype(bf16)
    inner_all = inner_ref[...].astype(f32)
    red_ref[pl.ds(0, 1), :] += jnp.sum(gy_all * inner_all, axis=0, keepdims=True)
    put_tiles(gy_sc, gy_all, subs)
    put_tiles(in_sc, inner_all, subs)
    put_spread(bb_sc, fwd_ref[...][:, rank:], 2 * states)
    sub_iota = lax.broadcasted_iota(jnp.int32, (SUB, LANES), 0)
    skip = dst_ref[...]
    order = (0, 4, 2, 6, 1, 5, 3, 7)

    def step(k, carried):
        ghs = list(carried[:states])
        accs = list(carried[states:])
        ti = rows // SUB - 1 - k
        for s in reversed(range(SUB)):
            t = ti * SUB + s
            row = ti * (subs * SUB) + s
            d = dl_ref[pl.ds(row, subs, stride=SUB), :]
            v = in_sc[pl.ds(row, subs, stride=SUB), :]
            gy = gy_sc[pl.ds(row, subs, stride=SUB), :]
            u = d * v
            da = jnp.where(keep_ref[first_row + chunk * rows + t] > 0, d, BIG)
            gd = gs = None
            for g in range(states // SUB):
                pb = [None] * SUB
                pc = [None] * SUB
                for o in order:
                    n = g * SUB + o
                    b = bb_sc[pl.ds((ti * 2 * states + n) * SUB + s, subs, stride=0), :]
                    c = bb_sc[pl.ds((ti * 2 * states + states + n) * SUB + s, subs, stride=0), :]
                    dec = dec_ref[pl.ds(n * subs, subs), :]
                    before = hs_ref[pl.ds(pl.multiple_of(t * span + n * subs, subs), subs), :]
                    after = hs_ref[pl.ds(pl.multiple_of((t + 1) * span + n * subs, subs), subs), :]
                    gh = c * gy + ghs[n]
                    ghs[n] = jnp.exp2(da * dec) * gh
                    q = ghs[n] * before
                    gd = dec * q if gd is None else gd + dec * q
                    accs[n] = accs[n] + q * d
                    gs = gh * b if gs is None else gs + gh * b
                    pb[o] = gh * u
                    pc[o] = after * gy
                at = chunk * rows + t
                r_sc[pl.ds(g * SUB * all_rows + at, SUB, stride=all_rows), :] = fold_rows(pb, sub_iota)
                r_sc[pl.ds((states + g * SUB) * all_rows + at, SUB, stride=all_rows), :] = fold_rows(pc, sub_iota)
            gd_sc[pl.ds(row, subs, stride=SUB), :] = gd * math.log(2.0) + gs * v
            go_sc[pl.ds(row, subs, stride=SUB), :] = gy * skip + gs * d
        return tuple(ghs + accs)

    init = tuple(gh_ref[pl.ds(n * subs, subs), :] for n in range(states))
    init = init + tuple(acc_ref[pl.ds(n * subs, subs), :] for n in range(states))
    out = lax.fori_loop(0, rows // SUB, step, init)
    for n in range(states):
        gh_ref[pl.ds(n * subs, subs), :] = out[n]
        acc_ref[pl.ds(n * subs, subs), :] = out[states + n]
    gi_ref[...] = get_tiles(go_sc, rows, subs)
    d_all = get_tiles(dl_ref, rows, subs)
    series = d_all * (1.0 - d_all * (0.5 - d_all * (1.0 / 6 - d_all * (1.0 / 24))))
    slope = jnp.where(d_all < 0.03125, series, 1.0 - jnp.exp(-d_all))
    gp = get_tiles(gd_sc, rows, subs) * slope
    red_ref[pl.ds(1, 1), :] += jnp.sum(gp, axis=0, keepdims=True)
    gp_ref[pl.ds(pl.multiple_of(chunk * rows, rows), rows), :] = gp.astype(bf16)

    @pl.when(i == last)
    def _():
        lane = lax.broadcasted_iota(jnp.int32, (LANES, LANES), 1)
        total = jnp.zeros((all_rows, LANES), f32)
        for n in range(2 * states):
            pick = jnp.where(lane == n, 1.0, 0.0).astype(bf16)
            part = r_sc[pl.ds(n * all_rows, all_rows), :].astype(bf16)
            total = total + jnp.dot(part, pick, preferred_element_type=f32)
        step = lax.dot_general(wdt_ref[...], gp_ref[...], (((1,), (1,)), ((), ())), preferred_element_type=f32)
        mixed_ref[pl.ds(0, rank), :] = step.astype(bf16)
        mixed_ref[pl.ds(rank, 2 * states), :] = total.T[: 2 * states].astype(bf16)


def scan_backward(h, keep, mixed, wdt, d_skip, dec, inner, gate, gg, ysum, hs, delta_tm, gh0, into=(), chunk_rows=64):
    rows, channels = gate.shape
    subs = channels // LANES
    rank = wdt.shape[0]
    mix = mixed.shape[1]
    states = dec.shape[0] // subs
    chunks = rows // chunk_rows
    span = states * subs
    skip_tm = d_skip.reshape(subs, LANES)

    def row_block(width, start=0):
        return pl.BlockSpec((chunk_rows, width), lambda i, *_: (start + chunks - 1 - i, 0))

    def fixed(shape):
        return pl.BlockSpec(shape, lambda i, *_: (0, 0))

    tile = pltpu.VMEM((chunk_rows * subs, LANES), f32)
    first = h * chunks
    grid_spec = pltpu.PrefetchScalarGridSpec(
        num_scalar_prefetch=1,
        grid=(chunks,),
        in_specs=[
            row_block(mix), fixed(wdt.shape), fixed(skip_tm.shape), fixed(dec.shape),
            row_block(channels, first), row_block(channels), row_block(channels, first), row_block(channels),
            pl.BlockSpec(((chunk_rows + 1) * span, LANES), lambda i, *_: (chunks - 1 - i, 0)),
            pl.BlockSpec((chunk_rows * subs, LANES), lambda i, *_: (chunks - 1 - i, 0)), fixed(gh0.shape),
        ]
        + [pl.BlockSpec(memory_space=pl.ANY) for _ in into],
        out_specs=[
            row_block(channels), row_block(channels, first), fixed((rows, channels)), fixed((rank + 2 * states, rows)),
            fixed((8, channels)), fixed((span, LANES)), fixed((span, LANES)),
        ],
        scratch_shapes=[
            tile, tile, pltpu.VMEM((chunk_rows * 2 * states, LANES), f32), tile, tile,
            pltpu.VMEM((2 * states * rows, LANES), f32),
        ],
    )
    made = jax.ShapeDtypeStruct
    return pl.pallas_call(
        functools.partial(bwd_body, states, subs, h * rows),
        grid_spec=grid_spec,
        out_shape=[
            made((rows, channels), f32), made(inner.shape, bf16), made(inner.shape, bf16),
            made((rank + 2 * states, rows), bf16), made((8, channels), f32), made((span, LANES), f32),
            made((span, LANES), f32),
        ],
        input_output_aliases={12 + i: 1 + i for i in range(len(into))},
        compiler_params=pltpu.CompilerParams(vmem_limit_bytes=58 << 20),
        cost_estimate=cost(100.0),
        name="scan_backward",
    )(keep, mixed, wdt, skip_tm, dec, inner, gate, gg, ysum, hs, delta_tm, gh0, *into)


def norm_body(gain_ref, rows_ref, out_ref):
    value = rows_ref[...].astype(f32)
    factor = lax.rsqrt(jnp.mean(value * value, axis=1, keepdims=True) + EPSILON)
    out_ref[...] = (value * factor * gain_ref[...]).astype(bf16)


def norm_rows(rows_all, gain, parts):
    rows, width = rows_all.shape
    block = pl.BlockSpec((rows // parts, width), lambda i: (i, 0))
    return pl.pallas_call(
        norm_body,
        grid=(parts,),
        in_specs=[pl.BlockSpec(gain.shape, lambda i: (0, 0)), block],
        out_specs=block,
        out_shape=jax.ShapeDtypeStruct((rows, width), bf16),
        compiler_params=pltpu.CompilerParams(vmem_limit_bytes=24 << 20),
        cost_estimate=cost(0.02),
        name="norm_rows",
    )(gain, rows_all)


def weave(one, two, own):
    pieces = []
    for at in range(0, one.shape[0], own):
        pieces += [one[at : at + own], two[at : at + own]]
    return jnp.concatenate(pieces, axis=0)


def weight_specs(chunk, width):
    whole = pl.BlockSpec((chunk, width), lambda i: (0, 0))
    first = pl.BlockSpec((chunk // 2, width), lambda i: (jnp.minimum(i, 1), 0))
    second = pl.BlockSpec((chunk // 2, width), lambda i: (jnp.maximum(i - 2, 0), 0))
    return [whole] * 4 + [first, first, second, second]


def front_body(
    own, normed_ref, *refs
):
    x_refs, g_refs, refs = refs[:4], refs[4:8], refs[8:]
    taps_ref, bias_ref, wxp_ref, dist_ref = refs[:4]
    refs = refs[4:]
    sig_ref, gate_ref, inner_ref, mixed_ref, ext_sc, acc_sc = refs[-6:]
    i = pl.program_id(0)
    rows = normed_ref.shape[0]
    dims = (((1,), (1,)), ((), ()))

    def project(x_ref, one_ref, two_ref):
        normed = normed_ref[...]
        ext_sc[pl.ds(SUB, rows), :] = lax.dot_general(normed, x_ref[...], dims, preferred_element_type=f32)
        gate = weave(one_ref[...], two_ref[...], own)
        gate_ref[...] = lax.dot_general(normed, gate, dims, preferred_element_type=f32)

    for block in range(4):

        @pl.when(i == block)
        def _(block=block):
            project(x_refs[block], *g_refs[block // 2 * 2 : block // 2 * 2 + 2])

    ext_sc[pl.ds(0, SUB), :] = jnp.zeros((SUB, ext_sc.shape[1]), f32)
    taps = taps_ref.shape[0]
    signal = ext_sc[pl.ds(SUB, rows), :]
    sig_ref[...] = signal
    dist = dist_ref[...]
    pre = bias_ref[...] + taps_ref[pl.ds(taps - 1, 1), :] * signal
    for lag in range(1, taps):
        shifted = ext_sc[pl.ds(SUB - lag, rows), :]
        pre = pre + jnp.where(dist >= lag, taps_ref[pl.ds(taps - 1 - lag, 1), :] * shifted, 0.0)
    inner = (pre / (1.0 + jnp.exp(-pre))).astype(bf16)
    inner_ref[...] = inner
    part = lax.dot_general(wxp_ref[...], inner, dims, preferred_element_type=f32)

    @pl.when(i == 0)
    def _():
        acc_sc[...] = part

    @pl.when(i > 0)
    def _():
        acc_sc[...] += part

    mixed_ref[...] = acc_sc[...].astype(bf16)


def front(normed, weights, taps, bias, w_xp, dist, own):
    rows, width = normed.shape
    channels = taps.shape[1]
    chunk = channels // 4
    xw = w_xp.shape[0]

    def columns(height):
        return pl.BlockSpec((height, chunk), lambda i: (0, i))

    made = jax.ShapeDtypeStruct
    return pl.pallas_call(
        functools.partial(front_body, own),
        grid=(4,),
        in_specs=[pl.BlockSpec((rows, width), lambda i: (0, 0))]
        + weight_specs(chunk, width)
        + [columns(taps.shape[0]), columns(1), columns(xw), pl.BlockSpec((rows, 1), lambda i: (0, 0))],
        out_specs=[columns(rows), columns(rows), columns(rows), pl.BlockSpec((xw, rows), lambda i: (0, 0))],
        out_shape=[
            made((rows, channels), f32), made((rows, channels), f32), made((rows, channels), bf16),
            made((xw, rows), bf16),
        ],
        scratch_shapes=[pltpu.VMEM((rows + SUB, chunk), f32), pltpu.VMEM((xw, rows), f32)],
        compiler_params=pltpu.CompilerParams(vmem_limit_bytes=44 << 20),
        cost_estimate=cost(0.02),
        name="front",
    )(normed, *weights, taps, bias, w_xp, dist)


def turn_body(count, begins, ends, *refs):
    part_refs, refs = refs[:count], refs[count:]
    gis_ref, sig_ref, taps_ref, bias_ref, wxp_ref, dist_ref = refs[:6]
    more = list(refs[6:-6])
    gsig_ref, low_ref, head_ref, sums_ref, ext_sc, late_sc = refs[-6:]
    rows, chunk = gis_ref.shape
    taps = taps_ref.shape[0]
    nothing = jnp.zeros((SUB, chunk), f32)
    ext_sc[pl.ds(0, SUB), :] = nothing if begins else more.pop(0)[...]
    ext_sc[pl.ds(SUB, rows), :] = sig_ref[...]
    dist = dist_ref[...]
    signal = sig_ref[...]
    pre = bias_ref[...] + taps_ref[pl.ds(taps - 1, 1), :] * signal
    earlier = {}
    for lag in range(1, taps):
        earlier[lag] = jnp.where(dist >= lag, ext_sc[pl.ds(SUB - lag, rows), :], 0.0)
        pre = pre + taps_ref[pl.ds(taps - 1 - lag, 1), :] * earlier[lag]
    sig = 1.0 / (1.0 + jnp.exp(-pre))
    mixed = part_refs[0][...].astype(f32)
    for part_ref in part_refs[1:]:
        mixed = mixed + part_ref[...].astype(f32)
    low = mixed.astype(bf16)
    low_ref[...] = low
    g_inner = gis_ref[...] + lax.dot_general(
        low, wxp_ref[...], (((0,), (0,)), ((), ())), preferred_element_type=f32
    )
    g_pre = g_inner * (sig * (1.0 + pre * (1.0 - sig)))
    head_ref[...] = g_pre[:SUB, :]
    lines = [None] * taps
    lines[taps - 1] = jnp.sum(g_pre * signal, axis=0, keepdims=True)
    g_signal = taps_ref[pl.ds(taps - 1, 1), :] * g_pre
    if not ends:
        next_ref, dnext_ref = more.pop(0), more.pop(0)
    for lag in range(1, taps):
        masked = jnp.where(dist >= lag, g_pre, 0.0)
        lines[taps - 1 - lag] = jnp.sum(g_pre * earlier[lag], axis=0, keepdims=True)
        late_sc[pl.ds(0, rows), :] = masked
        late_sc[pl.ds(rows, SUB), :] = nothing if ends else jnp.where(dnext_ref[...] >= lag, next_ref[...], 0.0)
        g_signal = g_signal + taps_ref[pl.ds(taps - 1 - lag, 1), :] * late_sc[pl.ds(lag, rows), :]
    lines.append(jnp.sum(g_pre, axis=0, keepdims=True))
    sums_ref[...] = jnp.zeros_like(sums_ref)
    for k, value in enumerate(lines):
        sums_ref[pl.ds(k, 1), :] = value
    gsig_ref[...] = g_signal.astype(bf16)


def turn(h, parts, gis, signal, taps, bias, w_xp, dist, before=None, later=None):
    rows, channels = gis.shape
    chunk = min(256, channels // 2)
    xw = w_xp.shape[0]

    def columns(height, start=0):
        return pl.BlockSpec((height, chunk), lambda i: (start, i))

    def fixed(a):
        return pl.BlockSpec(a.shape, lambda i: (0, 0))

    extra, extra_specs, alias = [], [], {}
    if before is not None:
        extra.append(before)
        extra_specs.append(columns(SUB, rows // SUB - 1))
    if later is not None:
        extra += [later[2], dist, later[0]]
        extra_specs += [
            columns(SUB), pl.BlockSpec((SUB, 1), lambda i: ((h + 1) * rows // SUB, 0)), pl.BlockSpec(memory_space=pl.ANY)
        ]
        alias = {len(parts) + 6 + len(extra) - 1: 0}
    made = jax.ShapeDtypeStruct
    return pl.pallas_call(
        functools.partial(turn_body, len(parts), before is None, later is None),
        grid=(channels // chunk,),
        in_specs=[fixed(part) for part in parts]
        + [
            columns(rows), columns(rows), columns(taps.shape[0]), columns(1), columns(xw),
            pl.BlockSpec((rows, 1), lambda i: (h, 0)),
        ]
        + extra_specs,
        out_specs=[columns(rows, h), pl.BlockSpec((xw, rows), lambda i: (0, 0)), columns(SUB), columns(SUB)],
        out_shape=[
            made((dist.shape[0], channels), bf16), made((xw, rows), bf16), made((SUB, channels), f32),
            made((SUB, channels), f32),
        ],
        scratch_shapes=[pltpu.VMEM((rows + SUB, chunk), f32), pltpu.VMEM((rows + SUB, chunk), f32)],
        input_output_aliases=alias,
        compiler_params=pltpu.CompilerParams(vmem_limit_bytes=32 << 20),
        cost_estimate=cost(40.0),
        name="turn",
    )(*parts, gis, signal, taps, bias, w_xp, dist, *extra)


def rear_body(own, gs_ref, gx_ref, *refs):
    x_refs, g_refs, (normed_ref, out_ref, gain_ref, acc_sc) = refs[:4], refs[4:8], refs[8:]
    i = pl.program_id(0)
    for block in range(4):

        @pl.when(i == block)
        def _(block=block):
            gate = weave(*[ref[...] for ref in g_refs[block // 2 * 2 : block // 2 * 2 + 2]], own)
            part = jnp.dot(gs_ref[...], x_refs[block][...], preferred_element_type=f32) + jnp.dot(
                gx_ref[...], gate, preferred_element_type=f32
            )
            if block == 0:
                acc_sc[...] = part
            elif block < 3:
                acc_sc[...] += part
            else:
                total = acc_sc[...] + part
                out_ref[...] = total.astype(bf16)
                gain_ref[...] = jnp.sum(total * normed_ref[...].astype(f32), axis=0, keepdims=True)


def rear(g_signal, g_gate, weights, normed, own):
    rows, width = normed.shape
    channels = g_signal.shape[1]
    chunk = channels // 4
    columns = pl.BlockSpec((rows, chunk), lambda i: (0, i))
    whole = pl.BlockSpec((rows, width), lambda i: (0, 0))
    made = jax.ShapeDtypeStruct
    return pl.pallas_call(
        functools.partial(rear_body, own),
        grid=(4,),
        in_specs=[columns, columns] + weight_specs(chunk, width) + [whole],
        out_specs=[whole, pl.BlockSpec((1, width), lambda i: (0, 0))],
        out_shape=[made((rows, width), bf16), made((1, width), f32)],
        scratch_shapes=[pltpu.VMEM((rows, width), f32)],
        compiler_params=pltpu.CompilerParams(vmem_limit_bytes=60 << 20),
        cost_estimate=cost(40.0),
        name="rear",
    )(g_signal, g_gate, *weights, normed)


def cross_body(left_ref, right_ref, gated_ref, *refs):
    quarters, (gg_ref, out_ref) = refs[:4], refs[4:]
    chunk = quarters[0].shape[0]
    half = left_ref.shape[1]
    dims = (((1,), (1,)), ((), ()))
    total = None
    for q in range(4):
        w = quarters[q][...]
        cut = pl.ds(q * chunk, chunk)
        part = lax.dot_general(left_ref[...], w[:, :half], dims, preferred_element_type=f32)
        part = part + lax.dot_general(right_ref[...], w[:, half:], dims, preferred_element_type=f32)
        gg_ref[:, cut] = part.astype(bf16)
        part = jnp.dot(gated_ref[:, cut], w, preferred_element_type=f32)
        total = part if total is None else total + part
    out_ref[...] = total.astype(bf16)


def cross(cots, gated, quarters, parts=2):
    tokens, half = cots[0].shape
    channels = gated.shape[1]
    rows = tokens // parts

    def row_block(columns):
        return pl.BlockSpec((rows, columns), lambda i: (i, 0))

    made = jax.ShapeDtypeStruct
    return pl.pallas_call(
        cross_body,
        grid=(parts,),
        in_specs=[row_block(half), row_block(half), row_block(channels)]
        + [pl.BlockSpec(quarter.shape, lambda i: (0, 0)) for quarter in quarters],
        out_specs=[row_block(channels), row_block(2 * half)],
        out_shape=[made((tokens, channels), bf16), made((tokens, 2 * half), bf16)],
        compiler_params=pltpu.CompilerParams(vmem_limit_bytes=60 << 20),
        cost_estimate=cost(0.02),
        name="cross",
    )(*cots, gated, *quarters)


def stage_body(plans, *refs):
    refs = list(refs)
    sums = []
    for _ in plans:
        base, got = refs.pop(0), refs.pop(0)
        sums.append([base[k].astype(f32) + got[k].astype(f32) for k in range(base.shape[0])])
    for (stay, leave), blocks in zip(plans, sums):
        kept = refs.pop(0)
        for i, k in enumerate(stay):
            kept[i] = blocks[k]
        if leave:
            sent = refs.pop(0)
            for i, k in enumerate(leave):
                sent[i] = blocks[k].astype(bf16)


def stage(streams, plans, steps=2):
    height = streams[0][0][0].shape[1] // steps
    ins, in_specs, outs, out_specs = [], [], [], []
    for (base, got), (stay, leave), column in streams_with(streams, plans):
        width = base.shape[2] if column is None else base.shape[2] // len(streams)
        for a in (base, got):
            ins.append(a)
            in_specs.append(
                pl.BlockSpec((a.shape[0], height, width), lambda i, column=column: (0, i, 0 if column is None else column))
            )
        for blocks, kind in ((stay, f32), (leave, bf16)):
            if blocks:
                outs.append(jax.ShapeDtypeStruct((len(blocks), height * steps, width), kind))
                out_specs.append(pl.BlockSpec((len(blocks), height, width), lambda i: (0, i, 0)))
    return pl.pallas_call(
        functools.partial(stage_body, plans),
        grid=(steps,),
        in_specs=in_specs,
        out_specs=out_specs,
        out_shape=outs,
        compiler_params=pltpu.CompilerParams(vmem_limit_bytes=40 << 20),
        cost_estimate=cost(0.02),
        name="stage",
    )(*ins)


def streams_with(streams, plans):
    for (pair, column), plan in zip(streams, plans):
        yield pair, plan, column


def join_body(*refs):
    out_ref = refs[-1]
    pairs = [(refs[2 * i], refs[2 * i + 1]) for i in range((len(refs) - 1) // 2)]
    width = pairs[0][0].shape[2]
    for i, (base, got) in enumerate(pairs):
        out_ref[0, :, pl.ds(i * width, width)] = base[0].astype(f32) + got[0].astype(f32)


def join(pairs, plane, planes, into=None, steps=2):
    _, rows, width = pairs[0][0].shape
    height = rows // steps
    ins = [a for pair in pairs for a in pair]
    extra = [] if into is None else [into]

    def body(*refs):
        join_body(*refs[: len(ins)], refs[-1])

    return pl.pallas_call(
        body,
        grid=(steps,),
        in_specs=[pl.BlockSpec((1, height, width), lambda i: (0, i, 0)) for _ in ins]
        + [pl.BlockSpec(memory_space=pl.ANY) for _ in extra],
        out_specs=pl.BlockSpec((1, height, width * len(pairs)), lambda i: (plane, i, 0)),
        out_shape=jax.ShapeDtypeStruct((planes, rows, width * len(pairs)), f32),
        input_output_aliases={} if into is None else {len(ins): 0},
        compiler_params=pltpu.CompilerParams(vmem_limit_bytes=24 << 20),
        cost_estimate=cost(0.02),
        name="join",
    )(*ins, *extra)


def grad_body(lows_ref, *refs):
    out_ref = refs[-1]
    at = 0
    for ref in refs[:-1]:
        part = lax.dot_general(lows_ref[...], ref[...], (((0,), (0,)), ((), ())), preferred_element_type=f32)
        out_ref[:, pl.ds(at, ref.shape[1])] = part.astype(bf16)
        at += ref.shape[1]


def grad_half(h, lows, others):
    tokens, channels = lows.shape
    width = sum(other.shape[1] for other in others)
    chunk = min(256, channels // 2)
    steps = channels // 2 // chunk
    return pl.pallas_call(
        grad_body,
        grid=(steps,),
        in_specs=[pl.BlockSpec((tokens, chunk), lambda i: (0, h * steps + i))]
        + [pl.BlockSpec(other.shape, lambda i: (0, 0)) for other in others],
        out_specs=pl.BlockSpec((chunk, width), lambda i: (i, 0)),
        out_shape=jax.ShapeDtypeStruct((channels // 2, width), bf16),
        compiler_params=pltpu.CompilerParams(vmem_limit_bytes=24 << 20),
        cost_estimate=cost(0.02),
        name="grad_half",
    )(lows, *others)


def pack_body(half, rank, states, low_ref, mix_ref, inner_ref, gp_ref, acc_ref, dec_ref, sum_ref, red_ref, gain_ref,
              stay_ref, leave_ref, all_sc):
    i = pl.program_id(0)
    dims = (((0,), (0,)), ((), ()))
    chunk, xw = inner_ref.shape[1], low_ref.shape[0]
    all_sc[pl.ds(0, xw), :] = jnp.dot(low_ref[...], inner_ref[...], preferred_element_type=f32)
    step_in = mix_ref[...][:, :rank].astype(bf16)
    all_sc[pl.ds(xw, rank), :] = lax.dot_general(step_in, gp_ref[...], dims, preferred_element_type=f32)
    subs = dec_ref.shape[0] // states
    wide = chunk // LANES
    for j in range(wide):
        cut = pl.ds(i * wide + j, states, stride=subs)
        all_sc[pl.ds(xw + rank, states), pl.ds(j * LANES, LANES)] = acc_ref[cut, :] * (dec_ref[cut, :] * math.log(2.0))
    at = xw + rank + states
    all_sc[pl.ds(at, SUB), :] = sum_ref[...]
    all_sc[pl.ds(at + SUB, SUB), :] = red_ref[...]
    all_sc[pl.ds(at + 2 * SUB, SUB), :] = gain_ref[...]

    @pl.when(i < half)
    def _():
        stay_ref[...] = all_sc[...].astype(bf16)

    @pl.when(i >= half)
    def _():
        leave_ref[...] = all_sc[...].astype(bf16)


def pack(rank, states, low, mix, inner, gp, acc, dec, sums, reds, gain_rows):
    tokens, channels = inner.shape
    chunk = min(256, channels // 2)
    half = channels // 2 // chunk
    height = low.shape[0] + rank + states + 3 * SUB

    def columns(rows):
        return pl.BlockSpec((rows, chunk), lambda i: (0, i))

    def fixed(a):
        return pl.BlockSpec(a.shape, lambda i: (0, 0))

    made = jax.ShapeDtypeStruct((height, channels // 2), bf16)
    return pl.pallas_call(
        functools.partial(pack_body, half, rank, states),
        grid=(2 * half,),
        in_specs=[fixed(low), fixed(mix), columns(tokens), columns(tokens), fixed(acc), fixed(dec)] + [columns(SUB)] * 3,
        out_specs=[
            pl.BlockSpec((height, chunk), lambda i: (0, jnp.minimum(i, half - 1))),
            pl.BlockSpec((height, chunk), lambda i: (0, jnp.maximum(i - half, 0))),
        ],
        out_shape=[made, made],
        scratch_shapes=[pltpu.VMEM((height, chunk), f32)],
        compiler_params=pltpu.CompilerParams(vmem_limit_bytes=24 << 20),
        cost_estimate=cost(0.02),
        name="pack",
    )(low, mix, inner, gp, acc, dec, sums, reds, gain_rows)


def last_body(gn_ref, hidden_ref, cot_ref, gain_ref, out_ref):
    value = hidden_ref[...].astype(f32)
    factor = lax.rsqrt(jnp.mean(value * value, axis=1, keepdims=True) + EPSILON)
    xhat = value * factor
    scaled = gn_ref[...].astype(f32) * gain_ref[...]
    out_ref[...] = cot_ref[...].astype(f32) + factor * (scaled - xhat * jnp.mean(scaled * xhat, axis=1, keepdims=True))


def last(gn, hidden, cotangent, gain, parts=2):
    rows, width = hidden.shape
    block = pl.BlockSpec((rows // parts, width), lambda i: (i, 0))
    return pl.pallas_call(
        last_body,
        grid=(parts,),
        in_specs=[block, block, block, pl.BlockSpec(gain.shape, lambda i: (0, 0))],
        out_specs=block,
        out_shape=jax.ShapeDtypeStruct(hidden.shape, f32),
        cost_estimate=cost(0.02),
        name="last",
    )(gn, hidden, cotangent, gain)


def distances(lengths, pack_rows, row_count):
    slot_count = lengths.shape[0]
    picks = pack_rows[:, None] == jnp.arange(slot_count, dtype=jnp.int32)[None, :]
    packed = jnp.sum(jnp.where(picks, lengths[None, :], 0), axis=1)
    starts = jnp.cumsum(packed) - packed
    positions = jnp.arange(row_count, dtype=jnp.int32)
    latest = jnp.max(jnp.where(starts[None, :] <= positions[:, None], starts[None, :], 0), axis=1)
    return positions - latest


def after(value, *others):
    return lax.optimization_barrier((value,) + others)[0]


def swap(value, bit):
    count = lax.axis_size("fsdp")
    return lax.ppermute(value, "fsdp", [(i, i ^ bit) for i in range(count)])


class Gather:
    def __init__(self, value, order):
        self.pieces, self.order, self.size = {0: value}, list(order), value.shape[0]

    def send(self, *waits):
        bit = self.order.pop(0)
        self.keys, self.bit = sorted(self.pieces), bit
        sent = [self.pieces[k] for k in self.keys]
        sent = jnp.concatenate(sent, axis=0) if len(sent) > 1 else sent[0]
        self.sent = after(sent, *waits) if waits else sent
        self.got = swap(self.sent, bit)
        return self.got

    def take(self, *waits):
        got = after(self.got, *waits) if waits else self.got
        for i, k in enumerate(self.keys):
            self.pieces[k | self.bit] = lax.slice_in_dim(got, i * self.size, (i + 1) * self.size, axis=0)


class WeightGrad:
    def __init__(self, lows, other, kept, orders):
        self.orders = [list(order) for order in orders]
        self.keys = [list(kept) for _ in orders]
        self.leave = grad_half(1, lows, other)
        self.lows, self.other = lows, other
        self.columns = True

    def exchange(self, *waits):
        self.gots = [swap(after(self.leave, *waits) if waits else self.leave, 1)] * len(self.orders)

    def rest(self, *waits):
        self.bases = [grad_half(0, after(self.lows, self.leave, *waits), self.other)] * len(self.orders)
        return self.bases[0]

    def go(self, *waits):
        streams, plans, bits = [], [], []
        gots = [after(self.gots[0], *waits)] + self.gots[1:] if waits else self.gots
        if waits and self.columns:
            gots = [gots[0]] * len(gots)
        for s, keys in enumerate(self.keys):
            bit = self.orders[s].pop(0)
            shape = (len(keys), -1, self.bases[s].shape[-1])
            pair = (self.bases[s].reshape(shape), gots[s].reshape(shape))
            streams.append((pair, s if self.columns else None))
            leave = [i for i, k in enumerate(keys) if k & bit]
            stay = [i for i, k in enumerate(keys) if not k & bit]
            plans.append((stay, leave))
            bits.append(bit)
            self.keys[s] = [keys[i] for i in stay]
        made = stage(streams, plans)
        self.bases, sents = made[0::2], made[1::2]
        self.gots = [swap(sent, bit) for sent, bit in zip(sents, bits)]
        self.columns = False
        return tuple(sents)

    def finish(self, plane=0, planes=1, into=None):
        while self.orders[0]:
            self.go()
        return join(list(zip(self.bases, self.gots)), plane, planes, into)


def ring_parts(part):
    count = lax.axis_size("tensor")
    parts = [part]
    for step in range(1, count):
        parts.append(lax.ppermute(part, "tensor", [(i, (i + step) % count) for i in range(count)]))
    return parts


def placed(places):
    count = len(places)
    own = lax.axis_index("fsdp")
    owners = jnp.bitwise_xor(jnp.asarray(places, jnp.int32), own.astype(jnp.int32))
    return lax.broadcasted_iota(jnp.int32, (count, count), 0) == owners[None, :]


def shards(
    hidden,
    cotangent,
    seq_lengths,
    pack_order,
    norm_gain,
    w_in,
    conv_weight,
    conv_bias,
    w_xproj,
    w_dt,
    dt_bias,
    a_log,
    d_skip,
    w_out,
):
    n_fsdp = lax.axis_size("fsdp")
    n_tensor = lax.axis_size("tensor")
    place = lax.axis_index("tensor")
    own_channels = w_in.shape[1]
    width = hidden.shape[1]
    group_rows = hidden.shape[0] * n_tensor
    rank = w_dt.shape[1]
    states = a_log.shape[1]
    taps = conv_weight.shape[1]
    wide = [1 << i for i in range(1, n_fsdp.bit_length() - 1)]
    narrow = wide[::-1]
    kept = [k for k in range(n_fsdp) if not k & 1]
    places = kept + [k + 1 for k in kept]
    channels = own_channels * n_fsdp
    middle = channels // 2

    rows_all = lax.all_gather(hidden, "tensor", axis=0, tiled=True)
    gather_x, gather_g = Gather(w_in[0], wide), Gather(w_in[1], narrow)
    first_x, first_g = gather_x.send(), gather_g.send()
    first_x, first_g = lax.optimization_barrier((first_x, first_g))
    gather_x.got, gather_g.got = first_x, first_g
    gather_x.take()
    gather_g.take()
    for _ in wide[1:]:
        gather_x.send()
        gather_g.send()
        if gather_x.order:
            gather_x.take()
            gather_g.take()
    gain_own = after(norm_gain.reshape(1, -1), first_x, first_g)
    lines = lax.broadcasted_iota(jnp.int32, (n_tensor, 1), 0)
    gain_line = jnp.where(lines == place, gain_own, 0)
    for step in range(1, n_tensor):
        got = lax.ppermute(gain_own, "tensor", [(i, (i + step) % n_tensor) for i in range(n_tensor)])
        gain_line = jnp.where(lines == lax.rem(place - step + n_tensor, n_tensor), got, gain_line)
    gain_rows = width // n_fsdp // own_channels
    small = jnp.concatenate(
        [
            w_xproj.T,
            w_dt.T,
            a_log.T,
            conv_weight.T,
            conv_bias[None],
            dt_bias[None],
            d_skip[None],
            gain_line.reshape(gain_rows, own_channels),
        ],
        axis=0,
    )
    small_a = jnp.concatenate([small] + [swap(small, k) for k in kept[1:]], axis=1)
    small_all = jnp.concatenate([small_a, swap(small_a, 1)], axis=1)
    got_x, got_g = after(gather_x.got, small_a), after(gather_g.got, small_a)
    weights = (
        gather_x.sent, got_x, swap(gather_x.sent, 1), swap(got_x, 1),
        gather_g.sent, got_g, swap(gather_g.sent, 1), swap(got_g, 1),
    )
    half_width = width // 2
    cot_l = lax.all_gather(after(cotangent[:, :half_width], first_x), "tensor", axis=0, tiled=True)
    gather_o = Gather(after(w_out, got_x, got_g), wide)
    gather_o.send()

    xw = rank + 2 * states
    w_xp = small_all[:xw]
    w_dt_rows = small_all[xw : xw + rank]
    at = xw + rank
    a_rows = small_all[at : at + states].astype(f32)
    at = at + states
    conv_rows = small_all[at : at + taps].astype(f32)
    at = at + taps
    conv_b = small_all[at : at + 1].astype(f32)
    dt_b = small_all[at + 1 : at + 2].astype(f32)
    skip_row = small_all[at + 2 : at + 3].astype(f32)
    gain_all = small_all[at + 3 :].astype(f32).reshape(1, gain_rows, n_fsdp, own_channels)
    owners = placed(places)
    gain = jnp.sum(jnp.where(owners[:, None, :, None], gain_all, 0.0), axis=2).reshape(1, width)
    rates = (-jnp.exp(a_rows) * math.log2(math.e)).reshape(-1, LANES)

    offsets = distances(seq_lengths[0], pack_order[0], group_rows)
    keep = (offsets > 0).astype(jnp.int32)
    dist = offsets[:, None]
    normed = norm_rows(rows_all, gain, n_tensor)

    signal, gate, inner, mixed_own = front(normed, weights, conv_rows, conv_b, w_xp, dist, own_channels)
    parts = ring_parts(mixed_own)
    for _ in wide[1:]:
        gather_o.take(mixed_own)
        gather_o.send()
    cot_r = lax.all_gather(after(cotangent[:, half_width:], *parts), "tensor", axis=0, tiled=True)
    got_o, sent_o = after(gather_o.got, *parts[1:]), after(gather_o.sent, *parts[1:])
    quarters = (sent_o, got_o, swap(sent_o, 1), swap(got_o, 1))
    none = jnp.zeros(rates.shape, f32)
    states_all, deltas, sums, gated, mixed, _ = scan_forward(
        0, keep, parts, w_dt_rows, dt_b, skip_row, rates, inner, gate, none
    )
    quarters = tuple(after(quarter, mixed) for quarter in quarters)
    grad_gated, branch = cross((cot_l, cot_r), gated, quarters)
    branch_own = lax.psum_scatter(branch, "tensor", scatter_dimension=0, tiled=True)
    output = (hidden.astype(f32) + branch_own.astype(f32)).astype(bf16)
    orders = (wide, narrow)

    out_grad = WeightGrad(after(gated, branch), (cot_l, cot_r), kept, orders)
    out_grad.exchange()
    out_grad.rest()
    g_scan, g_gate, g_proj, g_mixed, reds, acc, _ = scan_backward(
        0, keep, after(mixed, out_grad.bases[0]), w_dt_rows, skip_row, rates, inner, gate, grad_gated, sums, states_all,
        deltas, none,
    )
    backs = ring_parts(g_mixed)
    gate_grad = WeightGrad(g_gate, (normed,), kept, orders)
    gate_grad.rest()
    sent = out_grad.go(gate_grad.bases[0])
    backs[0] = after(backs[0], *sent)
    gate_grad.exchange()
    g_signal, low, _, conv_sums = turn(0, backs, g_scan, signal, conv_rows, conv_b, w_xp, dist)
    sent = gate_grad.go(low)
    g_norm, gain_term = rear(
        after(g_signal, branch_own, *sent, *out_grad.gots), g_gate, weights, normed, own_channels
    )
    g_norm = after(g_norm, *gate_grad.gots)
    g_norm_own = lax.psum_scatter(g_norm, "tensor", scatter_dimension=0, tiled=True)
    gain_sum = sum(part.astype(f32) for part in ring_parts((gain_term / gain).astype(bf16)))
    gain_sum = lax.dynamic_index_in_dim(gain_sum.reshape(n_fsdp, n_tensor, -1), place, 1, False)
    gain_sum = jnp.sum(jnp.where(owners[:, :, None], gain_sum[:, None, :], 0.0), axis=0)
    gain_sum = jnp.pad(gain_sum, ((0, 0), (0, own_channels - gain_sum.shape[1]))).reshape(1, channels)
    gain_sum = jnp.concatenate([gain_sum, jnp.zeros((SUB - 1, channels), f32)], axis=0)
    sig_grad = WeightGrad(after(g_signal, g_norm), (normed,), kept, orders)
    sig_grad.exchange()
    sent = out_grad.go(sig_grad.leave)
    sig_grad.rest(*sent)
    sent = gate_grad.go(sig_grad.bases[0])
    sent = sig_grad.go(*sent)
    small_stay, small_leave = pack(
        rank, states, low, mixed, inner, g_proj, acc, rates, conv_sums, reds, after(gain_sum, *sent)
    )
    small_got = swap(small_leave, 1)
    out_grad.gots[0] = after(out_grad.gots[0], small_leave)
    grad_w_out = out_grad.finish()[0]
    small_half = small_stay.astype(f32) + after(small_got, grad_w_out).astype(f32)
    small_cuts = [small_half[:, i * own_channels : (i + 1) * own_channels] for i in range(len(kept))]
    small_lows = [cut.astype(bf16) for cut in small_cuts[1:]]
    small_gots = [swap(low, k) for low, k in zip(small_lows, kept[1:])]
    gate_grad.gots[0] = after(gate_grad.gots[0], *small_lows)
    grad_w_in = gate_grad.finish(1, 2)
    sig_grad.go(grad_w_in)
    small_gots[0] = after(small_gots[0], sig_grad.bases[0])
    small_own = small_cuts[0]
    for got in small_gots:
        small_own = small_own + got.astype(f32)
    grad_hidden = last(g_norm_own, hidden, cotangent, gain)
    sig_grad.gots[0] = after(sig_grad.gots[0], grad_hidden)
    grad_w_in = sig_grad.finish(0, 2, grad_w_in)
    at = xw + rank + states
    grad_gain = small_own[at + 2 * SUB, : norm_gain.shape[0]]
    columns = small_own.T
    return (
        output,
        grad_hidden,
        grad_gain,
        grad_w_in,
        columns[:, at : at + taps],
        small_own[at + taps],
        columns[:, :xw],
        columns[:, xw : xw + rank],
        small_own[at + SUB + 1],
        columns[:, at - states : at],
        small_own[at + SUB],
        grad_w_out,
    )


def solution(mesh):
    every = ("fsdp", "tensor")
    rows = P(every, None)
    line = P(every)
    planes = P(None, every, None)
    return jax.shard_map(
        shards,
        mesh=mesh,
        in_specs=(rows, rows, P("fsdp", None), P("fsdp", None), line, planes, rows, line, rows, rows, line, rows, line, rows),
        out_specs=(rows, rows, line, planes, rows, line, rows, rows, line, rows, line, rows),
        check_vma=False,
    )
```

```python
import functools
import math

import jax
import jax.numpy as jnp
from jax import lax
from jax.experimental import pallas as pl
from jax.experimental.pallas import tpu as pltpu
from jax.sharding import PartitionSpec as P

EPSILON = 1e-05
f32 = jnp.float32
bf16 = jnp.bfloat16
BIG = 1e30
LANES = 128
SUB = 8


def cost(micros):
    return pl.CostEstimate(flops=int(micros * 1e9), transcendentals=0, bytes_accessed=int(micros * 1e6))


def tile_rows(ti, j, subs):
    return pl.ds((ti * subs + j) * SUB, SUB)


def put_tiles(ref, value, subs):
    for ti in range(value.shape[0] // SUB):
        for j in range(subs):
            ref[tile_rows(ti, j, subs), :] = value[ti * SUB : (ti + 1) * SUB, j * LANES : (j + 1) * LANES]


def get_tiles(ref, rows, subs):
    lines = []
    for ti in range(rows // SUB):
        lines.append(jnp.concatenate([ref[tile_rows(ti, j, subs), :] for j in range(subs)], axis=1))
    return jnp.concatenate(lines, axis=0)


def put_spread(ref, value, count):
    for ti in range(value.shape[0] // SUB):
        for n in range(count):
            ref[pl.ds((ti * count + n) * SUB, SUB), :] = jnp.broadcast_to(
                value[ti * SUB : (ti + 1) * SUB, n : n + 1], (SUB, LANES)
            )


def fwd_body(
    states, subs, first_row, count, keep_ref, *refs
):
    part_refs, refs = refs[:count], refs[count:]
    wdt_ref, db_ref, ds_ref, dec_ref, inner_ref, gate_ref, h0_ref = refs[:7]
    hs_ref, dl_ref, ys_ref, gated_ref, mixed_ref, h_ref, du_sc, bb_sc, y_sc = refs[-9:]
    chunk = pl.program_id(0)
    rows = inner_ref.shape[0]
    span = states * subs
    rank = wdt_ref.shape[0]

    @pl.when(chunk == 0)
    def _():
        h_ref[...] = h0_ref[...]
        total = part_refs[0][...].astype(f32)
        for part_ref in part_refs[1:]:
            total = total + part_ref[...].astype(f32)
        mixed_ref[:, pl.ds(0, rank)] = total[:rank].T
        blank = jnp.zeros((LANES - 2 * states, total.shape[1]), f32)
        mixed_ref[:, pl.ds(rank, LANES)] = jnp.concatenate([total[rank:], blank], axis=0).T

    own_rows = pl.ds(pl.multiple_of(chunk * rows, rows), rows)
    step_in = mixed_ref[own_rows, pl.ds(0, rank)].astype(bf16)
    raw = jnp.dot(step_in, wdt_ref[...], preferred_element_type=f32) + db_ref[...]
    delta = jnp.maximum(raw, 0.0) + jnp.log1p(jnp.exp(-jnp.abs(raw)))
    inner = inner_ref[...].astype(f32)
    put_tiles(dl_ref, delta, subs)
    put_tiles(du_sc, delta * inner, subs)
    put_spread(bb_sc, mixed_ref[own_rows, pl.ds(rank, LANES)], 2 * states)
    hs_ref[pl.ds(0, span), :] = h_ref[...]
    decs = [dec_ref[pl.ds(n * subs, subs), :] for n in range(states)]

    def step(ti, hs):
        hs = list(hs)
        for s in range(SUB):
            t = ti * SUB + s
            row = ti * (subs * SUB) + s
            d = dl_ref[pl.ds(row, subs, stride=SUB), :]
            u = du_sc[pl.ds(row, subs, stride=SUB), :]
            d = jnp.where(keep_ref[first_row + chunk * rows + t] > 0, d, BIG)
            y = None
            for n in range(states):
                b = bb_sc[pl.ds((ti * 2 * states + n) * SUB + s, subs, stride=0), :]
                c = bb_sc[pl.ds((ti * 2 * states + states + n) * SUB + s, subs, stride=0), :]
                hs[n] = jnp.exp2(d * decs[n]) * hs[n] + u * b
                hs_ref[pl.ds(pl.multiple_of((t + 1) * span + n * subs, subs), subs), :] = hs[n]
                y = c * hs[n] if y is None else y + c * hs[n]
            y_sc[pl.ds(row, subs, stride=SUB), :] = y
        return tuple(hs)

    start = tuple(h_ref[pl.ds(n * subs, subs), :] for n in range(states))
    hs = lax.fori_loop(0, rows // SUB, step, start)
    for n in range(states):
        h_ref[pl.ds(n * subs, subs), :] = hs[n]
    total = get_tiles(y_sc, rows, subs) + ds_ref[...] * inner
    ys_ref[...] = total
    gate = gate_ref[...]
    gated_ref[...] = (total * gate / (1.0 + jnp.exp(-gate))).astype(bf16)


def scan_forward(h, keep, parts, wdt, dt_bias, d_skip, dec, inner, gate, h0, into=None, chunk_rows=64):
    rows, channels = gate.shape
    subs = channels // LANES
    rank = wdt.shape[0]
    states = (parts[0].shape[0] - rank) // 2
    mix = rank + LANES
    chunks = rows // chunk_rows
    span = states * subs

    def row_block(width, start=0):
        return pl.BlockSpec((chunk_rows, width), lambda i, *_: (start + i, 0))

    def whole(a):
        return pl.BlockSpec(a.shape, lambda i, *_: (0, 0))

    extra = [] if into is None else [into]
    grid_spec = pltpu.PrefetchScalarGridSpec(
        num_scalar_prefetch=1,
        grid=(chunks,),
        in_specs=[whole(part) for part in parts]
        + [whole(wdt), whole(dt_bias), whole(d_skip), whole(dec), row_block(channels, h * chunks), row_block(channels), whole(h0)]
        + [pl.BlockSpec(memory_space=pl.ANY) for _ in extra],
        out_specs=[
            pl.BlockSpec(((chunk_rows + 1) * span, LANES), lambda i, *_: (i, 0)),
            pl.BlockSpec((chunk_rows * subs, LANES), lambda i, *_: (i, 0)),
            row_block(channels), row_block(channels, h * chunks), pl.BlockSpec((rows, mix), lambda i, *_: (0, 0)), whole(h0),
        ],
        scratch_shapes=[
            pltpu.VMEM((chunk_rows * subs, LANES), f32),
            pltpu.VMEM((chunk_rows * 2 * states, LANES), f32),
            pltpu.VMEM((chunk_rows * subs, LANES), f32),
        ],
    )
    made = jax.ShapeDtypeStruct
    return pl.pallas_call(
        functools.partial(fwd_body, states, subs, h * rows, len(parts)),
        grid_spec=grid_spec,
        out_shape=[
            made((chunks * (chunk_rows + 1) * span, LANES), f32), made((rows * subs, LANES), f32),
            made((rows, channels), f32), made(inner.shape, bf16), made((rows, mix), f32), made((span, LANES), f32),
        ],
        input_output_aliases={} if into is None else {len(parts) + 8: 3},
        compiler_params=pltpu.CompilerParams(vmem_limit_bytes=58 << 20),
        cost_estimate=cost(40.0),
        name="scan_forward",
    )(keep, *parts, wdt, dt_bias, d_skip, dec, inner, gate, h0, *extra)


def fold_rows(parts, sub_iota):
    if parts[0].shape[0] != SUB:
        return jnp.concatenate([jnp.sum(p, axis=0, keepdims=True) for p in parts], axis=0)
    upper = sub_iota < 4
    xs = [
        jnp.where(upper, parts[n], parts[n + 4]) + pltpu.roll(jnp.where(upper, parts[n + 4], parts[n]), 4, 0)
        for n in range(4)
    ]
    pair = (sub_iota & 3) < 2
    ys = [
        jnp.where(pair, xs[n] + pltpu.roll(xs[n], 6, 0), xs[n + 2] + pltpu.roll(xs[n + 2], 2, 0))
        for n in range(2)
    ]
    even = (sub_iota & 1) == 0
    return jnp.where(even, ys[0] + pltpu.roll(ys[0], 7, 0), ys[1] + pltpu.roll(ys[1], 1, 0))


def bwd_body(
    states, subs, first_row, keep_ref, fwd_ref, wdt_ref, dst_ref, dec_ref, inner_ref, gate_ref, gg_ref, ys_ref, hs_ref,
    dl_ref, gh0_ref, *refs
):
    gi_ref, gx_ref, gp_ref, mixed_ref, red_ref, acc_ref, gh_ref, in_sc, gy_sc, bb_sc, gd_sc, go_sc, r_sc = refs[-13:]
    i = pl.program_id(0)
    last = pl.num_programs(0) - 1
    chunk = last - i
    rows = inner_ref.shape[0]
    all_rows = r_sc.shape[0] // (2 * states)
    span = states * subs
    rank = wdt_ref.shape[0]

    @pl.when(i == 0)
    def _():
        gh_ref[...] = gh0_ref[...]
        acc_ref[...] = jnp.zeros_like(acc_ref)
        red_ref[...] = jnp.zeros_like(red_ref)

    gate = gate_ref[...]
    sig = 1.0 / (1.0 + jnp.exp(-gate))
    gg = gg_ref[...].astype(f32)
    gy_all = gg * (gate * sig)
    gx_ref[...] = (gg * ys_ref[...] * (sig * (1.0 + gate * (1.0 - sig)))).astype(bf16)
    inner_all = inner_ref[...].astype(f32)
    red_ref[pl.ds(0, 1), :] += jnp.sum(gy_all * inner_all, axis=0, keepdims=True)
    put_tiles(gy_sc, gy_all, subs)
    put_tiles(in_sc, inner_all, subs)
    put_spread(bb_sc, fwd_ref[...][:, rank:], 2 * states)
    sub_iota = lax.broadcasted_iota(jnp.int32, (SUB, LANES), 0)
    skip = dst_ref[...]
    order = (0, 4, 2, 6, 1, 5, 3, 7)

    def step(k, carried):
        ghs = list(carried[:states])
        accs = list(carried[states:])
        ti = rows // SUB - 1 - k
        for s in reversed(range(SUB)):
            t = ti * SUB + s
            row = ti * (subs * SUB) + s
            d = dl_ref[pl.ds(row, subs, stride=SUB), :]
            v = in_sc[pl.ds(row, subs, stride=SUB), :]
            gy = gy_sc[pl.ds(row, subs, stride=SUB), :]
            u = d * v
            da = jnp.where(keep_ref[first_row + chunk * rows + t] > 0, d, BIG)
            gd = gs = None
            for g in range(states // SUB):
                pb = [None] * SUB
                pc = [None] * SUB
                for o in order:
                    n = g * SUB + o
                    b = bb_sc[pl.ds((ti * 2 * states + n) * SUB + s, subs, stride=0), :]
                    c = bb_sc[pl.ds((ti * 2 * states + states + n) * SUB + s, subs, stride=0), :]
                    dec = dec_ref[pl.ds(n * subs, subs), :]
                    before = hs_ref[pl.ds(pl.multiple_of(t * span + n * subs, subs), subs), :]
                    after = hs_ref[pl.ds(pl.multiple_of((t + 1) * span + n * subs, subs), subs), :]
                    gh = c * gy + ghs[n]
                    ghs[n] = jnp.exp2(da * dec) * gh
                    q = ghs[n] * before
                    gd = dec * q if gd is None else gd + dec * q
                    accs[n] = accs[n] + q * d
                    gs = gh * b if gs is None else gs + gh * b
                    pb[o] = gh * u
                    pc[o] = after * gy
                at = chunk * rows + t
                r_sc[pl.ds(g * SUB * all_rows + at, SUB, stride=all_rows), :] = fold_rows(pb, sub_iota)
                r_sc[pl.ds((states + g * SUB) * all_rows + at, SUB, stride=all_rows), :] = fold_rows(pc, sub_iota)
            gd_sc[pl.ds(row, subs, stride=SUB), :] = gd * math.log(2.0) + gs * v
            go_sc[pl.ds(row, subs, stride=SUB), :] = gy * skip + gs * d
        return tuple(ghs + accs)

    init = tuple(gh_ref[pl.ds(n * subs, subs), :] for n in range(states))
    init = init + tuple(acc_ref[pl.ds(n * subs, subs), :] for n in range(states))
    out = lax.fori_loop(0, rows // SUB, step, init)
    for n in range(states):
        gh_ref[pl.ds(n * subs, subs), :] = out[n]
        acc_ref[pl.ds(n * subs, subs), :] = out[states + n]
    gi_ref[...] = get_tiles(go_sc, rows, subs)
    d_all = get_tiles(dl_ref, rows, subs)
    series = d_all * (1.0 - d_all * (0.5 - d_all * (1.0 / 6 - d_all * (1.0 / 24))))
    slope = jnp.where(d_all < 0.03125, series, 1.0 - jnp.exp(-d_all))
    gp = get_tiles(gd_sc, rows, subs) * slope
    red_ref[pl.ds(1, 1), :] += jnp.sum(gp, axis=0, keepdims=True)
    gp_ref[pl.ds(pl.multiple_of(chunk * rows, rows), rows), :] = gp.astype(bf16)

    @pl.when(i == last)
    def _():
        lane = lax.broadcasted_iota(jnp.int32, (LANES, LANES), 1)
        total = jnp.zeros((all_rows, LANES), f32)
        for n in range(2 * states):
            pick = jnp.where(lane == n, 1.0, 0.0).astype(bf16)
            part = r_sc[pl.ds(n * all_rows, all_rows), :].astype(bf16)
            total = total + jnp.dot(part, pick, preferred_element_type=f32)
        step = lax.dot_general(wdt_ref[...], gp_ref[...], (((1,), (1,)), ((), ())), preferred_element_type=f32)
        mixed_ref[pl.ds(0, rank), :] = step.astype(bf16)
        mixed_ref[pl.ds(rank, 2 * states), :] = total.T[: 2 * states].astype(bf16)


def scan_backward(h, keep, mixed, wdt, d_skip, dec, inner, gate, gg, ysum, hs, delta_tm, gh0, into=(), chunk_rows=64):
    rows, channels = gate.shape
    subs = channels // LANES
    rank = wdt.shape[0]
    mix = mixed.shape[1]
    states = dec.shape[0] // subs
    chunks = rows // chunk_rows
    span = states * subs
    skip_tm = d_skip.reshape(subs, LANES)

    def row_block(width, start=0):
        return pl.BlockSpec((chunk_rows, width), lambda i, *_: (start + chunks - 1 - i, 0))

    def fixed(shape):
        return pl.BlockSpec(shape, lambda i, *_: (0, 0))

    tile = pltpu.VMEM((chunk_rows * subs, LANES), f32)
    first = h * chunks
    grid_spec = pltpu.PrefetchScalarGridSpec(
        num_scalar_prefetch=1,
        grid=(chunks,),
        in_specs=[
            row_block(mix), fixed(wdt.shape), fixed(skip_tm.shape), fixed(dec.shape),
            row_block(channels, first), row_block(channels), row_block(channels, first), row_block(channels),
            pl.BlockSpec(((chunk_rows + 1) * span, LANES), lambda i, *_: (chunks - 1 - i, 0)),
            pl.BlockSpec((chunk_rows * subs, LANES), lambda i, *_: (chunks - 1 - i, 0)), fixed(gh0.shape),
        ]
        + [pl.BlockSpec(memory_space=pl.ANY) for _ in into],
        out_specs=[
            row_block(channels), row_block(channels, first), fixed((rows, channels)), fixed((rank + 2 * states, rows)),
            fixed((8, channels)), fixed((span, LANES)), fixed((span, LANES)),
        ],
        scratch_shapes=[
            tile, tile, pltpu.VMEM((chunk_rows * 2 * states, LANES), f32), tile, tile,
            pltpu.VMEM((2 * states * rows, LANES), f32),
        ],
    )
    made = jax.ShapeDtypeStruct
    return pl.pallas_call(
        functools.partial(bwd_body, states, subs, h * rows),
        grid_spec=grid_spec,
        out_shape=[
            made((rows, channels), f32), made(inner.shape, bf16), made(inner.shape, bf16),
            made((rank + 2 * states, rows), bf16), made((8, channels), f32), made((span, LANES), f32),
            made((span, LANES), f32),
        ],
        input_output_aliases={12 + i: 1 + i for i in range(len(into))},
        compiler_params=pltpu.CompilerParams(vmem_limit_bytes=58 << 20),
        cost_estimate=cost(100.0),
        name="scan_backward",
    )(keep, mixed, wdt, skip_tm, dec, inner, gate, gg, ysum, hs, delta_tm, gh0, *into)


def norm_body(gain_ref, rows_ref, out_ref):
    value = rows_ref[...].astype(f32)
    factor = lax.rsqrt(jnp.mean(value * value, axis=1, keepdims=True) + EPSILON)
    out_ref[...] = (value * factor * gain_ref[...]).astype(bf16)


def norm_rows(rows_all, gain, parts):
    rows, width = rows_all.shape
    block = pl.BlockSpec((rows // parts, width), lambda i: (i, 0))
    return pl.pallas_call(
        norm_body,
        grid=(parts,),
        in_specs=[pl.BlockSpec(gain.shape, lambda i: (0, 0)), block],
        out_specs=block,
        out_shape=jax.ShapeDtypeStruct((rows, width), bf16),
        compiler_params=pltpu.CompilerParams(vmem_limit_bytes=24 << 20),
        cost_estimate=cost(0.02),
        name="norm_rows",
    )(gain, rows_all)


def weave(one, two, own):
    pieces = []
    for at in range(0, one.shape[0], own):
        pieces += [one[at : at + own], two[at : at + own]]
    return jnp.concatenate(pieces, axis=0)


def weight_specs(chunk, width):
    whole = pl.BlockSpec((chunk, width), lambda i: (0, 0))
    first = pl.BlockSpec((chunk // 2, width), lambda i: (jnp.minimum(i, 1), 0))
    second = pl.BlockSpec((chunk // 2, width), lambda i: (jnp.maximum(i - 2, 0), 0))
    return [whole] * 4 + [first, first, second, second]


def front_body(
    own, normed_ref, *refs
):
    x_refs, g_refs, refs = refs[:4], refs[4:8], refs[8:]
    taps_ref, bias_ref, wxp_ref, dist_ref = refs[:4]
    refs = refs[4:]
    sig_ref, gate_ref, inner_ref, mixed_ref, ext_sc, acc_sc = refs[-6:]
    i = pl.program_id(0)
    rows = normed_ref.shape[0]
    dims = (((1,), (1,)), ((), ()))

    def project(x_ref, one_ref, two_ref):
        normed = normed_ref[...]
        ext_sc[pl.ds(SUB, rows), :] = lax.dot_general(normed, x_ref[...], dims, preferred_element_type=f32)
        gate = weave(one_ref[...], two_ref[...], own)
        gate_ref[...] = lax.dot_general(normed, gate, dims, preferred_element_type=f32)

    for block in range(4):

        @pl.when(i == block)
        def _(block=block):
            project(x_refs[block], *g_refs[block // 2 * 2 : block // 2 * 2 + 2])

    ext_sc[pl.ds(0, SUB), :] = jnp.zeros((SUB, ext_sc.shape[1]), f32)
    taps = taps_ref.shape[0]
    signal = ext_sc[pl.ds(SUB, rows), :]
    sig_ref[...] = signal
    dist = dist_ref[...]
    pre = bias_ref[...] + taps_ref[pl.ds(taps - 1, 1), :] * signal
    for lag in range(1, taps):
        shifted = ext_sc[pl.ds(SUB - lag, rows), :]
        pre = pre + jnp.where(dist >= lag, taps_ref[pl.ds(taps - 1 - lag, 1), :] * shifted, 0.0)
    inner = (pre / (1.0 + jnp.exp(-pre))).astype(bf16)
    inner_ref[...] = inner
    part = lax.dot_general(wxp_ref[...], inner, dims, preferred_element_type=f32)

    @pl.when(i == 0)
    def _():
        acc_sc[...] = part

    @pl.when(i > 0)
    def _():
        acc_sc[...] += part

    mixed_ref[...] = acc_sc[...].astype(bf16)


def front(normed, weights, taps, bias, w_xp, dist, own):
    rows, width = normed.shape
    channels = taps.shape[1]
    chunk = channels // 4
    xw = w_xp.shape[0]

    def columns(height):
        return pl.BlockSpec((height, chunk), lambda i: (0, i))

    made = jax.ShapeDtypeStruct
    return pl.pallas_call(
        functools.partial(front_body, own),
        grid=(4,),
        in_specs=[pl.BlockSpec((rows, width), lambda i: (0, 0))]
        + weight_specs(chunk, width)
        + [columns(taps.shape[0]), columns(1), columns(xw), pl.BlockSpec((rows, 1), lambda i: (0, 0))],
        out_specs=[columns(rows), columns(rows), columns(rows), pl.BlockSpec((xw, rows), lambda i: (0, 0))],
        out_shape=[
            made((rows, channels), f32), made((rows, channels), f32), made((rows, channels), bf16),
            made((xw, rows), bf16),
        ],
        scratch_shapes=[pltpu.VMEM((rows + SUB, chunk), f32), pltpu.VMEM((xw, rows), f32)],
        compiler_params=pltpu.CompilerParams(vmem_limit_bytes=44 << 20),
        cost_estimate=cost(0.02),
        name="front",
    )(normed, *weights, taps, bias, w_xp, dist)


def turn_body(count, begins, ends, *refs):
    part_refs, refs = refs[:count], refs[count:]
    gis_ref, sig_ref, taps_ref, bias_ref, wxp_ref, dist_ref = refs[:6]
    more = list(refs[6:-6])
    gsig_ref, low_ref, head_ref, sums_ref, ext_sc, late_sc = refs[-6:]
    rows, chunk = gis_ref.shape
    taps = taps_ref.shape[0]
    nothing = jnp.zeros((SUB, chunk), f32)
    ext_sc[pl.ds(0, SUB), :] = nothing if begins else more.pop(0)[...]
    ext_sc[pl.ds(SUB, rows), :] = sig_ref[...]
    dist = dist_ref[...]
    signal = sig_ref[...]
    pre = bias_ref[...] + taps_ref[pl.ds(taps - 1, 1), :] * signal
    earlier = {}
    for lag in range(1, taps):
        earlier[lag] = jnp.where(dist >= lag, ext_sc[pl.ds(SUB - lag, rows), :], 0.0)
        pre = pre + taps_ref[pl.ds(taps - 1 - lag, 1), :] * earlier[lag]
    sig = 1.0 / (1.0 + jnp.exp(-pre))
    mixed = part_refs[0][...].astype(f32)
    for part_ref in part_refs[1:]:
        mixed = mixed + part_ref[...].astype(f32)
    low = mixed.astype(bf16)
    low_ref[...] = low
    g_inner = gis_ref[...] + lax.dot_general(
        low, wxp_ref[...], (((0,), (0,)), ((), ())), preferred_element_type=f32
    )
    g_pre = g_inner * (sig * (1.0 + pre * (1.0 - sig)))
    head_ref[...] = g_pre[:SUB, :]
    lines = [None] * taps
    lines[taps - 1] = jnp.sum(g_pre * signal, axis=0, keepdims=True)
    g_signal = taps_ref[pl.ds(taps - 1, 1), :] * g_pre
    if not ends:
        next_ref, dnext_ref = more.pop(0), more.pop(0)
    for lag in range(1, taps):
        masked = jnp.where(dist >= lag, g_pre, 0.0)
        lines[taps - 1 - lag] = jnp.sum(g_pre * earlier[lag], axis=0, keepdims=True)
        late_sc[pl.ds(0, rows), :] = masked
        late_sc[pl.ds(rows, SUB), :] = nothing if ends else jnp.where(dnext_ref[...] >= lag, next_ref[...], 0.0)
        g_signal = g_signal + taps_ref[pl.ds(taps - 1 - lag, 1), :] * late_sc[pl.ds(lag, rows), :]
    lines.append(jnp.sum(g_pre, axis=0, keepdims=True))
    sums_ref[...] = jnp.zeros_like(sums_ref)
    for k, value in enumerate(lines):
        sums_ref[pl.ds(k, 1), :] = value
    gsig_ref[...] = g_signal.astype(bf16)


def turn(h, parts, gis, signal, taps, bias, w_xp, dist, before=None, later=None):
    rows, channels = gis.shape
    chunk = min(256, channels // 2)
    xw = w_xp.shape[0]

    def columns(height, start=0):
        return pl.BlockSpec((height, chunk), lambda i: (start, i))

    def fixed(a):
        return pl.BlockSpec(a.shape, lambda i: (0, 0))

    extra, extra_specs, alias = [], [], {}
    if before is not None:
        extra.append(before)
        extra_specs.append(columns(SUB, rows // SUB - 1))
    if later is not None:
        extra += [later[2], dist, later[0]]
        extra_specs += [
            columns(SUB), pl.BlockSpec((SUB, 1), lambda i: ((h + 1) * rows // SUB, 0)), pl.BlockSpec(memory_space=pl.ANY)
        ]
        alias = {len(parts) + 6 + len(extra) - 1: 0}
    made = jax.ShapeDtypeStruct
    return pl.pallas_call(
        functools.partial(turn_body, len(parts), before is None, later is None),
        grid=(channels // chunk,),
        in_specs=[fixed(part) for part in parts]
        + [
            columns(rows), columns(rows), columns(taps.shape[0]), columns(1), columns(xw),
            pl.BlockSpec((rows, 1), lambda i: (h, 0)),
        ]
        + extra_specs,
        out_specs=[columns(rows, h), pl.BlockSpec((xw, rows), lambda i: (0, 0)), columns(SUB), columns(SUB)],
        out_shape=[
            made((dist.shape[0], channels), bf16), made((xw, rows), bf16), made((SUB, channels), f32),
            made((SUB, channels), f32),
        ],
        scratch_shapes=[pltpu.VMEM((rows + SUB, chunk), f32), pltpu.VMEM((rows + SUB, chunk), f32)],
        input_output_aliases=alias,
        compiler_params=pltpu.CompilerParams(vmem_limit_bytes=32 << 20),
        cost_estimate=cost(40.0),
        name="turn",
    )(*parts, gis, signal, taps, bias, w_xp, dist, *extra)


def rear_body(own, gs_ref, gx_ref, *refs):
    x_refs, g_refs, (normed_ref, out_ref, gain_ref, acc_sc) = refs[:4], refs[4:8], refs[8:]
    i = pl.program_id(0)
    for block in range(4):

        @pl.when(i == block)
        def _(block=block):
            gate = weave(*[ref[...] for ref in g_refs[block // 2 * 2 : block // 2 * 2 + 2]], own)
            part = jnp.dot(gs_ref[...], x_refs[block][...], preferred_element_type=f32) + jnp.dot(
                gx_ref[...], gate, preferred_element_type=f32
            )
            if block == 0:
                acc_sc[...] = part
            elif block < 3:
                acc_sc[...] += part
            else:
                total = acc_sc[...] + part
                out_ref[...] = total.astype(bf16)
                gain_ref[...] = jnp.sum(total * normed_ref[...].astype(f32), axis=0, keepdims=True)


def rear(g_signal, g_gate, weights, normed, own):
    rows, width = normed.shape
    channels = g_signal.shape[1]
    chunk = channels // 4
    columns = pl.BlockSpec((rows, chunk), lambda i: (0, i))
    whole = pl.BlockSpec((rows, width), lambda i: (0, 0))
    made = jax.ShapeDtypeStruct
    return pl.pallas_call(
        functools.partial(rear_body, own),
        grid=(4,),
        in_specs=[columns, columns] + weight_specs(chunk, width) + [whole],
        out_specs=[whole, pl.BlockSpec((1, width), lambda i: (0, 0))],
        out_shape=[made((rows, width), bf16), made((1, width), f32)],
        scratch_shapes=[pltpu.VMEM((rows, width), f32)],
        compiler_params=pltpu.CompilerParams(vmem_limit_bytes=60 << 20),
        cost_estimate=cost(40.0),
        name="rear",
    )(g_signal, g_gate, *weights, normed)


def quarters_of(pieces):
    each = len(pieces) // 4
    for q in range(4):
        yield jnp.concatenate([piece[...] for piece in pieces[q * each : (q + 1) * each]], axis=0)


def branch_body(gated_ref, *refs):
    total, at = None, 0
    for w in quarters_of(refs[:-1]):
        part = jnp.dot(gated_ref[:, pl.ds(at, w.shape[0])], w, preferred_element_type=f32)
        total = part if total is None else total + part
        at += w.shape[0]
    refs[-1][...] = total.astype(bf16)


def cross_body(left_ref, right_ref, *refs):
    half = left_ref.shape[1]
    dims = (((1,), (1,)), ((), ()))
    at = 0
    for w in quarters_of(refs[:-1]):
        part = lax.dot_general(left_ref[...], w[:, :half], dims, preferred_element_type=f32)
        part = part + lax.dot_general(right_ref[...], w[:, half:], dims, preferred_element_type=f32)
        refs[-1][:, pl.ds(at, w.shape[0])] = part.astype(bf16)
        at += w.shape[0]


def with_pieces(body, name, lefts, pieces, columns, parts=2):
    tokens = lefts[0].shape[0]
    rows = tokens // parts

    def row_block(width):
        return pl.BlockSpec((rows, width), lambda i: (i, 0))

    return pl.pallas_call(
        body,
        grid=(parts,),
        in_specs=[row_block(left.shape[1]) for left in lefts]
        + [pl.BlockSpec(piece.shape, lambda i: (0, 0)) for piece in pieces],
        out_specs=row_block(columns),
        out_shape=jax.ShapeDtypeStruct((tokens, columns), bf16),
        compiler_params=pltpu.CompilerParams(vmem_limit_bytes=60 << 20),
        cost_estimate=cost(0.02),
        name=name,
    )(*lefts, *pieces)


def stage_body(plans, *refs):
    refs = list(refs)
    sums = []
    for _ in plans:
        base, got = refs.pop(0), refs.pop(0)
        sums.append([base[k].astype(f32) + got[k].astype(f32) for k in range(base.shape[0])])
    for (stay, leave), blocks in zip(plans, sums):
        kept = refs.pop(0)
        for i, k in enumerate(stay):
            kept[i] = blocks[k]
        if leave:
            sent = refs.pop(0)
            for i, k in enumerate(leave):
                sent[i] = blocks[k].astype(bf16)


def stage(streams, plans, steps=1):
    height = streams[0][0][0].shape[1] // steps
    ins, in_specs, outs, out_specs = [], [], [], []
    for (base, got), (stay, leave), column in streams_with(streams, plans):
        width = base.shape[2] if column is None else base.shape[2] // len(streams)
        for a in (base, got):
            ins.append(a)
            in_specs.append(
                pl.BlockSpec((a.shape[0], height, width), lambda i, column=column: (0, i, 0 if column is None else column))
            )
        for blocks, kind in ((stay, f32), (leave, bf16)):
            if blocks:
                outs.append(jax.ShapeDtypeStruct((len(blocks), height * steps, width), kind))
                out_specs.append(pl.BlockSpec((len(blocks), height, width), lambda i: (0, i, 0)))
    return pl.pallas_call(
        functools.partial(stage_body, plans),
        grid=(steps,),
        in_specs=in_specs,
        out_specs=out_specs,
        out_shape=outs,
        compiler_params=pltpu.CompilerParams(vmem_limit_bytes=40 << 20),
        cost_estimate=cost(0.02),
        name="stage",
    )(*ins)


def streams_with(streams, plans):
    for (pair, column), plan in zip(streams, plans):
        yield pair, plan, column


def join_body(*refs):
    out_ref = refs[-1]
    pairs = [(refs[2 * i], refs[2 * i + 1]) for i in range((len(refs) - 1) // 2)]
    width = pairs[0][0].shape[2]
    for i, (base, got) in enumerate(pairs):
        out_ref[0, :, pl.ds(i * width, width)] = base[0].astype(f32) + got[0].astype(f32)


def join(pairs, plane, planes, into=None, steps=2):
    _, rows, width = pairs[0][0].shape
    height = rows // steps
    ins = [a for pair in pairs for a in pair]
    extra = [] if into is None else [into]

    def body(*refs):
        join_body(*refs[: len(ins)], refs[-1])

    return pl.pallas_call(
        body,
        grid=(steps,),
        in_specs=[pl.BlockSpec((1, height, width), lambda i: (0, i, 0)) for _ in ins]
        + [pl.BlockSpec(memory_space=pl.ANY) for _ in extra],
        out_specs=pl.BlockSpec((1, height, width * len(pairs)), lambda i: (plane, i, 0)),
        out_shape=jax.ShapeDtypeStruct((planes, rows, width * len(pairs)), f32),
        input_output_aliases={} if into is None else {len(ins): 0},
        compiler_params=pltpu.CompilerParams(vmem_limit_bytes=24 << 20),
        cost_estimate=cost(0.02),
        name="join",
    )(*ins, *extra)


def grad_body(lows_ref, *refs):
    out_ref = refs[-1]
    at = 0
    for ref in refs[:-1]:
        part = lax.dot_general(lows_ref[...], ref[...], (((0,), (0,)), ((), ())), preferred_element_type=f32)
        out_ref[:, pl.ds(at, ref.shape[1])] = part.astype(bf16)
        at += ref.shape[1]


def grad_half(h, lows, others):
    tokens, channels = lows.shape
    width = sum(other.shape[1] for other in others)
    chunk = min(256, channels // 2)
    steps = channels // 2 // chunk
    return pl.pallas_call(
        grad_body,
        grid=(steps,),
        in_specs=[pl.BlockSpec((tokens, chunk), lambda i: (0, h * steps + i))]
        + [pl.BlockSpec(other.shape, lambda i: (0, 0)) for other in others],
        out_specs=pl.BlockSpec((chunk, width), lambda i: (i, 0)),
        out_shape=jax.ShapeDtypeStruct((channels // 2, width), bf16),
        compiler_params=pltpu.CompilerParams(vmem_limit_bytes=24 << 20),
        cost_estimate=cost(0.02),
        name="grad_half",
    )(lows, *others)


def pack_body(half, rank, states, low_ref, mix_ref, inner_ref, gp_ref, acc_ref, dec_ref, sum_ref, red_ref, gain_ref,
              stay_ref, leave_ref, all_sc):
    i = pl.program_id(0)
    dims = (((0,), (0,)), ((), ()))
    chunk, xw = inner_ref.shape[1], low_ref.shape[0]
    all_sc[pl.ds(0, xw), :] = jnp.dot(low_ref[...], inner_ref[...], preferred_element_type=f32)
    step_in = mix_ref[...][:, :rank].astype(bf16)
    all_sc[pl.ds(xw, rank), :] = lax.dot_general(step_in, gp_ref[...], dims, preferred_element_type=f32)
    subs = dec_ref.shape[0] // states
    wide = chunk // LANES
    for j in range(wide):
        cut = pl.ds(i * wide + j, states, stride=subs)
        all_sc[pl.ds(xw + rank, states), pl.ds(j * LANES, LANES)] = acc_ref[cut, :] * (dec_ref[cut, :] * math.log(2.0))
    at = xw + rank + states
    all_sc[pl.ds(at, SUB), :] = sum_ref[...]
    all_sc[pl.ds(at + SUB, SUB), :] = red_ref[...]
    all_sc[pl.ds(at + 2 * SUB, SUB), :] = gain_ref[...]

    @pl.when(i < half)
    def _():
        stay_ref[...] = all_sc[...].astype(bf16)

    @pl.when(i >= half)
    def _():
        leave_ref[...] = all_sc[...].astype(bf16)


def pack(rank, states, low, mix, inner, gp, acc, dec, sums, reds, gain_rows):
    tokens, channels = inner.shape
    chunk = min(256, channels // 2)
    half = channels // 2 // chunk
    height = low.shape[0] + rank + states + 3 * SUB

    def columns(rows):
        return pl.BlockSpec((rows, chunk), lambda i: (0, i))

    def fixed(a):
        return pl.BlockSpec(a.shape, lambda i: (0, 0))

    made = jax.ShapeDtypeStruct((height, channels // 2), bf16)
    return pl.pallas_call(
        functools.partial(pack_body, half, rank, states),
        grid=(2 * half,),
        in_specs=[fixed(low), fixed(mix), columns(tokens), columns(tokens), fixed(acc), fixed(dec)] + [columns(SUB)] * 3,
        out_specs=[
            pl.BlockSpec((height, chunk), lambda i: (0, jnp.minimum(i, half - 1))),
            pl.BlockSpec((height, chunk), lambda i: (0, jnp.maximum(i - half, 0))),
        ],
        out_shape=[made, made],
        scratch_shapes=[pltpu.VMEM((height, chunk), f32)],
        compiler_params=pltpu.CompilerParams(vmem_limit_bytes=24 << 20),
        cost_estimate=cost(0.02),
        name="pack",
    )(low, mix, inner, gp, acc, dec, sums, reds, gain_rows)


def last_body(gn_ref, hidden_ref, cot_ref, gain_ref, out_ref):
    value = hidden_ref[...].astype(f32)
    factor = lax.rsqrt(jnp.mean(value * value, axis=1, keepdims=True) + EPSILON)
    xhat = value * factor
    scaled = gn_ref[...].astype(f32) * gain_ref[...]
    out_ref[...] = cot_ref[...].astype(f32) + factor * (scaled - xhat * jnp.mean(scaled * xhat, axis=1, keepdims=True))


def last(gn, hidden, cotangent, gain, parts=2):
    rows, width = hidden.shape
    block = pl.BlockSpec((rows // parts, width), lambda i: (i, 0))
    return pl.pallas_call(
        last_body,
        grid=(parts,),
        in_specs=[block, block, block, pl.BlockSpec(gain.shape, lambda i: (0, 0))],
        out_specs=block,
        out_shape=jax.ShapeDtypeStruct(hidden.shape, f32),
        cost_estimate=cost(0.02),
        name="last",
    )(gn, hidden, cotangent, gain)


def distances(lengths, pack_rows, row_count):
    slot_count = lengths.shape[0]
    picks = pack_rows[:, None] == jnp.arange(slot_count, dtype=jnp.int32)[None, :]
    packed = jnp.sum(jnp.where(picks, lengths[None, :], 0), axis=1)
    starts = jnp.cumsum(packed) - packed
    positions = jnp.arange(row_count, dtype=jnp.int32)
    latest = jnp.max(jnp.where(starts[None, :] <= positions[:, None], starts[None, :], 0), axis=1)
    return positions - latest


def after(value, *others):
    return lax.optimization_barrier((value,) + others)[0]


def swap(value, bit):
    count = lax.axis_size("fsdp")
    return lax.ppermute(value, "fsdp", [(i, i ^ bit) for i in range(count)])


class Gather:
    def __init__(self, value, order):
        self.pieces, self.order, self.size = {0: value}, list(order), value.shape[0]

    def send(self, *waits):
        bit = self.order.pop(0)
        self.keys, self.bit = sorted(self.pieces), bit
        sent = [self.pieces[k] for k in self.keys]
        sent = jnp.concatenate(sent, axis=0) if len(sent) > 1 else sent[0]
        self.sent = after(sent, *waits) if waits else sent
        self.got = swap(self.sent, bit)
        return self.got

    def take(self, *waits):
        got = after(self.got, *waits) if waits else self.got
        for i, k in enumerate(self.keys):
            self.pieces[k | self.bit] = lax.slice_in_dim(got, i * self.size, (i + 1) * self.size, axis=0)


class WeightGrad:
    def __init__(self, lows, other, kept, orders):
        self.orders = [list(order) for order in orders]
        self.keys = [list(kept) for _ in orders]
        self.leave = grad_half(1, lows, other)
        self.lows, self.other = lows, other
        self.columns = True

    def exchange(self, *waits):
        self.gots = [swap(after(self.leave, *waits) if waits else self.leave, 1)] * len(self.orders)

    def rest(self, *waits):
        self.bases = [grad_half(0, after(self.lows, self.leave, *waits), self.other)] * len(self.orders)
        return self.bases[0]

    def go(self, *waits):
        streams, plans, bits = [], [], []
        gots = [after(self.gots[0], *waits)] + self.gots[1:] if waits else self.gots
        if waits and self.columns:
            gots = [gots[0]] * len(gots)
        for s, keys in enumerate(self.keys):
            bit = self.orders[s].pop(0)
            shape = (len(keys), -1, self.bases[s].shape[-1])
            pair = (self.bases[s].reshape(shape), gots[s].reshape(shape))
            streams.append((pair, s if self.columns else None))
            leave = [i for i, k in enumerate(keys) if k & bit]
            stay = [i for i, k in enumerate(keys) if not k & bit]
            plans.append((stay, leave))
            bits.append(bit)
            self.keys[s] = [keys[i] for i in stay]
        made = stage(streams, plans)
        self.bases, sents = made[0::2], made[1::2]
        self.gots = [swap(sent, bit) for sent, bit in zip(sents, bits)]
        self.columns = False
        return tuple(sents)

    def finish(self, plane=0, planes=1, into=None):
        while self.orders[0]:
            self.go()
        return join(list(zip(self.bases, self.gots)), plane, planes, into)


def ring_parts(part):
    count = lax.axis_size("tensor")
    parts = [part]
    for step in range(1, count):
        parts.append(lax.ppermute(part, "tensor", [(i, (i + step) % count) for i in range(count)]))
    return parts


def placed(places):
    count = len(places)
    own = lax.axis_index("fsdp")
    owners = jnp.bitwise_xor(jnp.asarray(places, jnp.int32), own.astype(jnp.int32))
    return lax.broadcasted_iota(jnp.int32, (count, count), 0) == owners[None, :]


def shards(
    hidden,
    cotangent,
    seq_lengths,
    pack_order,
    norm_gain,
    w_in,
    conv_weight,
    conv_bias,
    w_xproj,
    w_dt,
    dt_bias,
    a_log,
    d_skip,
    w_out,
):
    n_fsdp = lax.axis_size("fsdp")
    n_tensor = lax.axis_size("tensor")
    place = lax.axis_index("tensor")
    own_channels = w_in.shape[1]
    width = hidden.shape[1]
    group_rows = hidden.shape[0] * n_tensor
    rank = w_dt.shape[1]
    states = a_log.shape[1]
    taps = conv_weight.shape[1]
    wide = [1 << i for i in range(1, n_fsdp.bit_length() - 1)]
    narrow = wide[::-1]
    kept = [k for k in range(n_fsdp) if not k & 1]
    places = kept + [k + 1 for k in kept]
    channels = own_channels * n_fsdp
    middle = channels // 2

    rows_all = lax.all_gather(hidden, "tensor", axis=0, tiled=True)
    gather_x, gather_g = Gather(w_in[0], wide), Gather(w_in[1], narrow)
    first_x, first_g = gather_x.send(), gather_g.send()
    first_x, first_g = lax.optimization_barrier((first_x, first_g))
    gather_x.got, gather_g.got = first_x, first_g
    gather_x.take()
    gather_g.take()
    for _ in wide[1:]:
        gather_x.send()
        gather_g.send()
        if gather_x.order:
            gather_x.take()
            gather_g.take()
    gain_own = after(norm_gain.reshape(1, -1), first_x, first_g)
    lines = lax.broadcasted_iota(jnp.int32, (n_tensor, 1), 0)
    gain_line = jnp.where(lines == place, gain_own, 0)
    for step in range(1, n_tensor):
        got = lax.ppermute(gain_own, "tensor", [(i, (i + step) % n_tensor) for i in range(n_tensor)])
        gain_line = jnp.where(lines == lax.rem(place - step + n_tensor, n_tensor), got, gain_line)
    gain_rows = width // n_fsdp // own_channels
    small = jnp.concatenate(
        [
            w_xproj.T,
            w_dt.T,
            a_log.T,
            conv_weight.T,
            conv_bias[None],
            dt_bias[None],
            d_skip[None],
            gain_line.reshape(gain_rows, own_channels),
        ],
        axis=0,
    )
    small_a = jnp.concatenate([small] + [swap(small, k) for k in kept[1:]], axis=1)
    small_all = jnp.concatenate([small_a, swap(small_a, 1)], axis=1)
    got_x, got_g = after(gather_x.got, small_a), after(gather_g.got, small_a)
    weights = (
        gather_x.sent, got_x, swap(gather_x.sent, 1), swap(got_x, 1),
        gather_g.sent, got_g, swap(gather_g.sent, 1), swap(got_g, 1),
    )
    half_width = width // 2
    cot_l = lax.all_gather(after(cotangent[:, :half_width], first_x), "tensor", axis=0, tiled=True)
    outs = {0: after(w_out, got_x, got_g)}
    for bit in wide:
        outs[bit] = swap(outs[0], bit)

    xw = rank + 2 * states
    w_xp = small_all[:xw]
    at = xw + rank
    a_rows = small_all[at : at + states].astype(f32)
    at = at + states
    conv_rows = small_all[at : at + taps].astype(f32)
    at = at + taps
    conv_b = small_all[at : at + 1].astype(f32)
    dt_b = small_all[at + 1 : at + 2].astype(f32)
    skip_row = small_all[at + 2 : at + 3].astype(f32)
    gain_all = small_all[at + 3 :].astype(f32).reshape(1, gain_rows, n_fsdp, own_channels)
    owners = placed(places)
    gain = jnp.sum(jnp.where(owners[:, None, :, None], gain_all, 0.0), axis=2).reshape(1, width)
    rates = (-jnp.exp(a_rows) * math.log2(math.e)).reshape(-1, LANES)

    offsets = distances(seq_lengths[0], pack_order[0], group_rows)
    keep = (offsets > 0).astype(jnp.int32)
    dist = offsets[:, None]
    normed = norm_rows(rows_all, gain, n_tensor)

    signal, gate, inner, mixed_own = front(normed, weights, conv_rows, conv_b, w_xp, dist, own_channels)
    parts = ring_parts(mixed_own)
    for i, bit in enumerate(wide):
        for k in kept[1 : 1 << i]:
            near = after(outs[k], outs[bit], mixed_own)
            outs[k | bit] = swap(near, bit)
    cot_r = lax.all_gather(after(cotangent[:, half_width:], *parts), "tensor", axis=0, tiled=True)
    late = [after(outs[k], *parts[1:]) for k in kept]
    quarters = late + [swap(piece, 1) for piece in late]
    parts[0] = after(parts[0], *late)
    w_dt_rows = after(small_all, *parts[1:])[xw : xw + rank]
    none = jnp.zeros(rates.shape, f32)
    states_all, deltas, sums, gated, mixed, _ = scan_forward(
        0, keep, parts, w_dt_rows, dt_b, skip_row, rates, inner, gate, none
    )
    quarters = tuple(after(quarter, mixed) for quarter in quarters)
    branch = with_pieces(branch_body, "branch", (gated,), quarters, width)
    grad_gated = with_pieces(cross_body, "cross", (after(cot_l, branch), after(cot_r, branch)), quarters, channels)
    branch_own = lax.psum_scatter(branch, "tensor", scatter_dimension=0, tiled=True)
    output = (hidden.astype(f32) + branch_own.astype(f32)).astype(bf16)
    orders = (wide, narrow)

    out_grad = WeightGrad(after(gated, grad_gated), (cot_l, cot_r), kept, orders)
    out_grad.exchange()
    g_scan, g_gate, g_proj, g_mixed, reds, acc, _ = scan_backward(
        0, keep, after(mixed, out_grad.leave), w_dt_rows, skip_row, rates, inner, gate, grad_gated, sums, states_all,
        deltas, none,
    )
    backs = ring_parts(g_mixed)
    gate_grad = WeightGrad(g_gate, (normed,), kept, orders)
    gate_grad.rest()
    out_grad.rest(gate_grad.bases[0])
    sent = out_grad.go()
    backs[0] = after(backs[0], *sent)
    gate_grad.exchange()
    g_signal, low, _, conv_sums = turn(0, backs, g_scan, signal, conv_rows, conv_b, w_xp, dist)
    sent_g = gate_grad.go(low)
    sent = sent_g + out_grad.go(*sent_g)
    g_norm, gain_term = rear(
        after(g_signal, branch_own, *sent), g_gate, weights, normed, own_channels
    )
    g_norm = after(g_norm, *gate_grad.gots)
    g_norm_own = lax.psum_scatter(g_norm, "tensor", scatter_dimension=0, tiled=True)
    gain_sum = sum(part.astype(f32) for part in ring_parts((gain_term / gain).astype(bf16)))
    gain_sum = lax.dynamic_index_in_dim(gain_sum.reshape(n_fsdp, n_tensor, -1), place, 1, False)
    gain_sum = jnp.sum(jnp.where(owners[:, :, None], gain_sum[:, None, :], 0.0), axis=0)
    gain_sum = jnp.pad(gain_sum, ((0, 0), (0, own_channels - gain_sum.shape[1]))).reshape(1, channels)
    gain_sum = jnp.concatenate([gain_sum, jnp.zeros((SUB - 1, channels), f32)], axis=0)
    sig_grad = WeightGrad(after(g_signal, g_norm), (normed,), kept, orders)
    sig_grad.exchange()
    sig_grad.rest(*out_grad.gots)
    sent = gate_grad.go(sig_grad.bases[0])
    sent = sig_grad.go(*sent)
    small_stay, small_leave = pack(
        rank, states, low, mixed, inner, g_proj, acc, rates, conv_sums, reds, after(gain_sum, *sent)
    )
    small_got = swap(small_leave, 1)
    out_grad.gots[0] = after(out_grad.gots[0], small_leave)
    grad_w_out = out_grad.finish()[0]
    small_half = small_stay.astype(f32) + after(small_got, grad_w_out).astype(f32)
    small_cuts = [small_half[:, i * own_channels : (i + 1) * own_channels] for i in range(len(kept))]
    small_lows = [cut.astype(bf16) for cut in small_cuts[1:]]
    small_gots = [swap(low, k) for low, k in zip(small_lows, kept[1:])]
    gate_grad.gots[0] = after(gate_grad.gots[0], *small_lows)
    grad_w_in = gate_grad.finish(1, 2)
    sig_grad.go(grad_w_in)
    small_gots[0] = after(small_gots[0], sig_grad.bases[0])
    small_own = small_cuts[0]
    for got in small_gots:
        small_own = small_own + got.astype(f32)
    grad_hidden = last(g_norm_own, hidden, cotangent, gain)
    sig_grad.gots[0] = after(sig_grad.gots[0], grad_hidden)
    grad_w_in = sig_grad.finish(0, 2, grad_w_in)
    at = xw + rank + states
    grad_gain = small_own[at + 2 * SUB, : norm_gain.shape[0]]
    columns = small_own.T
    return (
        output,
        grad_hidden,
        grad_gain,
        grad_w_in,
        columns[:, at : at + taps],
        small_own[at + taps],
        columns[:, :xw],
        columns[:, xw : xw + rank],
        small_own[at + SUB + 1],
        columns[:, at - states : at],
        small_own[at + SUB],
        grad_w_out,
    )


def solution(mesh):
    every = ("fsdp", "tensor")
    rows = P(every, None)
    line = P(every)
    planes = P(None, every, None)
    return jax.shard_map(
        shards,
        mesh=mesh,
        in_specs=(rows, rows, P("fsdp", None), P("fsdp", None), line, planes, rows, line, rows, rows, line, rows, line, rows),
        out_specs=(rows, rows, line, planes, rows, line, rows, rows, line, rows, line, rows),
        check_vma=False,
    )
```
